32 devices in a mesh: sky: 4 (over y, x), vel: 8 (over z, core).
Axes of the slice: x: 2, y: 2, z: 4, core: 2. Of those that a mesh axis runs over, the one named last changes fastest.
Arguments:
- psi_maps: float32 [4, 2048, 512], P(None, ('sky', 'vel')), may hold values from -6 to 6
- phi_maps: float32 [4, 2048, 512], P(None, ('sky', 'vel')), may hold values from 0.25 to 4
- psf_taps: float32 [9], replicated, may hold values from 0.1 to 1
- shifts: int32 [64, 4, 2], P('vel'), may hold values from -16 to 16, as said below
Outputs:
- likelihood: float32 [64, 2048, 512], P('vel', 'sky')
The draws below stay inside these ranges and needn't reach their ends.
Inputs may be any that keep to these rules, and one draw needn't show every extreme that they name: `shifts`: frame 0 has shift 0 in every trial.
All inputs are finite; a program needn't handle non-finite values.
Results may differ from the reference program's by a relative error of at most 0.0003.
Values sent between devices are 32-bit elements; how exact they have to be, the bound alone decides.
A program may use at most 128 MiB of HBM per device.

```python
import math
import jax
import jax.numpy as jnp
from jax import lax

FRAMES = 4
COLS = 512
KSIZE = 9
SHIFT = 16
NROWS = 2048
VELS = 64


def draw_shifts(key, part):
    values = jax.random.randint(key, (VELS, FRAMES, 2), -SHIFT, SHIFT + 1, dtype=jnp.int32)
    values = values.at[:, 0, :].set(0)
    values = values.at[0, FRAMES - 1, :].set(SHIFT)
    values = values.at[1, FRAMES - 1, :].set(-SHIFT)
    return values


def block_scale(rng, extent, cuts, smallest, largest):
    def one(dim, parts):
        steps = jax.random.uniform(jax.random.fold_in(jax.random.fold_in(rng, 6), dim), (parts,), jnp.float32, smallest / len(cuts), largest / len(cuts))
        return jnp.repeat(jnp.exp(steps), extent[dim] // parts).reshape((-1,) + (1,) * (len(extent) - dim - 1))

    gain = one(*cuts[0])
    for cut in cuts[1:]:
        gain = gain * one(*cut)
    return gain


def noise(rng, shape, spread, bound, shards=(), kind=jnp.bfloat16):
    loudness = block_scale(rng, shape, shards, -0.22, 0.18) if shards else 1.0
    array = jax.random.normal(rng, shape, jnp.float32) * spread * loudness
    return jnp.minimum(jnp.maximum(array, -bound), bound).astype(kind)


def setup_inputs(seed: int = 0) -> dict:
    splits = jax.random.split(jax.random.key(seed), 5)
    psi_maps = noise(splits[0], (FRAMES, NROWS, COLS), 1.0, 6.0, ((1, 32),), jnp.float32)
    phi_maps = jnp.clip(jnp.exp(math.log(4.0) - 2.7725887 * jax.random.uniform(splits[1], (FRAMES, NROWS, COLS), jnp.float32) ** block_scale(splits[1], (FRAMES, NROWS, COLS), ((1, 32),), -0.2, 0.2)), 0.25, 4.0)
    psf_taps = jnp.clip(jnp.exp(jax.random.uniform(splits[2], (KSIZE,), jnp.float32, math.log(0.1), math.log(1.0))), 0.1, 1.0)
    shifts = draw_shifts(jax.random.fold_in(splits[4], 71), 0)
    return dict(psi_maps=psi_maps, phi_maps=phi_maps, psf_taps=psf_taps, shifts=shifts)


def band_matrix(weights, width):
    row_index = lax.broadcasted_iota(jnp.int32, (width, width), 0)
    col_index = lax.broadcasted_iota(jnp.int32, (width, width), 1)
    offsets = row_index - col_index + weights.shape[0] // 2
    matrix = jnp.zeros((width, width), weights.dtype)
    for position in range(weights.shape[0]):
        matrix = matrix + jnp.where(offsets == position, weights[position], jnp.zeros((), weights.dtype))
    return matrix

def correlate(extended, weights, count):
    squared = weights * weights
    width = extended.shape[-1]
    along_psi = jnp.matmul(extended[0], band_matrix(weights, width), precision=lax.Precision.HIGHEST)
    along_phi = jnp.matmul(extended[1], band_matrix(squared, width), precision=lax.Precision.HIGHEST)
    blurred = jnp.stack([along_psi, along_phi])
    total = jnp.zeros(blurred.shape[:2] + (count, width), blurred.dtype)
    for position in range(weights.shape[0]):
        factor = jnp.stack([weights[position], squared[position]])
        total = total + factor[:, None, None, None] * blurred[:, :, position:position + count]
    return total

def reference(psi_maps, phi_maps, psf_taps, shifts):
    weights = psf_taps / jnp.sum(psf_taps)
    half = KSIZE // 2
    stacked = jnp.stack([psi_maps, phi_maps])
    padded = jnp.pad(stacked, ((0, 0), (0, 0), (half, half), (0, 0)))
    blurred = correlate(padded, weights, NROWS)
    reach = jnp.pad(blurred, ((0, 0), (0, 0), (SHIFT, SHIFT), (SHIFT, SHIFT)))
    anchor = jnp.zeros((), jnp.int32)

    def stack_trial(shift_rows):
        total = jnp.zeros((2, NROWS, COLS), reach.dtype)
        for frame in range(FRAMES):
            piece = lax.dynamic_slice(reach[:, frame], (anchor, (SHIFT + shift_rows[frame, 0]).astype(jnp.int32), (SHIFT + shift_rows[frame, 1]).astype(jnp.int32)), (2, NROWS, COLS))
            total = total + piece
        return total[0] / jnp.sqrt(total[1])
    return lax.map(stack_trial, shifts)
```

```python
import functools
import jax
import jax.numpy as jnp
from jax import lax
from jax.experimental import pallas as pl
from jax.experimental.pallas import tpu as pltpu
from jax.sharding import PartitionSpec as P

SHIFT = 16
BLOCK = 16
HALO = 2 * BLOCK
ABOVE = BLOCK + 8
CLOSING = 4 * BLOCK
LANES = 128
MESH = pl.DeviceIdType.MESH


def stack_rows(shifts_ref, maps_ref, out_ref, trial, first, count, skip, unroll):
    frames = shifts_ref.shape[0]
    tiles = maps_ref.shape[1]
    lane = lax.broadcasted_iota(jnp.int32, (8, LANES), 1)
    down, turn, inside = [], [], []
    for frame in range(1, frames):
        offset = shifts_ref[frame, 1, trial] + SHIFT
        down.append(shifts_ref[frame, 0, trial] + ABOVE)
        turn.append(lax.rem(LANES - offset, LANES))
        inside.append(lane >= offset)

    def one_group(group, carry):
        base = first + group * 8

        def stacked(kind):
            total = [
                maps_ref[kind * frames, tile, pl.ds(pl.multiple_of(base + ABOVE, 8), 8)]
                for tile in range(tiles - 1)
            ]
            for step in range(frames - 1):
                m = kind * frames + step + 1
                pieces = [maps_ref[m, tile, pl.ds(base + down[step], 8)] for tile in range(tiles)]
                for tile in range(tiles - 1):
                    joined = jnp.where(inside[step], pieces[tile], pieces[tile + 1])
                    total[tile] = total[tile] + pltpu.roll(joined, turn[step], 1)
            return total

        psi = stacked(0)
        phi = stacked(1)
        for tile in range(tiles - 1):
            out_ref[
                trial, pl.ds(pl.multiple_of(base - skip, 8), 8), tile * LANES : (tile + 1) * LANES
            ] = psi[tile] * lax.rsqrt(phi[tile])
        return carry

    lax.fori_loop(0, count // 8, one_group, 0, unroll=unroll)


def closing_row(chips, per, low):
    block = jnp.where(low, per * (chips - 1), per - 1)
    return pl.multiple_of(BLOCK * (block - 1) - 8, 8)


def stack_kernel(vels, shifts_ref, maps_ref, done_ref, out_ref, closing, sems):
    trials, rows, _ = done_ref.shape
    chips = vels // 2
    per = rows // (chips * BLOCK)
    low = lax.axis_index("vel") // 2 < chips // 2
    first = closing_row(chips, per, low)
    small = BLOCK * (per - 2) - 8
    large = rows - CLOSING - small
    large_row = pl.multiple_of(jnp.where(low, 0, small + CLOSING), 8)
    small_row = pl.multiple_of(jnp.where(low, large + CLOSING, 0), 8)

    def large_copy(trial):
        part = pl.ds(large_row, large)
        return pltpu.make_async_copy(done_ref.at[trial, part], out_ref.at[trial, part], sems.at[0, trial])

    def small_copy(trial):
        part = pl.ds(small_row, small)
        return pltpu.make_async_copy(done_ref.at[trial, part], out_ref.at[trial, part], sems.at[1, trial])

    def closing_copy(trial):
        part = pl.ds(first, CLOSING)
        return pltpu.make_async_copy(closing.at[trial], out_ref.at[trial, part], sems.at[2, trial])

    def begin(trial, carry):
        large_copy(trial).start()
        small_copy(trial).start()
        return carry

    lax.fori_loop(0, trials, begin, 0)

    def compute(trial, carry):
        stack_rows(shifts_ref, maps_ref, closing, trial, first, CLOSING, first, True)
        closing_copy(trial).start()
        return carry

    lax.fori_loop(0, trials, compute, 0)

    def finish(trial, carry):
        large_copy(trial).wait()
        small_copy(trial).wait()
        closing_copy(trial).wait()
        return carry

    lax.fori_loop(0, trials, finish, 0)


def gather_kernel(
    vels, skies, taps_ref, shifts_ref, psi_ref, phi_ref, out_ref, done_ref,
    raw, along, landing, top, bottom, band0, band1, weight,
    own_sem, trade_sems, recv_sem, right_sem, left_sem, pair_send, pair_recv, top_sems, bottom_sems,
):
    frames, share, width = psi_ref.shape
    trials = shifts_ref.shape[2]
    taps = taps_ref.shape[0]
    half = taps // 2
    chips = vels // 2
    tiles = width // LANES
    rows = vels * share
    blocks = rows // BLOCK
    per = blocks // chips
    steps = per * (chips - 1)
    sky = lax.axis_index("sky")
    vel = lax.axis_index("vel")
    chip = vel // 2
    core = vel % 2
    has_right = chip < chips - 1
    has_left = chip > 0
    has_next = sky < skies - 1
    has_prev = sky > 0
    low = chip < chips // 2
    partner = (sky, vel + 1 - 2 * core)

    own_rows = pl.ds(pl.multiple_of(vel * share, 8), share)

    def own_copy(source):
        return pltpu.make_async_copy(source, raw.at[:, own_rows], own_sem)

    @pl.when(core == 0)
    def _():
        own_copy(psi_ref).start()

    @pl.when(core == 1)
    def _():
        own_copy(phi_ref).start()

    neighbours = (
        (has_right, (sky, vel + 2)),
        (has_left, (sky, vel - 2)),
        (has_next, (sky + 1, vel)),
        (has_prev, (sky - 1, vel)),
    )
    barrier = pltpu.get_barrier_semaphore()
    pl.semaphore_signal(barrier, inc=1, device_id=partner, device_id_type=MESH)
    for present, device in neighbours:

        @pl.when(present)
        def _(device=device):
            pl.semaphore_signal(barrier, inc=1, device_id=device, device_id_type=MESH)

    peers = 1
    for present, _ in neighbours:
        peers = peers + present.astype(jnp.int32)
    pl.semaphore_wait(barrier, peers)

    def trade_copy(source):
        return pltpu.make_async_remote_copy(
            src_ref=source,
            dst_ref=raw.at[:, own_rows],
            send_sem=trade_sems.at[0],
            recv_sem=trade_sems.at[1],
            device_id=partner,
            device_id_type=MESH,
        )

    @pl.when(core == 0)
    def _():
        trade_copy(phi_ref).start()

    @pl.when(core == 1)
    def _():
        trade_copy(psi_ref).start()

    def block_rows(block):
        return pl.ds(pl.multiple_of(block * BLOCK, 8), BLOCK)

    def line_copy(block, to_right):
        return pltpu.make_async_remote_copy(
            src_ref=raw.at[:, block_rows(block)],
            dst_ref=raw.at[:, block_rows(block)],
            send_sem=(right_sem if to_right else left_sem).at[block // per],
            recv_sem=recv_sem.at[block],
            device_id=(sky, vel + 2) if to_right else (sky, vel - 2),
            device_id_type=MESH,
        )

    def halo_copy(to_next):
        source = raw.at[:, pl.ds(rows - HALO if to_next else 0, HALO)]
        sems = top_sems if to_next else bottom_sems
        return pltpu.make_async_remote_copy(
            src_ref=source,
            dst_ref=top if to_next else bottom,
            send_sem=sems.at[0],
            recv_sem=sems.at[1],
            device_id=(sky + 1, vel) if to_next else (sky - 1, vel),
            device_id_type=MESH,
        )

    def pair_rows(blur):
        return out_ref.at[
            pl.ds(core * frames, frames), :, pl.ds(pl.multiple_of((blur + 1) * BLOCK, 8), BLOCK)
        ]

    def pair_copy(blur):
        return pltpu.make_async_remote_copy(
            src_ref=pair_rows(blur),
            dst_ref=landing.at[blur + 1],
            send_sem=pair_send,
            recv_sem=pair_recv.at[blur + 1],
            device_id=partner,
            device_id_type=MESH,
        )

    def from_partner(blur):
        pair_copy(blur).wait_recv()
        place = pl.ds(pl.multiple_of((blur + 1) * BLOCK, 8), BLOCK)
        for m in range(frames):
            for tile in range(tiles + min(m, 1)):
                out_ref[(1 - core) * frames + m, tile, place] = landing[blur + 1, m, tile]

    right_up = chip == 0
    left_up = chip < chips - 1

    def send_half(to_right, upward, part):
        def one(index, carry):
            place = jnp.where(upward, index, per // 2 - 1 - index)
            line_copy(chip * per + part * (per // 2) + place, to_right).start()
            return carry

        lax.fori_loop(0, per // 2, one, 0)

    right_ready = right_up == (core == 0)
    left_ready = left_up == (core == 0)
    own_copy(psi_ref).wait()

    @pl.when(has_left & left_ready)
    def _():
        send_half(False, left_up, core)

    @pl.when(has_right & right_ready)
    def _():
        send_half(True, right_up, core)

    total = taps_ref[0]
    for i in range(1, taps):
        total = total + taps_ref[i]
    scale = 1.0 / jnp.full((8, LANES), total, jnp.float32)
    squared = jnp.full((8, LANES), core, jnp.int32) > 0
    for i in range(taps):
        value = jnp.full((8, LANES), taps_ref[i], jnp.float32) * scale
        weight[i] = jnp.where(squared, value * value, value)
    for lead, band in ((0, band0), (1, band1)):
        depth = (3 - lead) * LANES
        place = lax.broadcasted_iota(jnp.int32, (depth, LANES), 0)
        place = place - lax.broadcasted_iota(jnp.int32, (depth, LANES), 1)
        spot = place - (LANES - SHIFT * lead - half)
        matrix = jnp.zeros((depth, LANES), jnp.float32)
        for i in range(taps):
            value = jnp.broadcast_to(weight[i][:1], (depth, LANES))
            matrix = jnp.where(spot == i, value, matrix)
        coarse = matrix.astype(jnp.bfloat16)
        band[:depth] = coarse
        band[depth : 2 * depth] = coarse
        band[2 * depth :] = (matrix - coarse.astype(jnp.float32)).astype(jnp.bfloat16)

    trade_copy(psi_ref).wait_recv()

    @pl.when(has_left & jnp.logical_not(left_ready))
    def _():
        send_half(False, left_up, 1 - core)

    @pl.when(has_left & left_ready)
    def _():
        send_half(False, left_up, 1 - core)

    @pl.when(has_right & jnp.logical_not(right_ready))
    def _():
        send_half(True, right_up, 1 - core)

    @pl.when(has_right & right_ready)
    def _():
        send_half(True, right_up, 1 - core)

    @pl.when(has_left & jnp.logical_not(left_ready))
    def _():
        send_half(False, left_up, core)

    @pl.when(has_right & jnp.logical_not(right_ready))
    def _():
        send_half(True, right_up, core)

    @pl.when(has_next & (chip == chips - 1))
    def _():
        halo_copy(True).start()

    @pl.when(has_prev & (chip == 0))
    def _():
        halo_copy(False).start()

    def blur_along(source, start, count, place):
        def windows(values, lead):
            blank = jnp.zeros((values.shape[0], LANES), values.dtype)
            columns = [blank] + [values[:, t * LANES : (t + 1) * LANES] for t in range(tiles)] + [blank]
            wide = 3 - lead
            return jnp.concatenate(
                [jnp.concatenate(columns[t : t + wide], axis=1) for t in range(tiles + lead)], axis=0
            )

        for lead, band in ((0, band0), (1, band1)):
            if lead:
                values = source[1:frames, pl.ds(start, count)].reshape((frames - 1) * count, width)
            else:
                values = source[0, pl.ds(start, count)]
            height = values.shape[0]
            coarse = values.astype(jnp.bfloat16)
            fine = (values - coarse.astype(jnp.float32)).astype(jnp.bfloat16)
            high, rest = windows(coarse, lead), windows(fine, lead)
            blurred = jnp.dot(
                jnp.concatenate([high, rest, high], axis=1), band[...],
                preferred_element_type=jnp.float32,
            )
            for tile in range(tiles + lead):
                piece = blurred[tile * height : (tile + 1) * height]
                if lead and tile in (0, tiles):
                    lane = lax.broadcasted_iota(jnp.int32, (height, LANES), 1)
                    piece = jnp.where(lane >= SHIFT if tile == 0 else lane < SHIFT, piece, 0.0)
                for m in range(height // count):
                    along[lead + m, tile, pl.ds(place, count)] = piece[m * count : (m + 1) * count]

    def blur_block(block):
        start = pl.multiple_of(block * BLOCK, 8)
        blur_along(raw, start, BLOCK, pl.multiple_of(start + HALO, 8))

    def blur_across(blur, copied):
        factors = [weight[i] for i in range(taps)]
        start = blur * BLOCK + HALO - 8 - half
        place = (blur + 1) * BLOCK

        def one_map(m, carry):
            for tile in range(tiles + 1):
                for group in range(BLOCK // 8):
                    base = start + 8 * group
                    value = factors[0] * along[m, tile, pl.ds(base, 8)]
                    for i in range(1, taps):
                        value += factors[i] * along[m, tile, pl.ds(base + i, 8)]
                    out_ref[
                        core * frames + m, tile, pl.ds(pl.multiple_of(place + 8 * group, 8), 8)
                    ] = value
            return carry

        lax.fori_loop(0, frames, one_map, 0)
        if copied:
            pair_copy(blur).start()

    def stack(first, count, unroll):
        def one_trial(trial, carry):
            stack_rows(shifts_ref, out_ref, done_ref, trial, first, count, 0, unroll)
            return carry

        lax.fori_loop(0, trials, one_trial, 0)


    def own_block(block, carry):
        blur_block(block)
        return carry

    def own_blur(blur, carry):
        blur_across(blur, True)
        return carry

    def own_wait(blur, carry):
        from_partner(blur)
        return carry

    lax.fori_loop(chip * per, chip * per + per, own_block, 0)
    lax.fori_loop(chip * per + 1, chip * per + per, own_blur, 0)
    lax.fori_loop(chip * per + 1, chip * per + per, own_wait, 0)
    stack(pl.multiple_of((chip * per + 2) * BLOCK - 8, 8), BLOCK * (per - 3), 2)

    def stream(side, index):
        distance = index // per
        j = index % per
        origin = jnp.where(side == 1, chip + 1 + distance, chip - 1 - distance)
        present = (index >= 0) & (origin >= 0) & (origin < chips)
        edge = jnp.where(side == 1, origin == chips - 1, origin == 0)
        upward = (side == 1) != edge
        block = origin * per + jnp.where(upward, j, per - 1 - j)
        last = edge & (j == per - 1)
        return present, edge, upward, j, block, last

    def blurs(side, index, act):
        present, edge, upward, j, block, last = stream(side, index)
        count = jnp.where(present & jnp.logical_not(edge & (j == 0)), 1 + last.astype(jnp.int32), 0)
        begin = jnp.where(upward, block, block + 1)
        turn = jnp.where(upward, 1, -1)

        def one(k, carry):
            act(begin + turn * k)
            return carry

        lax.fori_loop(0, count, one, 0)

    def arrive(index):
        present, edge, _, j, block, _ = stream(1, index)

        @pl.when(present)
        def _():
            line_copy(block, True).wait_recv()

            @pl.when(has_left)
            def _():
                line_copy(block, False).start()

            @pl.when(edge & (j == 1) & has_next)
            def _():
                halo_copy(True).start()

        present, edge, _, j, block, _ = stream(0, index)

        @pl.when(present)
        def _():
            line_copy(block, False).wait_recv()

            @pl.when(has_right)
            def _():
                line_copy(block, True).start()

            @pl.when(edge & (j == 1) & has_prev)
            def _():
                halo_copy(False).start()

    def blur_side(index):
        def one_side(side, carry):
            present, _, _, _, block, _ = stream(side, index)

            @pl.when(present)
            def _():
                blur_block(block)

            blurs(side, index, lambda blur: blur_across(blur, True))
            return carry

        lax.fori_loop(0, 2, one_side, 0)

    def stack_side(index):
        def one_side(side, carry):
            present, edge, upward, j, block, last = stream(side, index)
            blurs(side, index, from_partner)

            @pl.when(present & jnp.logical_not(last) & (jnp.logical_not(edge) | (j > 2)))
            def _():
                stack(
                    pl.multiple_of(jnp.where(upward, block - 1, block + 2) * BLOCK - 8, 8), BLOCK, True
                )

            @pl.when(present & last & ((side == 1) != low))
            def _():
                stack(pl.multiple_of((block - 1) * BLOCK - 8, 8), CLOSING, 4)

            return carry

        lax.fori_loop(0, 2, one_side, 0)

    limit = steps - 2
    mirror = chips - 1 - chip
    top_step = jnp.minimum(jnp.maximum(per * (mirror - 1) + 4, per * (chip - 1) + 2), limit)
    bottom_step = jnp.minimum(jnp.maximum(per * (chip - 1) + 4, per * (mirror - 1) + 2), limit)

    def step(index, carry):
        @pl.when(index < steps)
        def _():
            arrive(index)
            blur_side(index)

        @pl.when(index == top_step)
        def _():
            @pl.when(has_prev)
            def _():
                halo_copy(True).wait_recv()
                blur_along(top, 0, HALO, 0)

            @pl.when(jnp.logical_not(has_prev))
            def _():
                for m in range(frames):
                    for tile in range(tiles + 1):
                        along[m, tile, pl.ds(0, HALO)] = jnp.zeros((HALO, LANES), jnp.float32)

            blur_across(-1, False)
            blur_across(0, False)

            @pl.when(jnp.logical_not(has_prev))
            def _():
                for m in range(frames):
                    for tile in range(tiles + 1):
                        out_ref[core * frames + m, tile, pl.ds(0, ABOVE)] = jnp.zeros(
                            (ABOVE, LANES), jnp.float32
                        )

            pair_copy(-1).start()
            pair_copy(0).start()

        @pl.when(index == bottom_step)
        def _():
            @pl.when(has_next)
            def _():
                halo_copy(False).wait_recv()
                blur_along(bottom, 0, HALO, rows + HALO)

            @pl.when(jnp.logical_not(has_next))
            def _():
                for m in range(frames):
                    for tile in range(tiles + 1):
                        along[m, tile, pl.ds(rows + HALO, HALO)] = jnp.zeros(
                            (HALO, LANES), jnp.float32
                        )

            blur_across(blocks, False)
            blur_across(blocks + 1, False)

            @pl.when(jnp.logical_not(has_next))
            def _():
                for m in range(frames):
                    for tile in range(tiles + 1):
                        out_ref[core * frames + m, tile, pl.ds(rows + ABOVE, ABOVE)] = jnp.zeros(
                            (ABOVE, LANES), jnp.float32
                        )

            pair_copy(blocks).start()
            pair_copy(blocks + 1).start()

        stack_side(index - 1)

        @pl.when(index - 1 == top_step)
        def _():
            from_partner(-1)
            from_partner(0)
            stack(0, ABOVE, True)

        @pl.when(index - 1 == bottom_step)
        def _():
            from_partner(blocks)
            from_partner(blocks + 1)
            stack(rows - ABOVE, ABOVE, True)

        return carry

    lax.fori_loop(0, steps + 1, step, 0)

    mine = out_ref.at[pl.ds(core * frames, frames)]
    pltpu.make_async_copy(mine, mine, pair_send).wait()
    trade_copy(psi_ref).wait_send()

    def drain(origin, carry):
        part = raw.at[:, pl.ds(pl.multiple_of(origin * (2 * share), 8), 2 * share)]

        @pl.when(has_right & (origin <= chip))
        def _():
            pltpu.make_async_copy(part, part, right_sem.at[origin]).wait()

        @pl.when(has_left & (origin >= chip))
        def _():
            pltpu.make_async_copy(part, part, left_sem.at[origin]).wait()

        return carry

    lax.fori_loop(0, chips, drain, 0)

    @pl.when(has_next)
    def _():
        halo_copy(True).wait_send()

    @pl.when(has_prev)
    def _():
        halo_copy(False).wait_send()


def per_device(vels, skies, psi_maps, phi_maps, psf_taps, shifts):
    frames, share, width = psi_maps.shape
    maps = 2 * frames
    tiles = width // LANES
    rows = share * vels
    trials = shifts.shape[0]
    blocks = rows // BLOCK
    taps = psf_taps.shape[0]
    shifts = jnp.transpose(shifts, (1, 2, 0))
    dma = pltpu.SemaphoreType.DMA
    blurred, done = pl.pallas_call(
        functools.partial(gather_kernel, vels, skies),
        out_shape=(
            jax.ShapeDtypeStruct((maps, tiles + 1, rows + 2 * ABOVE, LANES), jnp.float32),
            jax.ShapeDtypeStruct((trials, rows, width), jnp.float32),
        ),
        in_specs=[
            pl.BlockSpec(memory_space=pltpu.SMEM),
            pl.BlockSpec(memory_space=pltpu.SMEM),
            pl.BlockSpec(memory_space=pltpu.HBM),
            pl.BlockSpec(memory_space=pltpu.HBM),
        ],
        out_specs=(pl.BlockSpec(memory_space=pltpu.VMEM), pl.BlockSpec(memory_space=pltpu.VMEM)),
        scratch_shapes=[
            pltpu.VMEM((frames, rows, width), jnp.float32),
            pltpu.VMEM((frames, tiles + 1, rows + 2 * HALO, LANES), jnp.float32),
            pltpu.VMEM((blocks + 3, frames, tiles + 1, BLOCK, LANES), jnp.float32),
            pltpu.VMEM((frames, HALO, width), jnp.float32),
            pltpu.VMEM((frames, HALO, width), jnp.float32),
            pltpu.VMEM((9 * LANES, LANES), jnp.bfloat16),
            pltpu.VMEM((6 * LANES, LANES), jnp.bfloat16),
            pltpu.VMEM((taps, 8, LANES), jnp.float32),
            dma,
            dma((2,)),
            dma((blocks,)),
            dma((vels // 2,)),
            dma((vels // 2,)),
            dma,
            dma((blocks + 3,)),
            dma((2,)),
            dma((2,)),
        ],
        compiler_params=pltpu.CompilerParams(
            collective_id=0, has_side_effects=True, vmem_limit_bytes=24 * 2**20
        ),
        name="gather",
    )(psf_taps, shifts, psi_maps, phi_maps)
    return pl.pallas_call(
        functools.partial(stack_kernel, vels),
        out_shape=jax.ShapeDtypeStruct((trials, rows, width), jnp.float32),
        in_specs=[
            pl.BlockSpec(memory_space=pltpu.SMEM),
            pl.BlockSpec(memory_space=pltpu.VMEM),
            pl.BlockSpec(memory_space=pltpu.VMEM),
        ],
        out_specs=pl.BlockSpec(memory_space=pl.ANY),
        scratch_shapes=[
            pltpu.VMEM((trials, CLOSING, width), jnp.float32),
            dma((3, trials)),
        ],
        compiler_params=pltpu.CompilerParams(vmem_limit_bytes=4 * 2**20),
        name="stack",
    )(shifts, blurred, done)


def solution(mesh):
    return jax.shard_map(
        functools.partial(per_device, mesh.shape["vel"], mesh.shape["sky"]),
        mesh=mesh,
        in_specs=(
            P(None, ("sky", "vel"), None),
            P(None, ("sky", "vel"), None),
            P(),
            P("vel", None, None),
        ),
        out_specs=P("vel", "sky", None),
        check_vma=False,
    )
```

```python
import functools
import jax
import jax.numpy as jnp
from jax import lax
from jax.experimental import pallas as pl
from jax.experimental.pallas import tpu as pltpu
from jax.sharding import PartitionSpec as P

SHIFT = 16
BLOCK = 16
HALO = 2 * BLOCK
ABOVE = BLOCK + 8
CLOSING = 4 * BLOCK
LANES = 128
MESH = pl.DeviceIdType.MESH


def stack_rows(shifts_ref, maps_ref, out_ref, trial, first, count, skip, unroll):
    frames = shifts_ref.shape[0]
    tiles = maps_ref.shape[1]
    lane = lax.broadcasted_iota(jnp.int32, (8, LANES), 1)
    down, turn, inside = [], [], []
    for frame in range(1, frames):
        offset = shifts_ref[frame, 1, trial] + SHIFT
        down.append(shifts_ref[frame, 0, trial] + ABOVE)
        turn.append(lax.rem(LANES - offset, LANES))
        inside.append(lane >= offset)

    def one_group(group, carry):
        base = first + group * 8

        def stacked(kind):
            total = [
                maps_ref[kind * frames, tile, pl.ds(pl.multiple_of(base + ABOVE, 8), 8)]
                for tile in range(tiles - 1)
            ]
            for step in range(frames - 1):
                m = kind * frames + step + 1
                pieces = [maps_ref[m, tile, pl.ds(base + down[step], 8)] for tile in range(tiles)]
                for tile in range(tiles - 1):
                    joined = jnp.where(inside[step], pieces[tile], pieces[tile + 1])
                    total[tile] = total[tile] + pltpu.roll(joined, turn[step], 1)
            return total

        psi = stacked(0)
        phi = stacked(1)
        for tile in range(tiles - 1):
            out_ref[
                trial, pl.ds(pl.multiple_of(base - skip, 8), 8), tile * LANES : (tile + 1) * LANES
            ] = psi[tile] * lax.rsqrt(phi[tile])
        return carry

    lax.fori_loop(0, count // 8, one_group, 0, unroll=unroll)


def closing_row(chips, per, low):
    block = jnp.where(low, per * (chips - 1), per - 1)
    return pl.multiple_of(BLOCK * (block - 1) - 8, 8)


def stack_kernel(vels, shifts_hbm, maps_ref, done_ref, out_ref, shifts_ref, closing, shifts_sem, sems):
    shifts_copy = pltpu.make_async_copy(shifts_hbm, shifts_ref, shifts_sem)
    shifts_copy.start()
    trials, rows, _ = done_ref.shape
    chips = vels // 2
    per = rows // (chips * BLOCK)
    low = lax.axis_index("vel") // 2 < chips // 2
    first = closing_row(chips, per, low)
    small = BLOCK * (per - 2) - 8
    large = rows - CLOSING - small
    large_row = pl.multiple_of(jnp.where(low, 0, small + CLOSING), 8)
    small_row = pl.multiple_of(jnp.where(low, large + CLOSING, 0), 8)

    def large_copy(trial):
        part = pl.ds(large_row, large)
        return pltpu.make_async_copy(done_ref.at[trial, part], out_ref.at[trial, part], sems.at[0, trial])

    def small_copy(trial):
        part = pl.ds(small_row, small)
        return pltpu.make_async_copy(done_ref.at[trial, part], out_ref.at[trial, part], sems.at[1, trial])

    def closing_copy(trial):
        part = pl.ds(first, CLOSING)
        return pltpu.make_async_copy(closing.at[trial], out_ref.at[trial, part], sems.at[2, trial])

    def begin(trial, carry):
        large_copy(trial).start()
        small_copy(trial).start()
        return carry

    lax.fori_loop(0, trials, begin, 0)
    shifts_copy.wait()

    def compute(trial, carry):
        stack_rows(shifts_ref, maps_ref, closing, trial, first, CLOSING, first, True)
        closing_copy(trial).start()
        return carry

    lax.fori_loop(0, trials, compute, 0)

    def finish(trial, carry):
        large_copy(trial).wait()
        small_copy(trial).wait()
        closing_copy(trial).wait()
        return carry

    lax.fori_loop(0, trials, finish, 0)


def gather_kernel(
    vels, skies, taps_hbm, shifts_hbm, psi_ref, phi_ref, out_ref, done_ref,
    taps_ref, shifts_ref,
    raw, along, landing, top, bottom, band0, band1, weight,
    small_sems, own_sem, trade_sems, recv_sem, right_sem, left_sem, pair_send, pair_recv, top_sems, bottom_sems,
):
    frames, share, width = psi_ref.shape
    trials = shifts_ref.shape[2]
    taps = taps_ref.shape[0]
    half = taps // 2
    chips = vels // 2
    tiles = width // LANES
    rows = vels * share
    blocks = rows // BLOCK
    per = blocks // chips
    steps = per * (chips - 1)
    sky = lax.axis_index("sky")
    vel = lax.axis_index("vel")
    chip = vel // 2
    core = vel % 2
    has_right = chip < chips - 1
    has_left = chip > 0
    has_next = sky < skies - 1
    has_prev = sky > 0
    low = chip < chips // 2
    partner = (sky, vel + 1 - 2 * core)

    taps_copy = pltpu.make_async_copy(taps_hbm, taps_ref, small_sems.at[0])
    shifts_copy = pltpu.make_async_copy(shifts_hbm, shifts_ref, small_sems.at[1])
    own_rows = pl.ds(pl.multiple_of(vel * share, 8), share)

    def own_copy(source):
        return pltpu.make_async_copy(source, raw.at[:, own_rows], own_sem)

    @pl.when(core == 0)
    def _():
        own_copy(psi_ref).start()

    @pl.when(core == 1)
    def _():
        own_copy(phi_ref).start()

    taps_copy.start()
    shifts_copy.start()
    neighbours = (
        (has_right, (sky, vel + 2)),
        (has_left, (sky, vel - 2)),
        (has_next, (sky + 1, vel)),
        (has_prev, (sky - 1, vel)),
    )
    barrier = pltpu.get_barrier_semaphore()
    pl.semaphore_signal(barrier, inc=1, device_id=partner, device_id_type=MESH)
    for present, device in neighbours:

        @pl.when(present)
        def _(device=device):
            pl.semaphore_signal(barrier, inc=1, device_id=device, device_id_type=MESH)

    peers = 1
    for present, _ in neighbours:
        peers = peers + present.astype(jnp.int32)
    pl.semaphore_wait(barrier, peers)

    def trade_copy(source):
        return pltpu.make_async_remote_copy(
            src_ref=source,
            dst_ref=raw.at[:, own_rows],
            send_sem=trade_sems.at[0],
            recv_sem=trade_sems.at[1],
            device_id=partner,
            device_id_type=MESH,
        )

    @pl.when(core == 0)
    def _():
        trade_copy(phi_ref).start()

    @pl.when(core == 1)
    def _():
        trade_copy(psi_ref).start()

    def block_rows(block):
        return pl.ds(pl.multiple_of(block * BLOCK, 8), BLOCK)

    def line_copy(block, to_right):
        return pltpu.make_async_remote_copy(
            src_ref=raw.at[:, block_rows(block)],
            dst_ref=raw.at[:, block_rows(block)],
            send_sem=(right_sem if to_right else left_sem).at[block // per],
            recv_sem=recv_sem.at[block],
            device_id=(sky, vel + 2) if to_right else (sky, vel - 2),
            device_id_type=MESH,
        )

    def halo_copy(to_next):
        source = raw.at[:, pl.ds(rows - HALO if to_next else 0, HALO)]
        sems = top_sems if to_next else bottom_sems
        return pltpu.make_async_remote_copy(
            src_ref=source,
            dst_ref=top if to_next else bottom,
            send_sem=sems.at[0],
            recv_sem=sems.at[1],
            device_id=(sky + 1, vel) if to_next else (sky - 1, vel),
            device_id_type=MESH,
        )

    def pair_rows(blur):
        return out_ref.at[
            pl.ds(core * frames, frames), :, pl.ds(pl.multiple_of((blur + 1) * BLOCK, 8), BLOCK)
        ]

    def pair_copy(blur):
        return pltpu.make_async_remote_copy(
            src_ref=pair_rows(blur),
            dst_ref=landing.at[blur + 1],
            send_sem=pair_send,
            recv_sem=pair_recv.at[blur + 1],
            device_id=partner,
            device_id_type=MESH,
        )

    def from_partner(blur):
        pair_copy(blur).wait_recv()
        place = pl.ds(pl.multiple_of((blur + 1) * BLOCK, 8), BLOCK)
        for m in range(frames):
            for tile in range(tiles + min(m, 1)):
                out_ref[(1 - core) * frames + m, tile, place] = landing[blur + 1, m, tile]

    right_up = chip == 0
    left_up = chip < chips - 1

    def send_half(to_right, upward, part):
        def one(index, carry):
            place = jnp.where(upward, index, per // 2 - 1 - index)
            line_copy(chip * per + part * (per // 2) + place, to_right).start()
            return carry

        lax.fori_loop(0, per // 2, one, 0)

    right_ready = right_up == (core == 0)
    left_ready = left_up == (core == 0)
    own_copy(psi_ref).wait()

    @pl.when(has_left & left_ready)
    def _():
        send_half(False, left_up, core)

    @pl.when(has_right & right_ready)
    def _():
        send_half(True, right_up, core)

    taps_copy.wait()
    shifts_copy.wait()
    total = taps_ref[0]
    for i in range(1, taps):
        total = total + taps_ref[i]
    scale = 1.0 / jnp.full((8, LANES), total, jnp.float32)
    squared = jnp.full((8, LANES), core, jnp.int32) > 0
    for i in range(taps):
        value = jnp.full((8, LANES), taps_ref[i], jnp.float32) * scale
        weight[i] = jnp.where(squared, value * value, value)
    for lead, band in ((0, band0), (1, band1)):
        depth = (3 - lead) * LANES
        place = lax.broadcasted_iota(jnp.int32, (depth, LANES), 0)
        place = place - lax.broadcasted_iota(jnp.int32, (depth, LANES), 1)
        spot = place - (LANES - SHIFT * lead - half)
        matrix = jnp.zeros((depth, LANES), jnp.float32)
        for i in range(taps):
            value = jnp.broadcast_to(weight[i][:1], (depth, LANES))
            matrix = jnp.where(spot == i, value, matrix)
        coarse = matrix.astype(jnp.bfloat16)
        band[:depth] = coarse
        band[depth : 2 * depth] = coarse
        band[2 * depth :] = (matrix - coarse.astype(jnp.float32)).astype(jnp.bfloat16)

    trade_copy(psi_ref).wait_recv()

    @pl.when(has_left & jnp.logical_not(left_ready))
    def _():
        send_half(False, left_up, 1 - core)

    @pl.when(has_left & left_ready)
    def _():
        send_half(False, left_up, 1 - core)

    @pl.when(has_right & jnp.logical_not(right_ready))
    def _():
        send_half(True, right_up, 1 - core)

    @pl.when(has_right & right_ready)
    def _():
        send_half(True, right_up, 1 - core)

    @pl.when(has_left & jnp.logical_not(left_ready))
    def _():
        send_half(False, left_up, core)

    @pl.when(has_right & jnp.logical_not(right_ready))
    def _():
        send_half(True, right_up, core)

    @pl.when(has_next & (chip == chips - 1))
    def _():
        halo_copy(True).start()

    @pl.when(has_prev & (chip == 0))
    def _():
        halo_copy(False).start()

    def blur_along(source, start, count, place):
        def windows(values, lead):
            blank = jnp.zeros((values.shape[0], LANES), values.dtype)
            columns = [blank] + [values[:, t * LANES : (t + 1) * LANES] for t in range(tiles)] + [blank]
            wide = 3 - lead
            return jnp.concatenate(
                [jnp.concatenate(columns[t : t + wide], axis=1) for t in range(tiles + lead)], axis=0
            )

        for lead, band in ((0, band0), (1, band1)):
            if lead:
                values = source[1:frames, pl.ds(start, count)].reshape((frames - 1) * count, width)
            else:
                values = source[0, pl.ds(start, count)]
            height = values.shape[0]
            coarse = values.astype(jnp.bfloat16)
            fine = (values - coarse.astype(jnp.float32)).astype(jnp.bfloat16)
            high, rest = windows(coarse, lead), windows(fine, lead)
            blurred = jnp.dot(
                jnp.concatenate([high, rest, high], axis=1), band[...],
                preferred_element_type=jnp.float32,
            )
            for tile in range(tiles + lead):
                piece = blurred[tile * height : (tile + 1) * height]
                if lead and tile in (0, tiles):
                    lane = lax.broadcasted_iota(jnp.int32, (height, LANES), 1)
                    piece = jnp.where(lane >= SHIFT if tile == 0 else lane < SHIFT, piece, 0.0)
                for m in range(height // count):
                    along[lead + m, tile, pl.ds(place, count)] = piece[m * count : (m + 1) * count]

    def blur_block(block):
        start = pl.multiple_of(block * BLOCK, 8)
        blur_along(raw, start, BLOCK, pl.multiple_of(start + HALO, 8))

    def blur_across(blur, copied):
        factors = [weight[i] for i in range(taps)]
        start = blur * BLOCK + HALO - 8 - half
        place = (blur + 1) * BLOCK

        def one_map(m, carry):
            for tile in range(tiles + 1):
                for group in range(BLOCK // 8):
                    base = start + 8 * group
                    value = factors[0] * along[m, tile, pl.ds(base, 8)]
                    for i in range(1, taps):
                        value += factors[i] * along[m, tile, pl.ds(base + i, 8)]
                    out_ref[
                        core * frames + m, tile, pl.ds(pl.multiple_of(place + 8 * group, 8), 8)
                    ] = value
            return carry

        lax.fori_loop(0, frames, one_map, 0)
        if copied:
            pair_copy(blur).start()

    def stack(first, count, unroll):
        def one_trial(trial, carry):
            stack_rows(shifts_ref, out_ref, done_ref, trial, first, count, 0, unroll)
            return carry

        lax.fori_loop(0, trials, one_trial, 0)


    def own_block(block, carry):
        blur_block(block)
        return carry

    def own_blur(blur, carry):
        blur_across(blur, True)
        return carry

    def own_wait(blur, carry):
        from_partner(blur)
        return carry

    lax.fori_loop(chip * per, chip * per + per, own_block, 0)
    lax.fori_loop(chip * per + 1, chip * per + per, own_blur, 0)
    lax.fori_loop(chip * per + 1, chip * per + per, own_wait, 0)
    stack(pl.multiple_of((chip * per + 2) * BLOCK - 8, 8), BLOCK * (per - 3), 2)

    def stream(side, index):
        distance = index // per
        j = index % per
        origin = jnp.where(side == 1, chip + 1 + distance, chip - 1 - distance)
        present = (index >= 0) & (origin >= 0) & (origin < chips)
        edge = jnp.where(side == 1, origin == chips - 1, origin == 0)
        upward = (side == 1) != edge
        block = origin * per + jnp.where(upward, j, per - 1 - j)
        last = edge & (j == per - 1)
        return present, edge, upward, j, block, last

    def blurs(side, index, act):
        present, edge, upward, j, block, last = stream(side, index)
        count = jnp.where(present & jnp.logical_not(edge & (j == 0)), 1 + last.astype(jnp.int32), 0)
        begin = jnp.where(upward, block, block + 1)
        turn = jnp.where(upward, 1, -1)

        def one(k, carry):
            act(begin + turn * k)
            return carry

        lax.fori_loop(0, count, one, 0)

    def arrive(index):
        present, edge, _, j, block, _ = stream(1, index)

        @pl.when(present)
        def _():
            line_copy(block, True).wait_recv()

            @pl.when(has_left)
            def _():
                line_copy(block, False).start()

            @pl.when(edge & (j == 1) & has_next)
            def _():
                halo_copy(True).start()

        present, edge, _, j, block, _ = stream(0, index)

        @pl.when(present)
        def _():
            line_copy(block, False).wait_recv()

            @pl.when(has_right)
            def _():
                line_copy(block, True).start()

            @pl.when(edge & (j == 1) & has_prev)
            def _():
                halo_copy(False).start()

    def blur_side(index):
        def one_side(side, carry):
            present, _, _, _, block, _ = stream(side, index)

            @pl.when(present)
            def _():
                blur_block(block)

            blurs(side, index, lambda blur: blur_across(blur, True))
            return carry

        lax.fori_loop(0, 2, one_side, 0)

    def stack_side(index):
        def one_side(side, carry):
            present, edge, upward, j, block, last = stream(side, index)
            blurs(side, index, from_partner)

            @pl.when(present & jnp.logical_not(last) & (jnp.logical_not(edge) | (j > 2)))
            def _():
                stack(
                    pl.multiple_of(jnp.where(upward, block - 1, block + 2) * BLOCK - 8, 8), BLOCK, True
                )

            @pl.when(present & last & ((side == 1) != low))
            def _():
                stack(pl.multiple_of((block - 1) * BLOCK - 8, 8), CLOSING, 4)

            return carry

        lax.fori_loop(0, 2, one_side, 0)

    limit = steps - 2
    mirror = chips - 1 - chip
    top_step = jnp.minimum(jnp.maximum(per * (mirror - 1) + 4, per * (chip - 1) + 2), limit)
    bottom_step = jnp.minimum(jnp.maximum(per * (chip - 1) + 4, per * (mirror - 1) + 2), limit)

    def step(index, carry):
        @pl.when(index < steps)
        def _():
            arrive(index)
            blur_side(index)

        @pl.when(index == top_step)
        def _():
            @pl.when(has_prev)
            def _():
                halo_copy(True).wait_recv()
                blur_along(top, 0, HALO, 0)

            @pl.when(jnp.logical_not(has_prev))
            def _():
                for m in range(frames):
                    for tile in range(tiles + 1):
                        along[m, tile, pl.ds(0, HALO)] = jnp.zeros((HALO, LANES), jnp.float32)

            blur_across(-1, False)
            blur_across(0, False)

            @pl.when(jnp.logical_not(has_prev))
            def _():
                for m in range(frames):
                    for tile in range(tiles + 1):
                        out_ref[core * frames + m, tile, pl.ds(0, ABOVE)] = jnp.zeros(
                            (ABOVE, LANES), jnp.float32
                        )

            pair_copy(-1).start()
            pair_copy(0).start()

        @pl.when(index == bottom_step)
        def _():
            @pl.when(has_next)
            def _():
                halo_copy(False).wait_recv()
                blur_along(bottom, 0, HALO, rows + HALO)

            @pl.when(jnp.logical_not(has_next))
            def _():
                for m in range(frames):
                    for tile in range(tiles + 1):
                        along[m, tile, pl.ds(rows + HALO, HALO)] = jnp.zeros(
                            (HALO, LANES), jnp.float32
                        )

            blur_across(blocks, False)
            blur_across(blocks + 1, False)

            @pl.when(jnp.logical_not(has_next))
            def _():
                for m in range(frames):
                    for tile in range(tiles + 1):
                        out_ref[core * frames + m, tile, pl.ds(rows + ABOVE, ABOVE)] = jnp.zeros(
                            (ABOVE, LANES), jnp.float32
                        )

            pair_copy(blocks).start()
            pair_copy(blocks + 1).start()

        stack_side(index - 1)

        @pl.when(index - 1 == top_step)
        def _():
            from_partner(-1)
            from_partner(0)
            stack(0, ABOVE, True)

        @pl.when(index - 1 == bottom_step)
        def _():
            from_partner(blocks)
            from_partner(blocks + 1)
            stack(rows - ABOVE, ABOVE, True)

        return carry

    lax.fori_loop(0, steps + 1, step, 0)

    mine = out_ref.at[pl.ds(core * frames, frames)]
    pltpu.make_async_copy(mine, mine, pair_send).wait()
    trade_copy(psi_ref).wait_send()

    def drain(origin, carry):
        part = raw.at[:, pl.ds(pl.multiple_of(origin * (2 * share), 8), 2 * share)]

        @pl.when(has_right & (origin <= chip))
        def _():
            pltpu.make_async_copy(part, part, right_sem.at[origin]).wait()

        @pl.when(has_left & (origin >= chip))
        def _():
            pltpu.make_async_copy(part, part, left_sem.at[origin]).wait()

        return carry

    lax.fori_loop(0, chips, drain, 0)

    @pl.when(has_next)
    def _():
        halo_copy(True).wait_send()

    @pl.when(has_prev)
    def _():
        halo_copy(False).wait_send()


def per_device(vels, skies, psi_maps, phi_maps, psf_taps, shifts):
    frames, share, width = psi_maps.shape
    maps = 2 * frames
    tiles = width // LANES
    rows = share * vels
    trials = shifts.shape[0]
    blocks = rows // BLOCK
    taps = psf_taps.shape[0]
    shifts = pltpu.with_memory_space_constraint(jnp.transpose(shifts, (1, 2, 0)), pltpu.HBM)
    psf_taps = pltpu.with_memory_space_constraint(psf_taps, pltpu.HBM)
    psi_maps = pltpu.with_memory_space_constraint(psi_maps, pltpu.HBM)
    phi_maps = pltpu.with_memory_space_constraint(phi_maps, pltpu.HBM)
    dma = pltpu.SemaphoreType.DMA
    blurred, done = pl.pallas_call(
        functools.partial(gather_kernel, vels, skies),
        out_shape=(
            jax.ShapeDtypeStruct((maps, tiles + 1, rows + 2 * ABOVE, LANES), jnp.float32),
            jax.ShapeDtypeStruct((trials, rows, width), jnp.float32),
        ),
        in_specs=[
            pl.BlockSpec(memory_space=pl.ANY),
            pl.BlockSpec(memory_space=pl.ANY),
            pl.BlockSpec(memory_space=pl.ANY),
            pl.BlockSpec(memory_space=pl.ANY),
        ],
        out_specs=(pl.BlockSpec(memory_space=pltpu.VMEM), pl.BlockSpec(memory_space=pltpu.VMEM)),
        scratch_shapes=[
            pltpu.SMEM((taps,), jnp.float32),
            pltpu.SMEM(shifts.shape, jnp.int32),
            pltpu.VMEM((frames, rows, width), jnp.float32),
            pltpu.VMEM((frames, tiles + 1, rows + 2 * HALO, LANES), jnp.float32),
            pltpu.VMEM((blocks + 3, frames, tiles + 1, BLOCK, LANES), jnp.float32),
            pltpu.VMEM((frames, HALO, width), jnp.float32),
            pltpu.VMEM((frames, HALO, width), jnp.float32),
            pltpu.VMEM((9 * LANES, LANES), jnp.bfloat16),
            pltpu.VMEM((6 * LANES, LANES), jnp.bfloat16),
            pltpu.VMEM((taps, 8, LANES), jnp.float32),
            dma((2,)),
            dma,
            dma((2,)),
            dma((blocks,)),
            dma((vels // 2,)),
            dma((vels // 2,)),
            dma,
            dma((blocks + 3,)),
            dma((2,)),
            dma((2,)),
        ],
        compiler_params=pltpu.CompilerParams(
            collective_id=0, has_side_effects=True, vmem_limit_bytes=24 * 2**20
        ),
        name="gather",
    )(psf_taps, shifts, psi_maps, phi_maps)
    return pl.pallas_call(
        functools.partial(stack_kernel, vels),
        out_shape=jax.ShapeDtypeStruct((trials, rows, width), jnp.float32),
        in_specs=[
            pl.BlockSpec(memory_space=pl.ANY),
            pl.BlockSpec(memory_space=pltpu.VMEM),
            pl.BlockSpec(memory_space=pltpu.VMEM),
        ],
        out_specs=pl.BlockSpec(memory_space=pl.ANY),
        scratch_shapes=[
            pltpu.SMEM(shifts.shape, jnp.int32),
            pltpu.VMEM((trials, CLOSING, width), jnp.float32),
            dma,
            dma((3, trials)),
        ],
        compiler_params=pltpu.CompilerParams(vmem_limit_bytes=4 * 2**20),
        name="stack",
    )(shifts, blurred, done)


def solution(mesh):
    return jax.shard_map(
        functools.partial(per_device, mesh.shape["vel"], mesh.shape["sky"]),
        mesh=mesh,
        in_specs=(
            P(None, ("sky", "vel"), None),
            P(None, ("sky", "vel"), None),
            P(),
            P("vel", None, None),
        ),
        out_specs=P("vel", "sky", None),
        check_vma=False,
    )
```

```python
import functools
import jax
import jax.numpy as jnp
from jax import lax
from jax.experimental import pallas as pl
from jax.experimental.pallas import tpu as pltpu
from jax.sharding import PartitionSpec as P

SHIFT = 16
BLOCK = 16
HALO = 2 * BLOCK
ABOVE = BLOCK + 8
CLOSING = 4 * BLOCK
LANES = 128
MESH = pl.DeviceIdType.MESH


def stack_rows(shifts_ref, maps_ref, out_ref, trial, first, count, skip, unroll):
    frames = shifts_ref.shape[0]
    tiles = maps_ref.shape[1]
    lane = lax.broadcasted_iota(jnp.int32, (8, LANES), 1)
    down, turn, inside = [], [], []
    for frame in range(1, frames):
        offset = shifts_ref[frame, 1, trial] + SHIFT
        down.append(shifts_ref[frame, 0, trial] + ABOVE)
        turn.append(lax.rem(LANES - offset, LANES))
        inside.append(lane >= offset)

    def one_group(group, carry):
        base = first + group * 8

        def stacked(kind):
            total = [
                maps_ref[kind * frames, tile, pl.ds(pl.multiple_of(base + ABOVE, 8), 8)]
                for tile in range(tiles - 1)
            ]
            for step in range(frames - 1):
                m = kind * frames + step + 1
                pieces = [maps_ref[m, tile, pl.ds(base + down[step], 8)] for tile in range(tiles)]
                for tile in range(tiles - 1):
                    joined = jnp.where(inside[step], pieces[tile], pieces[tile + 1])
                    total[tile] = total[tile] + pltpu.roll(joined, turn[step], 1)
            return total

        psi = stacked(0)
        phi = stacked(1)
        for tile in range(tiles - 1):
            out_ref[
                trial, pl.ds(pl.multiple_of(base - skip, 8), 8), tile * LANES : (tile + 1) * LANES
            ] = psi[tile] * lax.rsqrt(phi[tile])
        return carry

    lax.fori_loop(0, count // 8, one_group, 0, unroll=unroll)


def closing_row(chips, per, low):
    block = jnp.where(low, per * (chips - 1), per - 1)
    return pl.multiple_of(BLOCK * (block - 1) - 8, 8)


def stack_kernel(vels, shifts_hbm, maps_ref, done_ref, out_ref, shifts_ref, closing, shifts_sem, sems):
    shifts_copy = pltpu.make_async_copy(shifts_hbm, shifts_ref, shifts_sem)
    shifts_copy.start()
    trials, rows, _ = done_ref.shape
    chips = vels // 2
    per = rows // (chips * BLOCK)
    low = lax.axis_index("vel") // 2 < chips // 2
    first = closing_row(chips, per, low)
    small = BLOCK * (per - 2) - 8
    large = rows - CLOSING - small
    large_row = pl.multiple_of(jnp.where(low, 0, small + CLOSING), 8)
    small_row = pl.multiple_of(jnp.where(low, large + CLOSING, 0), 8)

    def large_copy(trial):
        part = pl.ds(large_row, large)
        return pltpu.make_async_copy(done_ref.at[trial, part], out_ref.at[trial, part], sems.at[0, trial])

    def small_copy(trial):
        part = pl.ds(small_row, small)
        return pltpu.make_async_copy(done_ref.at[trial, part], out_ref.at[trial, part], sems.at[1, trial])

    def closing_copy(trial):
        part = pl.ds(first, CLOSING)
        return pltpu.make_async_copy(closing.at[trial], out_ref.at[trial, part], sems.at[2, trial])

    def begin(trial, carry):
        large_copy(trial).start()
        small_copy(trial).start()
        return carry

    lax.fori_loop(0, trials, begin, 0)
    shifts_copy.wait()

    def compute(trial, carry):
        stack_rows(shifts_ref, maps_ref, closing, trial, first, CLOSING, first, True)
        closing_copy(trial).start()
        return carry

    lax.fori_loop(0, trials, compute, 0)

    def finish(trial, carry):
        large_copy(trial).wait()
        small_copy(trial).wait()
        closing_copy(trial).wait()
        return carry

    lax.fori_loop(0, trials, finish, 0)


def gather_kernel(
    vels, skies, taps_hbm, shifts_hbm, psi_ref, phi_ref, out_ref, done_ref,
    taps_ref, shifts_ref,
    raw, along, landing, top, bottom, band0, band1, weight,
    answers, small_sems, own_sem, trade_sems, recv_sem, right_sem, left_sem, pair_send, pair_recv, top_sems, bottom_sems,
):
    frames, share, width = psi_ref.shape
    trials = shifts_ref.shape[2]
    taps = taps_ref.shape[0]
    half = taps // 2
    chips = vels // 2
    tiles = width // LANES
    rows = vels * share
    blocks = rows // BLOCK
    per = blocks // chips
    steps = per * (chips - 1)
    sky = lax.axis_index("sky")
    vel = lax.axis_index("vel")
    chip = vel // 2
    core = vel % 2
    has_right = chip < chips - 1
    has_left = chip > 0
    has_next = sky < skies - 1
    has_prev = sky > 0
    low = chip < chips // 2
    partner = (sky, vel + 1 - 2 * core)

    taps_copy = pltpu.make_async_copy(taps_hbm, taps_ref, small_sems.at[0])
    shifts_copy = pltpu.make_async_copy(shifts_hbm, shifts_ref, small_sems.at[1])
    own_rows = pl.ds(pl.multiple_of(vel * share, 8), share)

    def own_copy(source):
        return pltpu.make_async_copy(source, raw.at[:, own_rows], own_sem)

    @pl.when(core == 0)
    def _():
        own_copy(psi_ref).start()

    @pl.when(core == 1)
    def _():
        own_copy(phi_ref).start()

    taps_copy.start()
    shifts_copy.start()
    left, right = (sky, vel - 2), (sky, vel + 2)
    before, after = (sky - 1, vel), (sky + 1, vel)
    skies_near = ((has_prev & (core == 1), before), (has_next & (core == 1), after))
    barrier = pltpu.get_barrier_semaphore()

    def greet(semaphore, device, present):
        @pl.when(present)
        def _():
            pl.semaphore_signal(semaphore, inc=1, device_id=device, device_id_type=MESH)

    greet(barrier, right, has_right)
    greet(barrier, partner, (core == 0) | (chip == 0))
    for present, device in skies_near:
        greet(barrier, device, present)
    callers = (has_left | (core == 0)).astype(jnp.int32) + core
    for present, device in skies_near:
        callers = callers + present.astype(jnp.int32)
    pl.semaphore_wait(barrier, callers)
    greet(answers.at[0], left, has_left)
    greet(answers.at[1], partner, core == 1)
    for present, device in skies_near:
        greet(answers.at[2], device, present)

    def trade_copy(source):
        return pltpu.make_async_remote_copy(
            src_ref=source,
            dst_ref=raw.at[:, own_rows],
            send_sem=trade_sems.at[0],
            recv_sem=trade_sems.at[1],
            device_id=partner,
            device_id_type=MESH,
        )

    def block_rows(block):
        return pl.ds(pl.multiple_of(block * BLOCK, 8), BLOCK)

    def line_copy(block, to_right, source=None):
        return pltpu.make_async_remote_copy(
            src_ref=raw.at[:, block_rows(block)] if source is None else source,
            dst_ref=raw.at[:, block_rows(block)],
            send_sem=(right_sem if to_right else left_sem).at[block // per],
            recv_sem=recv_sem.at[block],
            device_id=(sky, vel + 2) if to_right else (sky, vel - 2),
            device_id_type=MESH,
        )

    def halo_copy(to_next):
        source = raw.at[:, pl.ds(rows - HALO if to_next else 0, HALO)]
        sems = top_sems if to_next else bottom_sems
        return pltpu.make_async_remote_copy(
            src_ref=source,
            dst_ref=top if to_next else bottom,
            send_sem=sems.at[0],
            recv_sem=sems.at[1],
            device_id=(sky + 1, vel) if to_next else (sky - 1, vel),
            device_id_type=MESH,
        )

    def pair_rows(blur):
        return out_ref.at[
            pl.ds(core * frames, frames), :, pl.ds(pl.multiple_of((blur + 1) * BLOCK, 8), BLOCK)
        ]

    def pair_copy(blur):
        return pltpu.make_async_remote_copy(
            src_ref=pair_rows(blur),
            dst_ref=landing.at[blur + 1],
            send_sem=pair_send,
            recv_sem=pair_recv.at[blur + 1],
            device_id=partner,
            device_id_type=MESH,
        )

    def from_partner(blur):
        pair_copy(blur).wait_recv()
        place = pl.ds(pl.multiple_of((blur + 1) * BLOCK, 8), BLOCK)
        for m in range(frames):
            for tile in range(tiles + min(m, 1)):
                out_ref[(1 - core) * frames + m, tile, place] = landing[blur + 1, m, tile]

    right_up = chip == 0
    left_up = chip < chips - 1

    def send_half(to_right, upward, part, source=None):
        def one(index, carry):
            place = jnp.where(upward, index, per // 2 - 1 - index)
            rows_there = None if source is None else source.at[:, block_rows(place)]
            line_copy(chip * per + part * (per // 2) + place, to_right, rows_there).start()
            return carry

        lax.fori_loop(0, per // 2, one, 0)

    def send_first(to_right, upward, ready):
        for kind, source in ((0, psi_ref), (1, phi_ref)):

            @pl.when(ready & (core == kind))
            def _(source=source):
                send_half(to_right, upward, core, source)

    right_ready = right_up == (core == 0)
    left_ready = left_up == (core == 0)
    send_first(False, left_up, has_left & left_ready)

    @pl.when(core == 0)
    def _():
        pl.semaphore_wait(answers.at[1], 1)
        trade_copy(phi_ref).start()

    @pl.when(core == 1)
    def _():
        trade_copy(psi_ref).start()

    @pl.when(has_right)
    def _():
        pl.semaphore_wait(answers.at[0], 1)

    send_first(True, right_up, has_right & right_ready)
    own_copy(psi_ref).wait()
    taps_copy.wait()
    shifts_copy.wait()
    total = taps_ref[0]
    for i in range(1, taps):
        total = total + taps_ref[i]
    scale = 1.0 / jnp.full((8, LANES), total, jnp.float32)
    squared = jnp.full((8, LANES), core, jnp.int32) > 0
    for i in range(taps):
        value = jnp.full((8, LANES), taps_ref[i], jnp.float32) * scale
        weight[i] = jnp.where(squared, value * value, value)
    for lead, band in ((0, band0), (1, band1)):
        depth = (3 - lead) * LANES
        place = lax.broadcasted_iota(jnp.int32, (depth, LANES), 0)
        place = place - lax.broadcasted_iota(jnp.int32, (depth, LANES), 1)
        spot = place - (LANES - SHIFT * lead - half)
        matrix = jnp.zeros((depth, LANES), jnp.float32)
        for i in range(taps):
            value = jnp.broadcast_to(weight[i][:1], (depth, LANES))
            matrix = jnp.where(spot == i, value, matrix)
        coarse = matrix.astype(jnp.bfloat16)
        band[:depth] = coarse
        band[depth : 2 * depth] = coarse
        band[2 * depth :] = (matrix - coarse.astype(jnp.float32)).astype(jnp.bfloat16)

    trade_copy(psi_ref).wait_recv()

    def send_rest(to_right, upward, present, ready):
        @pl.when(present)
        def _():
            send_half(to_right, upward, 1 - core)

        @pl.when(present & jnp.logical_not(ready))
        def _():
            send_half(to_right, upward, core)

    send_rest(False, left_up, has_left, left_ready)
    send_rest(True, right_up, has_right, right_ready)

    @pl.when(core == 1)
    def _():
        pl.semaphore_wait(answers.at[2], has_prev.astype(jnp.int32) + has_next.astype(jnp.int32))
        pl.semaphore_signal(answers.at[3], inc=1, device_id=partner, device_id_type=MESH)

    @pl.when(core == 0)
    def _():
        pl.semaphore_wait(answers.at[3], 1)

    @pl.when(has_next & (chip == chips - 1))
    def _():
        halo_copy(True).start()

    @pl.when(has_prev & (chip == 0))
    def _():
        halo_copy(False).start()

    def blur_along(source, start, count, place):
        def windows(values, lead):
            blank = jnp.zeros((values.shape[0], LANES), values.dtype)
            columns = [blank] + [values[:, t * LANES : (t + 1) * LANES] for t in range(tiles)] + [blank]
            wide = 3 - lead
            return jnp.concatenate(
                [jnp.concatenate(columns[t : t + wide], axis=1) for t in range(tiles + lead)], axis=0
            )

        for lead, band in ((0, band0), (1, band1)):
            if lead:
                values = source[1:frames, pl.ds(start, count)].reshape((frames - 1) * count, width)
            else:
                values = source[0, pl.ds(start, count)]
            height = values.shape[0]
            coarse = values.astype(jnp.bfloat16)
            fine = (values - coarse.astype(jnp.float32)).astype(jnp.bfloat16)
            high, rest = windows(coarse, lead), windows(fine, lead)
            blurred = jnp.dot(
                jnp.concatenate([high, rest, high], axis=1), band[...],
                preferred_element_type=jnp.float32,
            )
            for tile in range(tiles + lead):
                piece = blurred[tile * height : (tile + 1) * height]
                if lead and tile in (0, tiles):
                    lane = lax.broadcasted_iota(jnp.int32, (height, LANES), 1)
                    piece = jnp.where(lane >= SHIFT if tile == 0 else lane < SHIFT, piece, 0.0)
                for m in range(height // count):
                    along[lead + m, tile, pl.ds(place, count)] = piece[m * count : (m + 1) * count]

    def blur_block(block):
        start = pl.multiple_of(block * BLOCK, 8)
        blur_along(raw, start, BLOCK, pl.multiple_of(start + HALO, 8))

    def blur_across(blur, copied):
        factors = [weight[i] for i in range(taps)]
        start = blur * BLOCK + HALO - 8 - half
        place = (blur + 1) * BLOCK

        def one_map(m, carry):
            for tile in range(tiles + 1):
                for group in range(BLOCK // 8):
                    base = start + 8 * group
                    value = factors[0] * along[m, tile, pl.ds(base, 8)]
                    for i in range(1, taps):
                        value += factors[i] * along[m, tile, pl.ds(base + i, 8)]
                    out_ref[
                        core * frames + m, tile, pl.ds(pl.multiple_of(place + 8 * group, 8), 8)
                    ] = value
            return carry

        lax.fori_loop(0, frames, one_map, 0)
        if copied:
            pair_copy(blur).start()

    def stack(first, count, unroll):
        def one_trial(trial, carry):
            stack_rows(shifts_ref, out_ref, done_ref, trial, first, count, 0, unroll)
            return carry

        lax.fori_loop(0, trials, one_trial, 0)


    def own_block(block, carry):
        blur_block(block)
        return carry

    def own_blur(blur, carry):
        blur_across(blur, True)
        return carry

    def own_wait(blur, carry):
        from_partner(blur)
        return carry

    lax.fori_loop(chip * per, chip * per + per, own_block, 0)
    lax.fori_loop(chip * per + 1, chip * per + per, own_blur, 0)
    lax.fori_loop(chip * per + 1, chip * per + per, own_wait, 0)
    stack(pl.multiple_of((chip * per + 2) * BLOCK - 8, 8), BLOCK * (per - 3), 2)

    def stream(side, index):
        distance = index // per
        j = index % per
        origin = jnp.where(side == 1, chip + 1 + distance, chip - 1 - distance)
        present = (index >= 0) & (origin >= 0) & (origin < chips)
        edge = jnp.where(side == 1, origin == chips - 1, origin == 0)
        upward = (side == 1) != edge
        block = origin * per + jnp.where(upward, j, per - 1 - j)
        last = edge & (j == per - 1)
        return present, edge, upward, j, block, last

    def blurs(side, index, act):
        present, edge, upward, j, block, last = stream(side, index)
        count = jnp.where(present & jnp.logical_not(edge & (j == 0)), 1 + last.astype(jnp.int32), 0)
        begin = jnp.where(upward, block, block + 1)
        turn = jnp.where(upward, 1, -1)

        def one(k, carry):
            act(begin + turn * k)
            return carry

        lax.fori_loop(0, count, one, 0)

    def arrive(index):
        present, edge, _, j, block, _ = stream(1, index)

        @pl.when(present)
        def _():
            line_copy(block, True).wait_recv()

            @pl.when(has_left)
            def _():
                line_copy(block, False).start()

            @pl.when(edge & (j == 1) & has_next)
            def _():
                halo_copy(True).start()

        present, edge, _, j, block, _ = stream(0, index)

        @pl.when(present)
        def _():
            line_copy(block, False).wait_recv()

            @pl.when(has_right)
            def _():
                line_copy(block, True).start()

            @pl.when(edge & (j == 1) & has_prev)
            def _():
                halo_copy(False).start()

    def blur_side(index):
        def one_side(side, carry):
            present, _, _, _, block, _ = stream(side, index)

            @pl.when(present)
            def _():
                blur_block(block)

            blurs(side, index, lambda blur: blur_across(blur, True))
            return carry

        lax.fori_loop(0, 2, one_side, 0)

    def stack_side(index):
        def one_side(side, carry):
            present, edge, upward, j, block, last = stream(side, index)
            blurs(side, index, from_partner)

            @pl.when(present & jnp.logical_not(last) & (jnp.logical_not(edge) | (j > 2)))
            def _():
                stack(
                    pl.multiple_of(jnp.where(upward, block - 1, block + 2) * BLOCK - 8, 8), BLOCK, True
                )

            @pl.when(present & last & ((side == 1) != low))
            def _():
                stack(pl.multiple_of((block - 1) * BLOCK - 8, 8), CLOSING, 4)

            return carry

        lax.fori_loop(0, 2, one_side, 0)

    limit = steps - 2
    mirror = chips - 1 - chip
    top_step = jnp.minimum(jnp.maximum(per * (mirror - 1) + 4, per * (chip - 1) + 2), limit)
    bottom_step = jnp.minimum(jnp.maximum(per * (chip - 1) + 4, per * (mirror - 1) + 2), limit)

    def step(index, carry):
        @pl.when(index < steps)
        def _():
            arrive(index)
            blur_side(index)

        @pl.when(index == top_step)
        def _():
            @pl.when(has_prev)
            def _():
                halo_copy(True).wait_recv()
                blur_along(top, 0, HALO, 0)

            @pl.when(jnp.logical_not(has_prev))
            def _():
                for m in range(frames):
                    for tile in range(tiles + 1):
                        along[m, tile, pl.ds(0, HALO)] = jnp.zeros((HALO, LANES), jnp.float32)

            blur_across(-1, False)
            blur_across(0, False)

            @pl.when(jnp.logical_not(has_prev))
            def _():
                for m in range(frames):
                    for tile in range(tiles + 1):
                        out_ref[core * frames + m, tile, pl.ds(0, ABOVE)] = jnp.zeros(
                            (ABOVE, LANES), jnp.float32
                        )

            pair_copy(-1).start()
            pair_copy(0).start()

        @pl.when(index == bottom_step)
        def _():
            @pl.when(has_next)
            def _():
                halo_copy(False).wait_recv()
                blur_along(bottom, 0, HALO, rows + HALO)

            @pl.when(jnp.logical_not(has_next))
            def _():
                for m in range(frames):
                    for tile in range(tiles + 1):
                        along[m, tile, pl.ds(rows + HALO, HALO)] = jnp.zeros(
                            (HALO, LANES), jnp.float32
                        )

            blur_across(blocks, False)
            blur_across(blocks + 1, False)

            @pl.when(jnp.logical_not(has_next))
            def _():
                for m in range(frames):
                    for tile in range(tiles + 1):
                        out_ref[core * frames + m, tile, pl.ds(rows + ABOVE, ABOVE)] = jnp.zeros(
                            (ABOVE, LANES), jnp.float32
                        )

            pair_copy(blocks).start()
            pair_copy(blocks + 1).start()

        stack_side(index - 1)

        @pl.when(index - 1 == top_step)
        def _():
            from_partner(-1)
            from_partner(0)
            stack(0, ABOVE, True)

        @pl.when(index - 1 == bottom_step)
        def _():
            from_partner(blocks)
            from_partner(blocks + 1)
            stack(rows - ABOVE, ABOVE, True)

        return carry

    lax.fori_loop(0, steps + 1, step, 0)

    mine = out_ref.at[pl.ds(core * frames, frames)]
    pltpu.make_async_copy(mine, mine, pair_send).wait()
    trade_copy(psi_ref).wait_send()

    def drain(origin, carry):
        part = raw.at[:, pl.ds(pl.multiple_of(origin * (2 * share), 8), 2 * share)]

        @pl.when(has_right & (origin <= chip))
        def _():
            pltpu.make_async_copy(part, part, right_sem.at[origin]).wait()

        @pl.when(has_left & (origin >= chip))
        def _():
            pltpu.make_async_copy(part, part, left_sem.at[origin]).wait()

        return carry

    lax.fori_loop(0, chips, drain, 0)

    @pl.when(has_next)
    def _():
        halo_copy(True).wait_send()

    @pl.when(has_prev)
    def _():
        halo_copy(False).wait_send()


def per_device(vels, skies, psi_maps, phi_maps, psf_taps, shifts):
    frames, share, width = psi_maps.shape
    maps = 2 * frames
    tiles = width // LANES
    rows = share * vels
    trials = shifts.shape[0]
    blocks = rows // BLOCK
    taps = psf_taps.shape[0]
    shifts = pltpu.with_memory_space_constraint(jnp.transpose(shifts, (1, 2, 0)), pltpu.HBM)
    psf_taps = pltpu.with_memory_space_constraint(psf_taps, pltpu.HBM)
    psi_maps = pltpu.with_memory_space_constraint(psi_maps, pltpu.HBM)
    phi_maps = pltpu.with_memory_space_constraint(phi_maps, pltpu.HBM)
    dma = pltpu.SemaphoreType.DMA
    blurred, done = pl.pallas_call(
        functools.partial(gather_kernel, vels, skies),
        out_shape=(
            jax.ShapeDtypeStruct((maps, tiles + 1, rows + 2 * ABOVE, LANES), jnp.float32),
            jax.ShapeDtypeStruct((trials, rows, width), jnp.float32),
        ),
        in_specs=[
            pl.BlockSpec(memory_space=pl.ANY),
            pl.BlockSpec(memory_space=pl.ANY),
            pl.BlockSpec(memory_space=pl.ANY),
            pl.BlockSpec(memory_space=pl.ANY),
        ],
        out_specs=(pl.BlockSpec(memory_space=pltpu.VMEM), pl.BlockSpec(memory_space=pltpu.VMEM)),
        scratch_shapes=[
            pltpu.SMEM((taps,), jnp.float32),
            pltpu.SMEM(shifts.shape, jnp.int32),
            pltpu.VMEM((frames, rows, width), jnp.float32),
            pltpu.VMEM((frames, tiles + 1, rows + 2 * HALO, LANES), jnp.float32),
            pltpu.VMEM((blocks + 3, frames, tiles + 1, BLOCK, LANES), jnp.float32),
            pltpu.VMEM((frames, HALO, width), jnp.float32),
            pltpu.VMEM((frames, HALO, width), jnp.float32),
            pltpu.VMEM((9 * LANES, LANES), jnp.bfloat16),
            pltpu.VMEM((6 * LANES, LANES), jnp.bfloat16),
            pltpu.VMEM((taps, 8, LANES), jnp.float32),
            pltpu.SemaphoreType.REGULAR((4,)),
            dma((2,)),
            dma,
            dma((2,)),
            dma((blocks,)),
            dma((vels // 2,)),
            dma((vels // 2,)),
            dma,
            dma((blocks + 3,)),
            dma((2,)),
            dma((2,)),
        ],
        compiler_params=pltpu.CompilerParams(
            collective_id=0, has_side_effects=True, vmem_limit_bytes=24 * 2**20
        ),
        name="gather",
    )(psf_taps, shifts, psi_maps, phi_maps)
    return pl.pallas_call(
        functools.partial(stack_kernel, vels),
        out_shape=jax.ShapeDtypeStruct((trials, rows, width), jnp.float32),
        in_specs=[
            pl.BlockSpec(memory_space=pl.ANY),
            pl.BlockSpec(memory_space=pltpu.VMEM),
            pl.BlockSpec(memory_space=pltpu.VMEM),
        ],
        out_specs=pl.BlockSpec(memory_space=pl.ANY),
        scratch_shapes=[
            pltpu.SMEM(shifts.shape, jnp.int32),
            pltpu.VMEM((trials, CLOSING, width), jnp.float32),
            dma,
            dma((3, trials)),
        ],
        compiler_params=pltpu.CompilerParams(vmem_limit_bytes=4 * 2**20),
        name="stack",
    )(shifts, blurred, done)


def solution(mesh):
    return jax.shard_map(
        functools.partial(per_device, mesh.shape["vel"], mesh.shape["sky"]),
        mesh=mesh,
        in_specs=(
            P(None, ("sky", "vel"), None),
            P(None, ("sky", "vel"), None),
            P(),
            P("vel", None, None),
        ),
        out_specs=P("vel", "sky", None),
        check_vma=False,
    )
```

```python
import functools
import jax
import jax.numpy as jnp
from jax import lax
from jax.experimental import pallas as pl
from jax.experimental.pallas import tpu as pltpu
from jax.sharding import PartitionSpec as P

SHIFT = 16
BLOCK = 16
HALO = 2 * BLOCK
ABOVE = BLOCK + 8
JOIN = 4 * BLOCK
LANES = 128
MESH = pl.DeviceIdType.MESH


def stack_rows(shifts_ref, maps_ref, out_ref, trial, first, count, skip, partial, unroll):
    frames = shifts_ref.shape[0]
    tiles = maps_ref.shape[1]
    lane = lax.broadcasted_iota(jnp.int32, (8, LANES), 1)
    down, turn, inside = [], [], []
    for frame in range(1, frames):
        offset = shifts_ref[frame, 1, trial] + SHIFT
        down.append(shifts_ref[frame, 0, trial] + ABOVE)
        turn.append(lax.rem(LANES - offset, LANES))
        inside.append(lane >= offset)

    def one_group(group, carry):
        base = first + group * 8

        def stacked(kind):
            total = [None] * (tiles - 1)
            if not partial:
                total = [
                    maps_ref[kind * frames, tile, pl.ds(pl.multiple_of(base + ABOVE, 8), 8)]
                    for tile in range(tiles - 1)
                ]
            for step in range(frames - 1):
                m = kind * frames + step + 1
                pieces = [maps_ref[m, tile, pl.ds(base + down[step], 8)] for tile in range(tiles)]
                for tile in range(tiles - 1):
                    joined = jnp.where(inside[step], pieces[tile], pieces[tile + 1])
                    moved = pltpu.roll(joined, turn[step], 1)
                    total[tile] = moved if total[tile] is None else total[tile] + moved
            return total

        psi = stacked(0)
        phi = stacked(1)
        rows = pl.ds(pl.multiple_of(base - skip, 8), 8)
        for tile in range(tiles - 1):
            columns = slice(tile * LANES, (tile + 1) * LANES)
            if partial:
                out_ref[0, trial, rows, columns] = psi[tile]
                out_ref[1, trial, rows, columns] = phi[tile]
            else:
                out_ref[trial, rows, columns] = psi[tile] * lax.rsqrt(phi[tile])
        return carry

    lax.fori_loop(0, count // 8, one_group, 0, unroll=unroll)


def last_row(chips, per, to_right):
    return pl.multiple_of(jnp.where(to_right, ABOVE, BLOCK * per * (chips - 1) - ABOVE), 8)


def finish_kernel(vels, part_ref, fresh_ref, done_ref, out_ref, closing, sems):
    trials, rows, width = done_ref.shape
    count = part_ref.shape[2]
    chips = vels // 2
    low = lax.axis_index("vel") // 2 < chips // 2
    first = last_row(chips, count // BLOCK, jnp.logical_not(low))
    small = ABOVE
    large = rows - count - small
    large_row = pl.multiple_of(jnp.where(low, 0, small + count), 8)
    small_row = pl.multiple_of(jnp.where(low, large + count, 0), 8)

    def large_copy(trial):
        part = pl.ds(large_row, large)
        return pltpu.make_async_copy(done_ref.at[trial, part], out_ref.at[trial, part], sems.at[0, trial])

    def small_copy(trial):
        part = pl.ds(small_row, small)
        return pltpu.make_async_copy(done_ref.at[trial, part], out_ref.at[trial, part], sems.at[1, trial])

    def closing_copy(trial):
        part = pl.ds(first, count)
        return pltpu.make_async_copy(closing.at[trial], out_ref.at[trial, part], sems.at[2, trial])

    def begin(trial, carry):
        large_copy(trial).start()
        small_copy(trial).start()
        return carry

    lax.fori_loop(0, trials, begin, 0)

    def compute(trial, carry):
        for tile in range(width // LANES):
            columns = slice(tile * LANES, (tile + 1) * LANES)
            psi = part_ref[0, trial, :, columns] + fresh_ref[0, 0, tile]
            phi = part_ref[1, trial, :, columns] + fresh_ref[0, 1, tile]
            closing[trial, :, columns] = psi * lax.rsqrt(phi)
        closing_copy(trial).start()
        return carry

    lax.fori_loop(0, trials, compute, 0)

    def finish(trial, carry):
        large_copy(trial).wait()
        small_copy(trial).wait()
        closing_copy(trial).wait()
        return carry

    lax.fori_loop(0, trials, finish, 0)


def gather_kernel(
    vels, skies, taps_hbm, shifts_hbm, psi_ref, phi_ref, part_ref, fresh_ref, done_ref,
    taps_ref, shifts_ref, blurred, raw, along, landing, top, bottom, band0, band1, weight,
    answers, small_sems, own_sem, trade_sems, recv_sem, right_sem, left_sem, pair_sends, pair_recv, top_sems, bottom_sems,
    first_sems, fresh_send, fresh_recv,
):
    frames, share, width = psi_ref.shape
    trials = shifts_ref.shape[2]
    taps = taps_ref.shape[0]
    half = taps // 2
    chips = vels // 2
    tiles = width // LANES
    rows = vels * share
    blocks = rows // BLOCK
    per = blocks // chips
    steps = per * (chips - 1)
    sky = lax.axis_index("sky")
    vel = lax.axis_index("vel")
    chip = vel // 2
    core = vel % 2
    has_right = chip < chips - 1
    has_left = chip > 0
    has_next = sky < skies - 1
    has_prev = sky > 0
    low = chip < chips // 2
    partner = (sky, vel + 1 - 2 * core)

    taps_copy = pltpu.make_async_copy(taps_hbm, taps_ref, small_sems.at[0])
    shifts_copy = pltpu.make_async_copy(shifts_hbm, shifts_ref, small_sems.at[1])
    own_rows = pl.ds(pl.multiple_of(vel * share, 8), share)

    def own_copy(source):
        return pltpu.make_async_copy(source, raw.at[:, own_rows], own_sem)

    @pl.when(core == 0)
    def _():
        own_copy(psi_ref).start()

    @pl.when(core == 1)
    def _():
        own_copy(phi_ref).start()

    taps_copy.start()
    shifts_copy.start()
    left, right = (sky, vel - 2), (sky, vel + 2)
    before, after = (sky - 1, vel), (sky + 1, vel)
    skies_near = ((has_prev & (core == 1), before), (has_next & (core == 1), after))
    barrier = pltpu.get_barrier_semaphore()

    def greet(semaphore, device, present):
        @pl.when(present)
        def _():
            pl.semaphore_signal(semaphore, inc=1, device_id=device, device_id_type=MESH)

    greet(barrier, right, has_right)
    greet(barrier, partner, (core == 0) | (chip == 0))
    for present, device in skies_near:
        greet(barrier, device, present)
    callers = (has_left | (core == 0)).astype(jnp.int32) + core
    for present, device in skies_near:
        callers = callers + present.astype(jnp.int32)
    pl.semaphore_wait(barrier, callers)
    greet(answers.at[0], left, has_left)
    greet(answers.at[1], partner, core == 1)
    for present, device in skies_near:
        greet(answers.at[2], device, present)

    def trade_copy(source):
        return pltpu.make_async_remote_copy(
            src_ref=source,
            dst_ref=raw.at[:, own_rows],
            send_sem=trade_sems.at[0],
            recv_sem=trade_sems.at[1],
            device_id=partner,
            device_id_type=MESH,
        )

    def block_rows(block):
        return pl.ds(pl.multiple_of(block * BLOCK, 8), BLOCK)

    def line_copy(block, to_right, late, source=None):
        maps = pl.ds(1, frames - 1) if late else pl.ds(0, frames)
        place = raw.at[maps, block_rows(block)]
        return pltpu.make_async_remote_copy(
            src_ref=place if source is None else source[0].at[maps, block_rows(source[1])],
            dst_ref=place,
            send_sem=(right_sem if to_right else left_sem).at[block // per],
            recv_sem=recv_sem.at[block],
            device_id=(sky, vel + 2) if to_right else (sky, vel - 2),
            device_id_type=MESH,
        )

    def send_block(block, to_right, source=None):
        if to_right:
            late = (block < per) & (block > 1)
        else:
            late = (block >= blocks - per) & (block < blocks - 2)

        @pl.when(late)
        def _():
            line_copy(block, to_right, True, source).start()

        @pl.when(jnp.logical_not(late))
        def _():
            line_copy(block, to_right, False, source).start()

    def first_row(to_right):
        return HALO if to_right else BLOCK * per * (chips - 1)

    def first_copy(to_right):
        place = raw.at[0, pl.ds(first_row(to_right), BLOCK * (per - 2))]
        return pltpu.make_async_remote_copy(
            src_ref=place,
            dst_ref=place,
            send_sem=right_sem.at[0] if to_right else left_sem.at[chips - 1],
            recv_sem=first_sems.at[1 if to_right else 0],
            device_id=(sky, vel + 2) if to_right else (sky, vel - 2),
            device_id_type=MESH,
        )

    def fresh_copy(slot):
        place = fresh_ref.at[slot, core]
        return pltpu.make_async_remote_copy(
            src_ref=place,
            dst_ref=place,
            send_sem=fresh_send.at[slot],
            recv_sem=fresh_recv.at[slot],
            device_id=partner,
            device_id_type=MESH,
        )

    def halo_copy(to_next):
        source = raw.at[:, pl.ds(rows - HALO if to_next else 0, HALO)]
        sems = top_sems if to_next else bottom_sems
        return pltpu.make_async_remote_copy(
            src_ref=source,
            dst_ref=top if to_next else bottom,
            send_sem=sems.at[0],
            recv_sem=sems.at[1],
            device_id=(sky + 1, vel) if to_next else (sky - 1, vel),
            device_id_type=MESH,
        )

    def pair_copy(blur, late):
        skip = 1 if late else 0
        place = pl.ds(pl.multiple_of((blur + 1) * BLOCK, 8), BLOCK)
        return pltpu.make_async_remote_copy(
            src_ref=blurred.at[pl.ds(core * frames + skip, frames - skip), :, place],
            dst_ref=landing.at[blur + 1, pl.ds(skip, frames - skip)],
            send_sem=pair_sends.at[skip],
            recv_sem=pair_recv.at[blur + 1],
            device_id=partner,
            device_id_type=MESH,
        )

    def to_partner(blur, late):
        @pl.when(late)
        def _():
            pair_copy(blur, True).start()

        @pl.when(jnp.logical_not(late))
        def _():
            pair_copy(blur, False).start()

    def from_partner(blur, late):
        place = pl.ds(pl.multiple_of((blur + 1) * BLOCK, 8), BLOCK)

        @pl.when(late)
        def _():
            pair_copy(blur, True).wait_recv()

        @pl.when(jnp.logical_not(late))
        def _():
            pair_copy(blur, False).wait_recv()
            for tile in range(tiles):
                blurred[(1 - core) * frames, tile, place] = landing[blur + 1, 0, tile]

        for m in range(1, frames):
            for tile in range(tiles + 1):
                blurred[(1 - core) * frames + m, tile, place] = landing[blur + 1, m, tile]

    right_up = chip == 0
    left_up = chip < chips - 1

    def send_half(to_right, upward, part, source=None):
        def one(index, carry):
            place = jnp.where(upward, index, per // 2 - 1 - index)
            there = None if source is None else (source, place)
            send_block(chip * per + part * (per // 2) + place, to_right, there)
            return carry

        lax.fori_loop(0, per // 2, one, 0)

    def send_first(to_right, upward, ready):
        for kind, source in ((0, psi_ref), (1, phi_ref)):

            @pl.when(ready & (core == kind))
            def _(source=source):
                send_half(to_right, upward, core, source)

    right_ready = right_up == (core == 0)
    left_ready = left_up == (core == 0)
    send_first(False, left_up, has_left & left_ready)

    @pl.when(core == 0)
    def _():
        pl.semaphore_wait(answers.at[1], 1)
        trade_copy(phi_ref).start()

    @pl.when(core == 1)
    def _():
        trade_copy(psi_ref).start()

    @pl.when(has_right)
    def _():
        pl.semaphore_wait(answers.at[0], 1)

    send_first(True, right_up, has_right & right_ready)
    own_copy(psi_ref).wait()
    taps_copy.wait()
    shifts_copy.wait()
    total = taps_ref[0]
    for i in range(1, taps):
        total = total + taps_ref[i]
    scale = 1.0 / jnp.full((8, LANES), total, jnp.float32)
    squared = jnp.full((8, LANES), core, jnp.int32) > 0
    for i in range(taps):
        value = jnp.full((8, LANES), taps_ref[i], jnp.float32) * scale
        weight[i] = jnp.where(squared, value * value, value)
    for lead, band in ((0, band0), (1, band1)):
        depth = (3 - lead) * LANES
        place = lax.broadcasted_iota(jnp.int32, (depth, LANES), 0)
        place = place - lax.broadcasted_iota(jnp.int32, (depth, LANES), 1)
        spot = place - (LANES - SHIFT * lead - half)
        matrix = jnp.zeros((depth, LANES), jnp.float32)
        for i in range(taps):
            value = jnp.broadcast_to(weight[i][:1], (depth, LANES))
            matrix = jnp.where(spot == i, value, matrix)
        coarse = matrix.astype(jnp.bfloat16)
        band[:depth] = coarse
        band[depth : 2 * depth] = coarse
        band[2 * depth :] = (matrix - coarse.astype(jnp.float32)).astype(jnp.bfloat16)

    trade_copy(psi_ref).wait_recv()

    def send_rest(to_right, upward, present, ready):
        @pl.when(present)
        def _():
            send_half(to_right, upward, 1 - core)

        @pl.when(present & jnp.logical_not(ready))
        def _():
            send_half(to_right, upward, core)

    send_rest(False, left_up, has_left, left_ready)
    send_rest(True, right_up, has_right, right_ready)

    @pl.when(chip == chips - 1)
    def _():
        first_copy(False).start()

    @pl.when(chip == 0)
    def _():
        first_copy(True).start()

    @pl.when(core == 1)
    def _():
        pl.semaphore_wait(answers.at[2], has_prev.astype(jnp.int32) + has_next.astype(jnp.int32))
        pl.semaphore_signal(answers.at[3], inc=1, device_id=partner, device_id_type=MESH)

    @pl.when(core == 0)
    def _():
        pl.semaphore_wait(answers.at[3], 1)

    @pl.when(has_next & (chip == chips - 1))
    def _():
        halo_copy(True).start()

    @pl.when(has_prev & (chip == 0))
    def _():
        halo_copy(False).start()

    def blur_along(source, start, count, place, lead):
        def windows(values, lead):
            blank = jnp.zeros((values.shape[0], LANES), values.dtype)
            columns = [blank] + [values[:, t * LANES : (t + 1) * LANES] for t in range(tiles)] + [blank]
            wide = 3 - lead
            return jnp.concatenate(
                [jnp.concatenate(columns[t : t + wide], axis=1) for t in range(tiles + lead)], axis=0
            )

        band = band1 if lead else band0
        if lead:
            values = source[1:frames, pl.ds(start, count)].reshape((frames - 1) * count, width)
        else:
            values = source[0, pl.ds(start, count)]
        height = values.shape[0]
        coarse = values.astype(jnp.bfloat16)
        fine = (values - coarse.astype(jnp.float32)).astype(jnp.bfloat16)
        high, rest = windows(coarse, lead), windows(fine, lead)
        blurred = jnp.dot(
            jnp.concatenate([high, rest, high], axis=1), band[...],
            preferred_element_type=jnp.float32,
        )
        for tile in range(tiles + lead):
            piece = blurred[tile * height : (tile + 1) * height]
            if lead and tile in (0, tiles):
                lane = lax.broadcasted_iota(jnp.int32, (height, LANES), 1)
                piece = jnp.where(lane >= SHIFT if tile == 0 else lane < SHIFT, piece, 0.0)
            for m in range(height // count):
                along[lead + m, tile, pl.ds(place, count)] = piece[m * count : (m + 1) * count]

    def blur_block(block, late):
        start = pl.multiple_of(block * BLOCK, 8)
        place = pl.multiple_of(start + HALO, 8)
        blur_along(raw, start, BLOCK, place, 1)

        @pl.when(jnp.logical_not(late))
        def _():
            blur_along(raw, start, BLOCK, place, 0)

    def across(m, tile, start, target, place, count):
        factors = [weight[i] for i in range(taps)]
        for group in range(count // 8):
            base = start + 8 * group
            value = factors[0] * along[m, tile, pl.ds(base, 8)]
            for i in range(1, taps):
                value += factors[i] * along[m, tile, pl.ds(base + i, 8)]
            target[pl.ds(pl.multiple_of(place + 8 * group, 8), 8)] = value

    def blur_across(blur, late):
        start = blur * BLOCK + HALO - 8 - half
        place = (blur + 1) * BLOCK

        def one_map(m, carry):
            for tile in range(tiles + 1):
                across(m, tile, start, blurred.at[core * frames + m, tile], place, BLOCK)
            return carry

        lax.fori_loop(jnp.asarray(late, jnp.int32), frames, one_map, 0)

    def blur_first(to_right, slot):
        start = first_row(to_right)
        count = BLOCK * (per - 2)
        blur_along(raw, start, count, start + HALO, 0)
        region = ABOVE if to_right else BLOCK * per * (chips - 1) - ABOVE

        def one_tile(tile, carry):
            across(0, tile, region + HALO - half, fresh_ref.at[slot, core, tile], 0, BLOCK * per)
            return carry

        lax.fori_loop(0, tiles, one_tile, 0)
        fresh_copy(slot).start()

    def first_arrives(to_right, slot):
        first_copy(to_right).wait_recv()

        @pl.when(has_right if to_right else has_left)
        def _():
            first_copy(to_right).start()

        blur_first(to_right, slot)

    def stack(first, count, unroll):
        def one_trial(trial, carry):
            stack_rows(shifts_ref, blurred, done_ref, trial, first, count, 0, False, unroll)
            return carry

        lax.fori_loop(0, trials, one_trial, 0)

    closing = last_row(chips, per, jnp.logical_not(low))
    other = last_row(chips, per, low)

    def stack_part(first, count, unroll):
        def one_trial(trial, carry):
            stack_rows(shifts_ref, blurred, part_ref, trial, first, count, closing, True, unroll)
            return carry

        lax.fori_loop(0, trials, one_trial, 0)


    def own_block(block, carry):
        blur_block(block, False)
        return carry

    def own_blur(blur, carry):
        blur_across(blur, False)
        pair_copy(blur, False).start()
        return carry

    def own_wait(blur, carry):
        from_partner(blur, False)
        return carry

    lax.fori_loop(chip * per, chip * per + per, own_block, 0)
    lax.fori_loop(chip * per + 1, chip * per + per, own_blur, 0)
    lax.fori_loop(chip * per + 1, chip * per + per, own_wait, 0)
    stack(pl.multiple_of((chip * per + 2) * BLOCK - 8, 8), BLOCK * (per - 3), 2)

    def stream(side, index):
        distance = index // per
        j = index % per
        origin = jnp.where(side == 1, chip + 1 + distance, chip - 1 - distance)
        present = (index >= 0) & (origin >= 0) & (origin < chips)
        edge = jnp.where(side == 1, origin == chips - 1, origin == 0)
        upward = (side == 1) != edge
        block = origin * per + jnp.where(upward, j, per - 1 - j)
        last = edge & (j == per - 1)
        return present, edge, upward, j, block, last

    def blurs(side, index, act):
        present, edge, upward, j, block, last = stream(side, index)
        count = jnp.where(present & jnp.logical_not(edge & (j == 0)), 1 + last.astype(jnp.int32), 0)
        begin = jnp.where(upward, block, block + 1)
        turn = jnp.where(upward, 1, -1)

        def one(k, carry):
            act(begin + turn * k)
            return carry

        lax.fori_loop(0, count, one, 0)

    def arrive(index):
        for side in (1, 0):
            present, edge, _, j, block, _ = stream(side, index)
            late = edge & (j > 1)

            @pl.when(present & late)
            def _(side=side, block=block):
                line_copy(block, True, True).wait_recv()

            @pl.when(present & jnp.logical_not(late))
            def _(side=side, block=block):
                line_copy(block, True, False).wait_recv()

            @pl.when(present & (has_left if side else has_right))
            def _(side=side, block=block):
                send_block(block, side == 0)

            @pl.when(present & edge & (j == 1) & (has_next if side else has_prev))
            def _(side=side):
                halo_copy(side == 1).start()

    def blur_side(index):
        def one_side(side, carry):
            present, edge, _, j, block, _ = stream(side, index)
            late = edge & (j > 1)

            @pl.when(present)
            def _():
                blur_block(block, late)

            def spread(blur):
                blur_across(blur, late)
                to_partner(blur, late)

            blurs(side, index, spread)
            return carry

        lax.fori_loop(0, 2, one_side, 0)

    def stack_side(index):
        def one_side(side, carry):
            present, edge, upward, j, block, last = stream(side, index)
            late = edge & (j > 1)
            blurs(side, index, lambda blur: from_partner(blur, late))
            begin = pl.multiple_of(jnp.where(upward, block - 1, block + 2) * BLOCK - 8, 8)
            closes = (side == 1) == low

            @pl.when(present & jnp.logical_not(edge))
            def _():
                stack(begin, BLOCK, True)

            @pl.when(present & edge & closes & jnp.logical_not(last) & (j > 2))
            def _():
                stack_part(begin, BLOCK, True)

            @pl.when(present & closes & last)
            def _():
                stack_part(pl.multiple_of((block - 1) * BLOCK - 8, 8), JOIN, True)

            return carry

        lax.fori_loop(0, 2, one_side, 0)

    limit = steps - 2
    mirror = chips - 1 - chip
    top_step = jnp.minimum(jnp.maximum(per * (mirror - 1) + 4, per * (chip - 1) + 2), limit)
    bottom_step = jnp.minimum(jnp.maximum(per * (chip - 1) + 4, per * (mirror - 1) + 2), limit)

    others = jnp.where(low, chip, mirror)
    other_step = jnp.where(others > 0, per * others + 2, -2)

    def step(index, carry):
        @pl.when(index < steps)
        def _():
            arrive(index)
            blur_side(index)

        @pl.when(index == top_step)
        def _():
            @pl.when(has_prev)
            def _():
                halo_copy(True).wait_recv()
                blur_along(top, 0, HALO, 0, 0)
                blur_along(top, 0, HALO, 0, 1)

            @pl.when(jnp.logical_not(has_prev))
            def _():
                for m in range(frames):
                    for tile in range(tiles + 1):
                        along[m, tile, pl.ds(0, HALO)] = jnp.zeros((HALO, LANES), jnp.float32)

            blur_across(-1, False)
            blur_across(0, False)

            @pl.when(jnp.logical_not(has_prev))
            def _():
                for m in range(frames):
                    for tile in range(tiles + 1):
                        blurred[core * frames + m, tile, pl.ds(0, ABOVE)] = jnp.zeros(
                            (ABOVE, LANES), jnp.float32
                        )

            pair_copy(-1, False).start()
            pair_copy(0, False).start()

        @pl.when(index == bottom_step)
        def _():
            @pl.when(has_next)
            def _():
                halo_copy(False).wait_recv()
                blur_along(bottom, 0, HALO, rows + HALO, 0)
                blur_along(bottom, 0, HALO, rows + HALO, 1)

            @pl.when(jnp.logical_not(has_next))
            def _():
                for m in range(frames):
                    for tile in range(tiles + 1):
                        along[m, tile, pl.ds(rows + HALO, HALO)] = jnp.zeros(
                            (HALO, LANES), jnp.float32
                        )

            blur_across(blocks, False)
            blur_across(blocks + 1, False)

            @pl.when(jnp.logical_not(has_next))
            def _():
                for m in range(frames):
                    for tile in range(tiles + 1):
                        blurred[core * frames + m, tile, pl.ds(rows + ABOVE, ABOVE)] = jnp.zeros(
                            (ABOVE, LANES), jnp.float32
                        )

            pair_copy(blocks, False).start()
            pair_copy(blocks + 1, False).start()

        @pl.when(index == other_step)
        def _():
            @pl.when(low)
            def _():
                first_arrives(True, 1)

            @pl.when(jnp.logical_not(low))
            def _():
                first_arrives(False, 1)

        stack_side(index - 1)

        @pl.when(index - 1 == other_step)
        def _():
            fresh_copy(1).wait_recv()
            behind = jnp.where(low, 0, BLOCK)
            count = BLOCK * (per - 1)
            place = pl.ds(pl.multiple_of(other + behind + ABOVE, 8), count)
            for kind in range(2):
                for tile in range(tiles):
                    there = pl.ds(pl.multiple_of(behind, 8), count)
                    blurred[kind * frames, tile, place] = fresh_ref[1, kind, tile, there]
            stack(other, BLOCK * per, 4)

        @pl.when(index - 1 == top_step)
        def _():
            from_partner(-1, False)
            from_partner(0, False)
            stack(0, ABOVE, True)

        @pl.when(index - 1 == bottom_step)
        def _():
            from_partner(blocks, False)
            from_partner(blocks + 1, False)
            stack(rows - ABOVE, ABOVE, True)

        return carry

    lax.fori_loop(0, steps + 1, step, 0)

    @pl.when(low)
    def _():
        first_arrives(False, 0)

    @pl.when(jnp.logical_not(low))
    def _():
        first_arrives(True, 0)

    for sides in (1, 2):
        late = (per - 1) * sides
        whole = blurred.at[pl.ds(0, frames), :, pl.ds(0, (blocks + 3 - late) * BLOCK)]
        most = blurred.at[pl.ds(0, frames - 1), :, pl.ds(0, late * BLOCK)]

        @pl.when(has_left.astype(jnp.int32) + has_right.astype(jnp.int32) == sides)
        def _(whole=whole, most=most):
            pltpu.make_async_copy(whole, whole, pair_sends.at[0]).wait()
            pltpu.make_async_copy(most, most, pair_sends.at[1]).wait()

    trade_copy(psi_ref).wait_send()

    def drain(origin, carry):
        part = raw.at[:, pl.ds(pl.multiple_of(origin * (2 * share), 8), 2 * share)]

        @pl.when(has_right & (origin <= chip))
        def _():
            pltpu.make_async_copy(part, part, right_sem.at[origin]).wait()

        @pl.when(has_left & (origin >= chip))
        def _():
            pltpu.make_async_copy(part, part, left_sem.at[origin]).wait()

        return carry

    lax.fori_loop(0, chips, drain, 0)

    @pl.when(other_step > 0)
    def _():
        fresh_copy(1).wait_send()

    @pl.when(has_next)
    def _():
        halo_copy(True).wait_send()

    @pl.when(has_prev)
    def _():
        halo_copy(False).wait_send()

    fresh_copy(0).wait()


def per_device(vels, skies, psi_maps, phi_maps, psf_taps, shifts):
    frames, share, width = psi_maps.shape
    maps = 2 * frames
    tiles = width // LANES
    rows = share * vels
    trials = shifts.shape[0]
    blocks = rows // BLOCK
    taps = psf_taps.shape[0]
    shifts = pltpu.with_memory_space_constraint(jnp.transpose(shifts, (1, 2, 0)), pltpu.HBM)
    psf_taps = pltpu.with_memory_space_constraint(psf_taps, pltpu.HBM)
    psi_maps = pltpu.with_memory_space_constraint(psi_maps, pltpu.HBM)
    phi_maps = pltpu.with_memory_space_constraint(phi_maps, pltpu.HBM)
    dma = pltpu.SemaphoreType.DMA
    part, fresh, done = pl.pallas_call(
        functools.partial(gather_kernel, vels, skies),
        out_shape=(
            jax.ShapeDtypeStruct((2, trials, 2 * share, width), jnp.float32),
            jax.ShapeDtypeStruct((2, 2, tiles, 2 * share, LANES), jnp.float32),
            jax.ShapeDtypeStruct((trials, rows, width), jnp.float32),
        ),
        in_specs=[
            pl.BlockSpec(memory_space=pl.ANY),
            pl.BlockSpec(memory_space=pl.ANY),
            pl.BlockSpec(memory_space=pl.ANY),
            pl.BlockSpec(memory_space=pl.ANY),
        ],
        out_specs=(pl.BlockSpec(memory_space=pltpu.VMEM),) * 3,
        scratch_shapes=[
            pltpu.SMEM((taps,), jnp.float32),
            pltpu.SMEM(shifts.shape, jnp.int32),
            pltpu.VMEM((maps, tiles + 1, rows + 2 * ABOVE, LANES), jnp.float32),
            pltpu.VMEM((frames, rows, width), jnp.float32),
            pltpu.VMEM((frames, tiles + 1, rows + 2 * HALO, LANES), jnp.float32),
            pltpu.VMEM((blocks + 3, frames, tiles + 1, BLOCK, LANES), jnp.float32),
            pltpu.VMEM((frames, HALO, width), jnp.float32),
            pltpu.VMEM((frames, HALO, width), jnp.float32),
            pltpu.VMEM((9 * LANES, LANES), jnp.bfloat16),
            pltpu.VMEM((6 * LANES, LANES), jnp.bfloat16),
            pltpu.VMEM((taps, 8, LANES), jnp.float32),
            pltpu.SemaphoreType.REGULAR((4,)),
            dma((2,)),
            dma,
            dma((2,)),
            dma((blocks,)),
            dma((vels // 2,)),
            dma((vels // 2,)),
            dma((2,)),
            dma((blocks + 3,)),
            dma((2,)),
            dma((2,)),
            dma((2,)),
            dma((2,)),
            dma((2,)),
        ],
        compiler_params=pltpu.CompilerParams(
            collective_id=0, has_side_effects=True, vmem_limit_bytes=36 * 2**20
        ),
        name="gather",
    )(psf_taps, shifts, psi_maps, phi_maps)
    return pl.pallas_call(
        functools.partial(finish_kernel, vels),
        out_shape=jax.ShapeDtypeStruct((trials, rows, width), jnp.float32),
        in_specs=[pl.BlockSpec(memory_space=pltpu.VMEM)] * 3,
        out_specs=pl.BlockSpec(memory_space=pl.ANY),
        scratch_shapes=[
            pltpu.VMEM((trials, 2 * share, width), jnp.float32),
            dma((3, trials)),
        ],
        compiler_params=pltpu.CompilerParams(vmem_limit_bytes=4 * 2**20),
        name="finish",
    )(part, fresh, done)


def solution(mesh):
    return jax.shard_map(
        functools.partial(per_device, mesh.shape["vel"], mesh.shape["sky"]),
        mesh=mesh,
        in_specs=(
            P(None, ("sky", "vel"), None),
            P(None, ("sky", "vel"), None),
            P(),
            P("vel", None, None),
        ),
        out_specs=P("vel", "sky", None),
        check_vma=False,
    )
```

```python
import functools
import jax
import jax.numpy as jnp
from jax import lax
from jax.experimental import pallas as pl
from jax.experimental.pallas import tpu as pltpu
from jax.sharding import PartitionSpec as P

SHIFT = 16
BLOCK = 16
HALO = 2 * BLOCK
ABOVE = BLOCK + 8
JOIN = 4 * BLOCK
LANES = 128
MESH = pl.DeviceIdType.MESH


def stack_rows(shifts_ref, maps_ref, out_ref, trial, first, count, skip, partial, unroll):
    frames = shifts_ref.shape[0]
    tiles = maps_ref.shape[1]
    lane = lax.broadcasted_iota(jnp.int32, (8, LANES), 1)
    down, turn, inside = [], [], []
    for frame in range(1, frames):
        offset = shifts_ref[frame, 1, trial] + SHIFT
        down.append(shifts_ref[frame, 0, trial] + ABOVE)
        turn.append(lax.rem(LANES - offset, LANES))
        inside.append(lane >= offset)

    def one_group(group, carry):
        base = first + group * 8

        def stacked(kind):
            total = [None] * (tiles - 1)
            if not partial:
                total = [
                    maps_ref[kind * frames, tile, pl.ds(pl.multiple_of(base + ABOVE, 8), 8)]
                    for tile in range(tiles - 1)
                ]
            for step in range(frames - 1):
                m = kind * frames + step + 1
                pieces = [maps_ref[m, tile, pl.ds(base + down[step], 8)] for tile in range(tiles)]
                for tile in range(tiles - 1):
                    joined = jnp.where(inside[step], pieces[tile], pieces[tile + 1])
                    moved = pltpu.roll(joined, turn[step], 1)
                    total[tile] = moved if total[tile] is None else total[tile] + moved
            return total

        psi = stacked(0)
        phi = stacked(1)
        rows = pl.ds(pl.multiple_of(base - skip, 8), 8)
        for tile in range(tiles - 1):
            columns = slice(tile * LANES, (tile + 1) * LANES)
            if partial:
                out_ref[0, trial, rows, columns] = psi[tile]
                out_ref[1, trial, rows, columns] = phi[tile]
            else:
                out_ref[trial, rows, columns] = psi[tile] * lax.rsqrt(phi[tile])
        return carry

    lax.fori_loop(0, count // 8, one_group, 0, unroll=unroll)


def last_row(chips, per, to_right):
    return pl.multiple_of(jnp.where(to_right, ABOVE, BLOCK * per * (chips - 1) - ABOVE), 8)


def finish_kernel(vels, part_ref, fresh_ref, done_ref, out_ref, closing, sems):
    trials, rows, width = done_ref.shape
    count = part_ref.shape[2]
    chips = vels // 2
    low = lax.axis_index("vel") // 2 < chips // 2
    first = last_row(chips, count // BLOCK, jnp.logical_not(low))
    small = ABOVE
    large = rows - count - small
    large_row = pl.multiple_of(jnp.where(low, 0, small + count), 8)
    small_row = pl.multiple_of(jnp.where(low, large + count, 0), 8)

    def large_copy(trial):
        part = pl.ds(large_row, large)
        return pltpu.make_async_copy(done_ref.at[trial, part], out_ref.at[trial, part], sems.at[0, trial])

    def small_copy(trial):
        part = pl.ds(small_row, small)
        return pltpu.make_async_copy(done_ref.at[trial, part], out_ref.at[trial, part], sems.at[1, trial])

    def closing_copy(trial):
        part = pl.ds(first, count)
        return pltpu.make_async_copy(closing.at[trial], out_ref.at[trial, part], sems.at[2, trial])

    def begin(trial, carry):
        large_copy(trial).start()
        small_copy(trial).start()
        return carry

    lax.fori_loop(0, trials, begin, 0)

    def compute(trial, carry):
        for tile in range(width // LANES):
            columns = slice(tile * LANES, (tile + 1) * LANES)
            psi = part_ref[0, trial, :, columns] + fresh_ref[0, 0, tile]
            phi = part_ref[1, trial, :, columns] + fresh_ref[0, 1, tile]
            closing[trial, :, columns] = psi * lax.rsqrt(phi)
        closing_copy(trial).start()
        return carry

    lax.fori_loop(0, trials, compute, 0)

    def finish(trial, carry):
        large_copy(trial).wait()
        small_copy(trial).wait()
        closing_copy(trial).wait()
        return carry

    lax.fori_loop(0, trials, finish, 0)


def gather_kernel(
    vels, skies, taps_hbm, shifts_hbm, psi_ref, phi_ref, part_ref, fresh_ref, done_ref,
    taps_ref, shifts_ref, blurred, raw, along, landing, top, bottom, band0, band1, weight,
    answers, small_sems, own_sem, trade_sems, recv_sem, right_sem, left_sem, pair_sends, pair_recv, top_sems, bottom_sems,
    first_sems, fresh_send, fresh_recv,
):
    frames, share, width = psi_ref.shape
    trials = shifts_ref.shape[2]
    taps = taps_ref.shape[0]
    half = taps // 2
    chips = vels // 2
    tiles = width // LANES
    rows = vels * share
    blocks = rows // BLOCK
    per = blocks // chips
    steps = per * (chips - 1)
    sky = lax.axis_index("sky")
    vel = lax.axis_index("vel")
    chip = vel // 2
    core = vel % 2
    has_right = chip < chips - 1
    has_left = chip > 0
    has_next = sky < skies - 1
    has_prev = sky > 0
    low = chip < chips // 2
    partner = (sky, vel + 1 - 2 * core)

    taps_copy = pltpu.make_async_copy(taps_hbm, taps_ref, small_sems.at[0])
    shifts_copy = pltpu.make_async_copy(shifts_hbm, shifts_ref, small_sems.at[1])
    own_rows = pl.ds(pl.multiple_of(vel * share, 8), share)

    def own_copy(source):
        return pltpu.make_async_copy(source, raw.at[:, own_rows], own_sem)

    @pl.when(core == 0)
    def _():
        own_copy(psi_ref).start()

    @pl.when(core == 1)
    def _():
        own_copy(phi_ref).start()

    taps_copy.start()
    shifts_copy.start()
    left, right = (sky, vel - 2), (sky, vel + 2)
    before, after = (sky - 1, vel), (sky + 1, vel)
    skies_near = ((has_prev & (core == 1), before), (has_next & (core == 1), after))
    barrier = pltpu.get_barrier_semaphore()

    def greet(semaphore, device, present):
        @pl.when(present)
        def _():
            pl.semaphore_signal(semaphore, inc=1, device_id=device, device_id_type=MESH)

    greet(barrier, right, has_right)
    greet(barrier, partner, (core == 0) | (chip == 0))
    for present, device in skies_near:
        greet(barrier, device, present)
    callers = (has_left | (core == 0)).astype(jnp.int32) + core
    for present, device in skies_near:
        callers = callers + present.astype(jnp.int32)
    pl.semaphore_wait(barrier, callers)
    greet(answers.at[0], left, has_left)
    greet(answers.at[1], partner, core == 1)
    for present, device in skies_near:
        greet(answers.at[2], device, present)

    def trade_copy(source):
        return pltpu.make_async_remote_copy(
            src_ref=source,
            dst_ref=raw.at[:, own_rows],
            send_sem=trade_sems.at[0],
            recv_sem=trade_sems.at[1],
            device_id=partner,
            device_id_type=MESH,
        )

    def block_rows(block):
        return pl.ds(pl.multiple_of(block * BLOCK, 8), BLOCK)

    def line_copy(block, to_right, late, source=None):
        maps = pl.ds(1, frames - 1) if late else pl.ds(0, frames)
        place = raw.at[maps, block_rows(block)]
        return pltpu.make_async_remote_copy(
            src_ref=place if source is None else source[0].at[maps, block_rows(source[1])],
            dst_ref=place,
            send_sem=(right_sem if to_right else left_sem).at[block // per],
            recv_sem=recv_sem.at[block],
            device_id=(sky, vel + 2) if to_right else (sky, vel - 2),
            device_id_type=MESH,
        )

    def send_block(block, to_right, source=None):
        if to_right:
            late = (block < per) & (block > 1)
        else:
            late = (block >= blocks - per) & (block < blocks - 2)

        @pl.when(late)
        def _():
            line_copy(block, to_right, True, source).start()

        @pl.when(jnp.logical_not(late))
        def _():
            line_copy(block, to_right, False, source).start()

    def first_row(to_right):
        return HALO if to_right else BLOCK * per * (chips - 1)

    def first_copy(to_right):
        place = raw.at[0, pl.ds(first_row(to_right), BLOCK * (per - 2))]
        return pltpu.make_async_remote_copy(
            src_ref=place,
            dst_ref=place,
            send_sem=right_sem.at[0] if to_right else left_sem.at[chips - 1],
            recv_sem=first_sems.at[1 if to_right else 0],
            device_id=(sky, vel + 2) if to_right else (sky, vel - 2),
            device_id_type=MESH,
        )

    def fresh_copy(slot):
        place = fresh_ref.at[slot, core]
        return pltpu.make_async_remote_copy(
            src_ref=place,
            dst_ref=place,
            send_sem=fresh_send.at[slot],
            recv_sem=fresh_recv.at[slot],
            device_id=partner,
            device_id_type=MESH,
        )

    def halo_copy(to_next):
        source = raw.at[:, pl.ds(rows - HALO if to_next else 0, HALO)]
        sems = top_sems if to_next else bottom_sems
        return pltpu.make_async_remote_copy(
            src_ref=source,
            dst_ref=top if to_next else bottom,
            send_sem=sems.at[0],
            recv_sem=sems.at[1],
            device_id=(sky + 1, vel) if to_next else (sky - 1, vel),
            device_id_type=MESH,
        )

    def pair_copy(blur, late):
        skip = 1 if late else 0
        place = pl.ds(pl.multiple_of((blur + 1) * BLOCK, 8), BLOCK)
        return pltpu.make_async_remote_copy(
            src_ref=blurred.at[pl.ds(core * frames + skip, frames - skip), :, place],
            dst_ref=landing.at[blur + 1, pl.ds(skip, frames - skip)],
            send_sem=pair_sends.at[skip],
            recv_sem=pair_recv.at[blur + 1],
            device_id=partner,
            device_id_type=MESH,
        )

    def to_partner(blur, late):
        @pl.when(late)
        def _():
            pair_copy(blur, True).start()

        @pl.when(jnp.logical_not(late))
        def _():
            pair_copy(blur, False).start()

    def from_partner(blur, late):
        place = pl.ds(pl.multiple_of((blur + 1) * BLOCK, 8), BLOCK)

        @pl.when(late)
        def _():
            pair_copy(blur, True).wait_recv()

        @pl.when(jnp.logical_not(late))
        def _():
            pair_copy(blur, False).wait_recv()
            for tile in range(tiles):
                blurred[(1 - core) * frames, tile, place] = landing[blur + 1, 0, tile]

        for m in range(1, frames):
            for tile in range(tiles + 1):
                blurred[(1 - core) * frames + m, tile, place] = landing[blur + 1, m, tile]

    right_up = chip == 0
    left_up = chip < chips - 1

    def send_half(to_right, upward, part, source=None):
        def one(index, carry):
            place = jnp.where(upward, index, per // 2 - 1 - index)
            there = None if source is None else (source, place)
            send_block(chip * per + part * (per // 2) + place, to_right, there)
            return carry

        lax.fori_loop(0, per // 2, one, 0)

    def send_first(to_right, upward, ready):
        for kind, source in ((0, psi_ref), (1, phi_ref)):

            @pl.when(ready & (core == kind))
            def _(source=source):
                send_half(to_right, upward, core, source)

    right_ready = (chip > 0) | (core == 0)
    left_ready = (chip < chips - 1) | (core == 1)
    send_first(False, left_up, has_left & left_ready)

    @pl.when(core == 0)
    def _():
        pl.semaphore_wait(answers.at[1], 1)
        trade_copy(phi_ref).start()

    @pl.when(core == 1)
    def _():
        trade_copy(psi_ref).start()

    @pl.when(has_right)
    def _():
        pl.semaphore_wait(answers.at[0], 1)

    send_first(True, right_up, has_right & right_ready)
    own_copy(psi_ref).wait()
    taps_copy.wait()
    shifts_copy.wait()
    total = taps_ref[0]
    for i in range(1, taps):
        total = total + taps_ref[i]
    scale = 1.0 / jnp.full((8, LANES), total, jnp.float32)
    squared = jnp.full((8, LANES), core, jnp.int32) > 0
    for i in range(taps):
        value = jnp.full((8, LANES), taps_ref[i], jnp.float32) * scale
        weight[i] = jnp.where(squared, value * value, value)
    for lead, band in ((0, band0), (1, band1)):
        depth = (3 - lead) * LANES
        place = lax.broadcasted_iota(jnp.int32, (depth, LANES), 0)
        place = place - lax.broadcasted_iota(jnp.int32, (depth, LANES), 1)
        spot = place - (LANES - SHIFT * lead - half)
        matrix = jnp.zeros((depth, LANES), jnp.float32)
        for i in range(taps):
            value = jnp.broadcast_to(weight[i][:1], (depth, LANES))
            matrix = jnp.where(spot == i, value, matrix)
        coarse = matrix.astype(jnp.bfloat16)
        band[:depth] = coarse
        band[depth : 2 * depth] = coarse
        band[2 * depth :] = (matrix - coarse.astype(jnp.float32)).astype(jnp.bfloat16)

    trade_copy(psi_ref).wait_recv()

    def send_rest(to_right, upward, present, ready):
        @pl.when(present)
        def _():
            send_half(to_right, upward, 1 - core)

        @pl.when(present & jnp.logical_not(ready))
        def _():
            send_half(to_right, upward, core)

    send_rest(False, left_up, has_left, left_ready)
    send_rest(True, right_up, has_right, right_ready)

    @pl.when(chip == chips - 1)
    def _():
        first_copy(False).start()

    @pl.when(chip == 0)
    def _():
        first_copy(True).start()

    @pl.when(core == 1)
    def _():
        pl.semaphore_wait(answers.at[2], has_prev.astype(jnp.int32) + has_next.astype(jnp.int32))
        pl.semaphore_signal(answers.at[3], inc=1, device_id=partner, device_id_type=MESH)

    @pl.when(core == 0)
    def _():
        pl.semaphore_wait(answers.at[3], 1)

    @pl.when(has_next & (chip == chips - 1))
    def _():
        halo_copy(True).start()

    @pl.when(has_prev & (chip == 0))
    def _():
        halo_copy(False).start()

    def blur_along(source, start, count, place, lead):
        def windows(values, lead):
            blank = jnp.zeros((values.shape[0], LANES), values.dtype)
            columns = [blank] + [values[:, t * LANES : (t + 1) * LANES] for t in range(tiles)] + [blank]
            wide = 3 - lead
            return jnp.concatenate(
                [jnp.concatenate(columns[t : t + wide], axis=1) for t in range(tiles + lead)], axis=0
            )

        band = band1 if lead else band0
        if lead:
            values = source[1:frames, pl.ds(start, count)].reshape((frames - 1) * count, width)
        else:
            values = source[0, pl.ds(start, count)]
        height = values.shape[0]
        coarse = values.astype(jnp.bfloat16)
        fine = (values - coarse.astype(jnp.float32)).astype(jnp.bfloat16)
        high, rest = windows(coarse, lead), windows(fine, lead)
        blurred = jnp.dot(
            jnp.concatenate([high, rest, high], axis=1), band[...],
            preferred_element_type=jnp.float32,
        )
        for tile in range(tiles + lead):
            piece = blurred[tile * height : (tile + 1) * height]
            if lead and tile in (0, tiles):
                lane = lax.broadcasted_iota(jnp.int32, (height, LANES), 1)
                piece = jnp.where(lane >= SHIFT if tile == 0 else lane < SHIFT, piece, 0.0)
            for m in range(height // count):
                along[lead + m, tile, pl.ds(place, count)] = piece[m * count : (m + 1) * count]

    def blur_block(block, late):
        start = pl.multiple_of(block * BLOCK, 8)
        place = pl.multiple_of(start + HALO, 8)
        blur_along(raw, start, BLOCK, place, 1)

        @pl.when(jnp.logical_not(late))
        def _():
            blur_along(raw, start, BLOCK, place, 0)

    def across(m, tile, start, target, place, count):
        factors = [weight[i] for i in range(taps)]
        for group in range(count // 8):
            base = start + 8 * group
            value = factors[0] * along[m, tile, pl.ds(base, 8)]
            for i in range(1, taps):
                value += factors[i] * along[m, tile, pl.ds(base + i, 8)]
            target[pl.ds(pl.multiple_of(place + 8 * group, 8), 8)] = value

    def blur_across(blur, late):
        start = blur * BLOCK + HALO - 8 - half
        place = (blur + 1) * BLOCK

        def one_map(m, carry):
            for tile in range(tiles + 1):
                across(m, tile, start, blurred.at[core * frames + m, tile], place, BLOCK)
            return carry

        lax.fori_loop(jnp.asarray(late, jnp.int32), frames, one_map, 0)

    def blur_first(to_right, slot):
        start = first_row(to_right)
        count = BLOCK * (per - 2)
        blur_along(raw, start, count, start + HALO, 0)
        region = ABOVE if to_right else BLOCK * per * (chips - 1) - ABOVE

        def one_tile(tile, carry):
            across(0, tile, region + HALO - half, fresh_ref.at[slot, core, tile], 0, BLOCK * per)
            return carry

        lax.fori_loop(0, tiles, one_tile, 0)
        fresh_copy(slot).start()

    def first_arrives(to_right, slot):
        first_copy(to_right).wait_recv()

        @pl.when(has_right if to_right else has_left)
        def _():
            first_copy(to_right).start()

        blur_first(to_right, slot)

    def together(count):
        return max(JOIN // count, 1) if trials % 4 == 0 else 1

    def stack(first, count, unroll):
        def one_trial(trial, carry):
            stack_rows(shifts_ref, blurred, done_ref, trial, first, count, 0, False, unroll)
            return carry

        lax.fori_loop(0, trials, one_trial, 0, unroll=together(count))

    closing = last_row(chips, per, jnp.logical_not(low))
    other = last_row(chips, per, low)

    def stack_part(first, count, unroll):
        def one_trial(trial, carry):
            stack_rows(shifts_ref, blurred, part_ref, trial, first, count, closing, True, unroll)
            return carry

        lax.fori_loop(0, trials, one_trial, 0, unroll=together(count))


    def own_block(block, carry):
        blur_block(block, False)
        return carry

    def own_blur(blur, carry):
        blur_across(blur, False)
        pair_copy(blur, False).start()
        return carry

    def own_wait(blur, carry):
        from_partner(blur, False)
        return carry

    lax.fori_loop(chip * per, chip * per + per, own_block, 0)
    lax.fori_loop(chip * per + 1, chip * per + per, own_blur, 0)
    lax.fori_loop(chip * per + 1, chip * per + per, own_wait, 0)
    stack(pl.multiple_of((chip * per + 2) * BLOCK - 8, 8), BLOCK * (per - 3), 2)

    def stream(side, index):
        distance = index // per
        j = index % per
        origin = jnp.where(side == 1, chip + 1 + distance, chip - 1 - distance)
        present = (index >= 0) & (origin >= 0) & (origin < chips)
        edge = jnp.where(side == 1, origin == chips - 1, origin == 0)
        upward = (side == 1) != edge
        block = origin * per + jnp.where(upward, j, per - 1 - j)
        last = edge & (j == per - 1)
        return present, edge, upward, j, block, last

    def blurs(side, index, act):
        present, edge, upward, j, block, last = stream(side, index)
        count = jnp.where(present & jnp.logical_not(edge & (j == 0)), 1 + last.astype(jnp.int32), 0)
        begin = jnp.where(upward, block, block + 1)
        turn = jnp.where(upward, 1, -1)

        def one(k, carry):
            act(begin + turn * k)
            return carry

        lax.fori_loop(0, count, one, 0)

    def arrive(index):
        for side in (1, 0):
            present, edge, _, j, block, _ = stream(side, index)
            late = edge & (j > 1)

            @pl.when(present & late)
            def _(side=side, block=block):
                line_copy(block, True, True).wait_recv()

            @pl.when(present & jnp.logical_not(late))
            def _(side=side, block=block):
                line_copy(block, True, False).wait_recv()

            @pl.when(present & (has_left if side else has_right))
            def _(side=side, block=block):
                send_block(block, side == 0)

            @pl.when(present & edge & (j == 1) & (has_next if side else has_prev))
            def _(side=side):
                halo_copy(side == 1).start()

    def blur_side(index):
        def one_side(side, carry):
            present, edge, _, j, block, _ = stream(side, index)
            late = edge & (j > 1)

            @pl.when(present)
            def _():
                blur_block(block, late)

            def spread(blur):
                blur_across(blur, late)
                to_partner(blur, late)

            blurs(side, index, spread)
            return carry

        lax.fori_loop(0, 2, one_side, 0)

    def stack_side(index):
        def one_side(side, carry):
            present, edge, upward, j, block, last = stream(side, index)
            late = edge & (j > 1)
            blurs(side, index, lambda blur: from_partner(blur, late))
            begin = pl.multiple_of(jnp.where(upward, block - 1, block + 2) * BLOCK - 8, 8)
            closes = (side == 1) == low

            @pl.when(present & jnp.logical_not(edge))
            def _():
                stack(begin, BLOCK, True)

            @pl.when(present & edge & closes & jnp.logical_not(last) & (j > 2))
            def _():
                stack_part(begin, BLOCK, True)

            @pl.when(present & closes & last)
            def _():
                stack_part(pl.multiple_of((block - 1) * BLOCK - 8, 8), JOIN, True)

            return carry

        lax.fori_loop(0, 2, one_side, 0)

    limit = steps - 2
    mirror = chips - 1 - chip
    top_step = jnp.minimum(jnp.maximum(per * (mirror - 1) + 4, per * (chip - 1) + 2), limit)
    bottom_step = jnp.minimum(jnp.maximum(per * (chip - 1) + 4, per * (mirror - 1) + 2), limit)

    others = jnp.where(low, chip, mirror)
    other_step = jnp.where(others > 0, per * others + 2, -2)

    def step(index, carry):
        @pl.when(index < steps)
        def _():
            arrive(index)
            blur_side(index)

        @pl.when(index == top_step)
        def _():
            @pl.when(has_prev)
            def _():
                halo_copy(True).wait_recv()
                blur_along(top, 0, HALO, 0, 0)
                blur_along(top, 0, HALO, 0, 1)

            @pl.when(jnp.logical_not(has_prev))
            def _():
                for m in range(frames):
                    for tile in range(tiles + 1):
                        along[m, tile, pl.ds(0, HALO)] = jnp.zeros((HALO, LANES), jnp.float32)

            blur_across(-1, False)
            blur_across(0, False)

            @pl.when(jnp.logical_not(has_prev))
            def _():
                for m in range(frames):
                    for tile in range(tiles + 1):
                        blurred[core * frames + m, tile, pl.ds(0, ABOVE)] = jnp.zeros(
                            (ABOVE, LANES), jnp.float32
                        )

            pair_copy(-1, False).start()
            pair_copy(0, False).start()

        @pl.when(index == bottom_step)
        def _():
            @pl.when(has_next)
            def _():
                halo_copy(False).wait_recv()
                blur_along(bottom, 0, HALO, rows + HALO, 0)
                blur_along(bottom, 0, HALO, rows + HALO, 1)

            @pl.when(jnp.logical_not(has_next))
            def _():
                for m in range(frames):
                    for tile in range(tiles + 1):
                        along[m, tile, pl.ds(rows + HALO, HALO)] = jnp.zeros(
                            (HALO, LANES), jnp.float32
                        )

            blur_across(blocks, False)
            blur_across(blocks + 1, False)

            @pl.when(jnp.logical_not(has_next))
            def _():
                for m in range(frames):
                    for tile in range(tiles + 1):
                        blurred[core * frames + m, tile, pl.ds(rows + ABOVE, ABOVE)] = jnp.zeros(
                            (ABOVE, LANES), jnp.float32
                        )

            pair_copy(blocks, False).start()
            pair_copy(blocks + 1, False).start()

        @pl.when(index == other_step)
        def _():
            @pl.when(low)
            def _():
                first_arrives(True, 1)

            @pl.when(jnp.logical_not(low))
            def _():
                first_arrives(False, 1)

        stack_side(index - 1)

        @pl.when(index - 1 == other_step)
        def _():
            fresh_copy(1).wait_recv()
            behind = jnp.where(low, 0, BLOCK)
            count = BLOCK * (per - 1)
            place = pl.ds(pl.multiple_of(other + behind + ABOVE, 8), count)
            for kind in range(2):
                for tile in range(tiles):
                    there = pl.ds(pl.multiple_of(behind, 8), count)
                    blurred[kind * frames, tile, place] = fresh_ref[1, kind, tile, there]
            stack(other, BLOCK * per, 4)

        @pl.when(index - 1 == top_step)
        def _():
            from_partner(-1, False)
            from_partner(0, False)
            stack(0, ABOVE, True)

        @pl.when(index - 1 == bottom_step)
        def _():
            from_partner(blocks, False)
            from_partner(blocks + 1, False)
            stack(rows - ABOVE, ABOVE, True)

        return carry

    lax.fori_loop(0, steps + 1, step, 0)

    @pl.when(low)
    def _():
        first_arrives(False, 0)

    @pl.when(jnp.logical_not(low))
    def _():
        first_arrives(True, 0)

    for sides in (1, 2):
        late = (per - 1) * sides
        whole = blurred.at[pl.ds(0, frames), :, pl.ds(0, (blocks + 3 - late) * BLOCK)]
        most = blurred.at[pl.ds(0, frames - 1), :, pl.ds(0, late * BLOCK)]

        @pl.when(has_left.astype(jnp.int32) + has_right.astype(jnp.int32) == sides)
        def _(whole=whole, most=most):
            pltpu.make_async_copy(whole, whole, pair_sends.at[0]).wait()
            pltpu.make_async_copy(most, most, pair_sends.at[1]).wait()

    trade_copy(psi_ref).wait_send()

    def drain(origin, carry):
        part = raw.at[:, pl.ds(pl.multiple_of(origin * (2 * share), 8), 2 * share)]

        @pl.when(has_right & (origin <= chip))
        def _():
            pltpu.make_async_copy(part, part, right_sem.at[origin]).wait()

        @pl.when(has_left & (origin >= chip))
        def _():
            pltpu.make_async_copy(part, part, left_sem.at[origin]).wait()

        return carry

    lax.fori_loop(0, chips, drain, 0)

    @pl.when(other_step > 0)
    def _():
        fresh_copy(1).wait_send()

    @pl.when(has_next)
    def _():
        halo_copy(True).wait_send()

    @pl.when(has_prev)
    def _():
        halo_copy(False).wait_send()

    fresh_copy(0).wait()


def per_device(vels, skies, psi_maps, phi_maps, psf_taps, shifts):
    frames, share, width = psi_maps.shape
    maps = 2 * frames
    tiles = width // LANES
    rows = share * vels
    trials = shifts.shape[0]
    blocks = rows // BLOCK
    taps = psf_taps.shape[0]
    shifts = pltpu.with_memory_space_constraint(jnp.transpose(shifts, (1, 2, 0)), pltpu.HBM)
    psf_taps = pltpu.with_memory_space_constraint(psf_taps, pltpu.HBM)
    psi_maps = pltpu.with_memory_space_constraint(psi_maps, pltpu.HBM)
    phi_maps = pltpu.with_memory_space_constraint(phi_maps, pltpu.HBM)
    dma = pltpu.SemaphoreType.DMA
    part, fresh, done = pl.pallas_call(
        functools.partial(gather_kernel, vels, skies),
        out_shape=(
            jax.ShapeDtypeStruct((2, trials, 2 * share, width), jnp.float32),
            jax.ShapeDtypeStruct((2, 2, tiles, 2 * share, LANES), jnp.float32),
            jax.ShapeDtypeStruct((trials, rows, width), jnp.float32),
        ),
        in_specs=[
            pl.BlockSpec(memory_space=pl.ANY),
            pl.BlockSpec(memory_space=pl.ANY),
            pl.BlockSpec(memory_space=pl.ANY),
            pl.BlockSpec(memory_space=pl.ANY),
        ],
        out_specs=(pl.BlockSpec(memory_space=pltpu.VMEM),) * 3,
        scratch_shapes=[
            pltpu.SMEM((taps,), jnp.float32),
            pltpu.SMEM(shifts.shape, jnp.int32),
            pltpu.VMEM((maps, tiles + 1, rows + 2 * ABOVE, LANES), jnp.float32),
            pltpu.VMEM((frames, rows, width), jnp.float32),
            pltpu.VMEM((frames, tiles + 1, rows + 2 * HALO, LANES), jnp.float32),
            pltpu.VMEM((blocks + 3, frames, tiles + 1, BLOCK, LANES), jnp.float32),
            pltpu.VMEM((frames, HALO, width), jnp.float32),
            pltpu.VMEM((frames, HALO, width), jnp.float32),
            pltpu.VMEM((9 * LANES, LANES), jnp.bfloat16),
            pltpu.VMEM((6 * LANES, LANES), jnp.bfloat16),
            pltpu.VMEM((taps, 8, LANES), jnp.float32),
            pltpu.SemaphoreType.REGULAR((4,)),
            dma((2,)),
            dma,
            dma((2,)),
            dma((blocks,)),
            dma((vels // 2,)),
            dma((vels // 2,)),
            dma((2,)),
            dma((blocks + 3,)),
            dma((2,)),
            dma((2,)),
            dma((2,)),
            dma((2,)),
            dma((2,)),
        ],
        compiler_params=pltpu.CompilerParams(
            collective_id=0, has_side_effects=True, vmem_limit_bytes=36 * 2**20
        ),
        name="gather",
    )(psf_taps, shifts, psi_maps, phi_maps)
    return pl.pallas_call(
        functools.partial(finish_kernel, vels),
        out_shape=jax.ShapeDtypeStruct((trials, rows, width), jnp.float32),
        in_specs=[pl.BlockSpec(memory_space=pltpu.VMEM)] * 3,
        out_specs=pl.BlockSpec(memory_space=pl.ANY),
        scratch_shapes=[
            pltpu.VMEM((trials, 2 * share, width), jnp.float32),
            dma((3, trials)),
        ],
        compiler_params=pltpu.CompilerParams(vmem_limit_bytes=4 * 2**20),
        name="finish",
    )(part, fresh, done)


def solution(mesh):
    return jax.shard_map(
        functools.partial(per_device, mesh.shape["vel"], mesh.shape["sky"]),
        mesh=mesh,
        in_specs=(
            P(None, ("sky", "vel"), None),
            P(None, ("sky", "vel"), None),
            P(),
            P("vel", None, None),
        ),
        out_specs=P("vel", "sky", None),
        check_vma=False,
    )
```

```python
import functools
import jax
import jax.numpy as jnp
from jax import lax
from jax.experimental import pallas as pl
from jax.experimental.pallas import tpu as pltpu
from jax.sharding import PartitionSpec as P

SHIFT = 16
BLOCK = 16
HALO = 2 * BLOCK
ABOVE = BLOCK + 8
JOIN = 4 * BLOCK
LANES = 128
MESH = pl.DeviceIdType.MESH


def stack_rows(shifts_ref, maps_ref, out_ref, trial, first, count, skip, partial, unroll):
    frames = shifts_ref.shape[0]
    tiles = maps_ref.shape[1]
    lane = lax.broadcasted_iota(jnp.int32, (8, LANES), 1)
    down, turn, inside = [], [], []
    for frame in range(1, frames):
        offset = shifts_ref[frame, 1, trial] + SHIFT
        down.append(shifts_ref[frame, 0, trial] + ABOVE)
        turn.append(lax.rem(LANES - offset, LANES))
        inside.append(lane >= offset)

    def one_group(group, carry):
        base = first + group * 8

        def stacked(kind):
            total = [None] * (tiles - 1)
            if not partial:
                total = [
                    maps_ref[kind * frames, tile, pl.ds(pl.multiple_of(base + ABOVE, 8), 8)]
                    for tile in range(tiles - 1)
                ]
            for step in range(frames - 1):
                m = kind * frames + step + 1
                pieces = [maps_ref[m, tile, pl.ds(base + down[step], 8)] for tile in range(tiles)]
                for tile in range(tiles - 1):
                    joined = jnp.where(inside[step], pieces[tile], pieces[tile + 1])
                    moved = pltpu.roll(joined, turn[step], 1)
                    total[tile] = moved if total[tile] is None else total[tile] + moved
            return total

        psi = stacked(0)
        phi = stacked(1)
        rows = pl.ds(pl.multiple_of(base - skip, 8), 8)
        for tile in range(tiles - 1):
            columns = slice(tile * LANES, (tile + 1) * LANES)
            if partial:
                out_ref[0, trial, rows, columns] = psi[tile]
                out_ref[1, trial, rows, columns] = phi[tile]
            else:
                out_ref[trial, rows, columns] = psi[tile] * lax.rsqrt(phi[tile])
        return carry

    lax.fori_loop(0, count // 8, one_group, 0, unroll=unroll)


def last_row(chips, per, to_right):
    return pl.multiple_of(jnp.where(to_right, ABOVE, BLOCK * per * (chips - 1) - ABOVE), 8)


def finish_kernel(vels, part_ref, fresh_ref, done_ref, out_ref, closing, sems):
    trials, rows, width = done_ref.shape
    count = part_ref.shape[2]
    chips = vels // 2
    low = lax.axis_index("vel") // 2 < chips // 2
    first = last_row(chips, count // BLOCK, jnp.logical_not(low))
    small = ABOVE
    large = rows - count - small
    large_row = pl.multiple_of(jnp.where(low, 0, small + count), 8)
    small_row = pl.multiple_of(jnp.where(low, large + count, 0), 8)

    def large_copy(trial):
        part = pl.ds(large_row, large)
        return pltpu.make_async_copy(done_ref.at[trial, part], out_ref.at[trial, part], sems.at[0, trial])

    def small_copy(trial):
        part = pl.ds(small_row, small)
        return pltpu.make_async_copy(done_ref.at[trial, part], out_ref.at[trial, part], sems.at[1, trial])

    def closing_copy(trial):
        part = pl.ds(first, count)
        return pltpu.make_async_copy(closing.at[trial], out_ref.at[trial, part], sems.at[2, trial])

    def begin(trial, carry):
        large_copy(trial).start()
        small_copy(trial).start()
        return carry

    lax.fori_loop(0, trials, begin, 0)

    def compute(trial, carry):
        for tile in range(width // LANES):
            columns = slice(tile * LANES, (tile + 1) * LANES)
            psi = part_ref[0, trial, :, columns] + fresh_ref[0, 0, tile]
            phi = part_ref[1, trial, :, columns] + fresh_ref[0, 1, tile]
            closing[trial, :, columns] = psi * lax.rsqrt(phi)
        closing_copy(trial).start()
        return carry

    lax.fori_loop(0, trials, compute, 0)

    def finish(trial, carry):
        large_copy(trial).wait()
        small_copy(trial).wait()
        closing_copy(trial).wait()
        return carry

    lax.fori_loop(0, trials, finish, 0)


def gather_kernel(
    vels, skies, taps_hbm, shifts_hbm, psi_ref, phi_ref, part_ref, fresh_ref, done_ref,
    taps_ref, shifts_ref, blurred, raw, along, landing, top, bottom, band0, band1, weight,
    answers, small_sems, own_sem, trade_sems, recv_sem, right_sem, left_sem, pair_sends, pair_recv, top_sems, bottom_sems,
    first_sems, fresh_send, fresh_recv,
):
    frames, share, width = psi_ref.shape
    trials = shifts_ref.shape[2]
    taps = taps_ref.shape[0]
    half = taps // 2
    chips = vels // 2
    tiles = width // LANES
    rows = vels * share
    blocks = rows // BLOCK
    per = blocks // chips
    steps = per * (chips - 1)
    sky = lax.axis_index("sky")
    vel = lax.axis_index("vel")
    chip = vel // 2
    core = vel % 2
    has_right = chip < chips - 1
    has_left = chip > 0
    has_next = sky < skies - 1
    has_prev = sky > 0
    low = chip < chips // 2
    partner = (sky, vel + 1 - 2 * core)

    taps_copy = pltpu.make_async_copy(taps_hbm, taps_ref, small_sems.at[0])
    shifts_copy = pltpu.make_async_copy(shifts_hbm, shifts_ref, small_sems.at[1])
    own_rows = pl.ds(pl.multiple_of(vel * share, 8), share)

    def own_copy(source):
        return pltpu.make_async_copy(source, raw.at[:, own_rows], own_sem)

    @pl.when(core == 0)
    def _():
        own_copy(psi_ref).start()

    @pl.when(core == 1)
    def _():
        own_copy(phi_ref).start()

    taps_copy.start()
    shifts_copy.start()
    left, right = (sky, vel - 2), (sky, vel + 2)
    before, after = (sky - 1, vel), (sky + 1, vel)
    skies_near = ((has_prev & (core == 1), before), (has_next & (core == 1), after))
    barrier = pltpu.get_barrier_semaphore()

    def greet(semaphore, device, present):
        @pl.when(present)
        def _():
            pl.semaphore_signal(semaphore, inc=1, device_id=device, device_id_type=MESH)

    greet(barrier, right, has_right)
    greet(barrier, partner, (core == 0) | (chip == 0))
    for present, device in skies_near:
        greet(barrier, device, present)
    callers = (has_left | (core == 0)).astype(jnp.int32) + core
    for present, device in skies_near:
        callers = callers + present.astype(jnp.int32)
    pl.semaphore_wait(barrier, callers)
    greet(answers.at[0], left, has_left)
    greet(answers.at[1], partner, core == 1)
    for present, device in skies_near:
        greet(answers.at[2], device, present)

    def trade_copy(source):
        return pltpu.make_async_remote_copy(
            src_ref=source,
            dst_ref=raw.at[:, own_rows],
            send_sem=trade_sems.at[0],
            recv_sem=trade_sems.at[1],
            device_id=partner,
            device_id_type=MESH,
        )

    def block_rows(block):
        return pl.ds(pl.multiple_of(block * BLOCK, 8), BLOCK)

    def line_copy(block, to_right, late, source=None):
        maps = pl.ds(1, frames - 1) if late else pl.ds(0, frames)
        place = raw.at[maps, block_rows(block)]
        return pltpu.make_async_remote_copy(
            src_ref=place if source is None else source[0].at[maps, block_rows(source[1])],
            dst_ref=place,
            send_sem=(right_sem if to_right else left_sem).at[block // per],
            recv_sem=recv_sem.at[block],
            device_id=(sky, vel + 2) if to_right else (sky, vel - 2),
            device_id_type=MESH,
        )

    def send_block(block, to_right, source=None):
        if to_right:
            late = (block < per) & (block > 1)
        else:
            late = (block >= blocks - per) & (block < blocks - 2)

        @pl.when(late)
        def _():
            line_copy(block, to_right, True, source).start()

        @pl.when(jnp.logical_not(late))
        def _():
            line_copy(block, to_right, False, source).start()

    most = BLOCK * (per - 3)
    rest = 3 * BLOCK

    def first_rows(to_right, piece):
        begin = HALO if to_right else BLOCK * per * (chips - 1)
        if piece == 0:
            return begin + (0 if to_right else BLOCK), most
        return begin + (most if to_right else 0), BLOCK

    def fresh_rows(to_right, piece):
        if piece == 0:
            return (0 if to_right else rest), most
        return (most if to_right else 0), rest

    def first_copy(to_right, piece):
        place = raw.at[0, pl.ds(*first_rows(to_right, piece))]
        return pltpu.make_async_remote_copy(
            src_ref=place,
            dst_ref=place,
            send_sem=right_sem.at[0] if to_right else left_sem.at[chips - 1],
            recv_sem=first_sems.at[1 if to_right else 0, piece],
            device_id=(sky, vel + 2) if to_right else (sky, vel - 2),
            device_id_type=MESH,
        )

    def fresh_copy(to_right, slot, piece):
        place = fresh_ref.at[slot, core, :, pl.ds(*fresh_rows(to_right, piece))]
        return pltpu.make_async_remote_copy(
            src_ref=place,
            dst_ref=place,
            send_sem=fresh_send.at[slot, piece],
            recv_sem=fresh_recv.at[slot, piece],
            device_id=partner,
            device_id_type=MESH,
        )

    def halo_copy(to_next):
        source = raw.at[:, pl.ds(rows - HALO if to_next else 0, HALO)]
        sems = top_sems if to_next else bottom_sems
        return pltpu.make_async_remote_copy(
            src_ref=source,
            dst_ref=top if to_next else bottom,
            send_sem=sems.at[0],
            recv_sem=sems.at[1],
            device_id=(sky + 1, vel) if to_next else (sky - 1, vel),
            device_id_type=MESH,
        )

    def pair_copy(blur, late):
        skip = 1 if late else 0
        place = pl.ds(pl.multiple_of((blur + 1) * BLOCK, 8), BLOCK)
        return pltpu.make_async_remote_copy(
            src_ref=blurred.at[pl.ds(core * frames + skip, frames - skip), :, place],
            dst_ref=landing.at[blur + 1, pl.ds(skip, frames - skip)],
            send_sem=pair_sends.at[skip],
            recv_sem=pair_recv.at[blur + 1],
            device_id=partner,
            device_id_type=MESH,
        )

    def to_partner(blur, late):
        @pl.when(late)
        def _():
            pair_copy(blur, True).start()

        @pl.when(jnp.logical_not(late))
        def _():
            pair_copy(blur, False).start()

    def from_partner(blur, late):
        place = pl.ds(pl.multiple_of((blur + 1) * BLOCK, 8), BLOCK)

        @pl.when(late)
        def _():
            pair_copy(blur, True).wait_recv()

        @pl.when(jnp.logical_not(late))
        def _():
            pair_copy(blur, False).wait_recv()
            for tile in range(tiles):
                blurred[(1 - core) * frames, tile, place] = landing[blur + 1, 0, tile]

        for m in range(1, frames):
            for tile in range(tiles + 1):
                blurred[(1 - core) * frames + m, tile, place] = landing[blur + 1, m, tile]

    right_up = chip == 0
    left_up = chip < chips - 1

    def send_half(to_right, upward, part, source=None):
        def one(index, carry):
            place = jnp.where(upward, index, per // 2 - 1 - index)
            there = None if source is None else (source, place)
            send_block(chip * per + part * (per // 2) + place, to_right, there)
            return carry

        lax.fori_loop(0, per // 2, one, 0)

    def send_first(to_right, upward, ready):
        for kind, source in ((0, psi_ref), (1, phi_ref)):

            @pl.when(ready & (core == kind))
            def _(source=source):
                send_half(to_right, upward, core, source)

    right_ready = (chip > 0) | (core == 0)
    left_ready = (chip < chips - 1) | (core == 1)
    send_first(False, left_up, has_left & left_ready)

    @pl.when(core == 0)
    def _():
        pl.semaphore_wait(answers.at[1], 1)
        trade_copy(phi_ref).start()

    @pl.when(core == 1)
    def _():
        trade_copy(psi_ref).start()

    @pl.when(has_right)
    def _():
        pl.semaphore_wait(answers.at[0], 1)

    send_first(True, right_up, has_right & right_ready)
    own_copy(psi_ref).wait()
    taps_copy.wait()
    shifts_copy.wait()
    total = taps_ref[0]
    for i in range(1, taps):
        total = total + taps_ref[i]
    scale = 1.0 / jnp.full((8, LANES), total, jnp.float32)
    squared = jnp.full((8, LANES), core, jnp.int32) > 0
    for i in range(taps):
        value = jnp.full((8, LANES), taps_ref[i], jnp.float32) * scale
        weight[i] = jnp.where(squared, value * value, value)
    for lead, band in ((0, band0), (1, band1)):
        depth = (3 - lead) * LANES
        place = lax.broadcasted_iota(jnp.int32, (depth, LANES), 0)
        place = place - lax.broadcasted_iota(jnp.int32, (depth, LANES), 1)
        spot = place - (LANES - SHIFT * lead - half)
        matrix = jnp.zeros((depth, LANES), jnp.float32)
        for i in range(taps):
            value = jnp.broadcast_to(weight[i][:1], (depth, LANES))
            matrix = jnp.where(spot == i, value, matrix)
        coarse = matrix.astype(jnp.bfloat16)
        band[:depth] = coarse
        band[depth : 2 * depth] = coarse
        band[2 * depth :] = (matrix - coarse.astype(jnp.float32)).astype(jnp.bfloat16)

    trade_copy(psi_ref).wait_recv()

    def send_rest(to_right, upward, present, ready):
        @pl.when(present)
        def _():
            send_half(to_right, upward, 1 - core)

        @pl.when(present & jnp.logical_not(ready))
        def _():
            send_half(to_right, upward, core)

    send_rest(False, left_up, has_left, left_ready)
    send_rest(True, right_up, has_right, right_ready)

    @pl.when(chip == chips - 1)
    def _():
        first_copy(False, 0).start()
        first_copy(False, 1).start()

    @pl.when(chip == 0)
    def _():
        first_copy(True, 0).start()
        first_copy(True, 1).start()

    @pl.when(core == 1)
    def _():
        pl.semaphore_wait(answers.at[2], has_prev.astype(jnp.int32) + has_next.astype(jnp.int32))
        pl.semaphore_signal(answers.at[3], inc=1, device_id=partner, device_id_type=MESH)

    @pl.when(core == 0)
    def _():
        pl.semaphore_wait(answers.at[3], 1)

    @pl.when(has_next & (chip == chips - 1))
    def _():
        halo_copy(True).start()

    @pl.when(has_prev & (chip == 0))
    def _():
        halo_copy(False).start()

    def blur_along(source, start, count, place, lead):
        def windows(values, lead):
            blank = jnp.zeros((values.shape[0], LANES), values.dtype)
            columns = [blank] + [values[:, t * LANES : (t + 1) * LANES] for t in range(tiles)] + [blank]
            wide = 3 - lead
            return jnp.concatenate(
                [jnp.concatenate(columns[t : t + wide], axis=1) for t in range(tiles + lead)], axis=0
            )

        band = band1 if lead else band0
        if lead:
            values = source[1:frames, pl.ds(start, count)].reshape((frames - 1) * count, width)
        else:
            values = source[0, pl.ds(start, count)]
        height = values.shape[0]
        coarse = values.astype(jnp.bfloat16)
        fine = (values - coarse.astype(jnp.float32)).astype(jnp.bfloat16)
        high, rest = windows(coarse, lead), windows(fine, lead)
        blurred = jnp.dot(
            jnp.concatenate([high, rest, high], axis=1), band[...],
            preferred_element_type=jnp.float32,
        )
        for tile in range(tiles + lead):
            piece = blurred[tile * height : (tile + 1) * height]
            if lead and tile in (0, tiles):
                lane = lax.broadcasted_iota(jnp.int32, (height, LANES), 1)
                piece = jnp.where(lane >= SHIFT if tile == 0 else lane < SHIFT, piece, 0.0)
            for m in range(height // count):
                along[lead + m, tile, pl.ds(place, count)] = piece[m * count : (m + 1) * count]

    def blur_block(block, late):
        start = pl.multiple_of(block * BLOCK, 8)
        place = pl.multiple_of(start + HALO, 8)
        blur_along(raw, start, BLOCK, place, 1)

        @pl.when(jnp.logical_not(late))
        def _():
            blur_along(raw, start, BLOCK, place, 0)

    def across(m, tile, start, target, place, count):
        factors = [weight[i] for i in range(taps)]
        for group in range(count // 8):
            base = start + 8 * group
            value = factors[0] * along[m, tile, pl.ds(base, 8)]
            for i in range(1, taps):
                value += factors[i] * along[m, tile, pl.ds(base + i, 8)]
            target[pl.ds(pl.multiple_of(place + 8 * group, 8), 8)] = value

    def blur_across(blur, late):
        start = blur * BLOCK + HALO - 8 - half
        place = (blur + 1) * BLOCK

        def one_map(m, carry):
            for tile in range(tiles + 1):
                across(m, tile, start, blurred.at[core * frames + m, tile], place, BLOCK)
            return carry

        lax.fori_loop(jnp.asarray(late, jnp.int32), frames, one_map, 0)

    def first_arrives(to_right, slot):
        region = ABOVE if to_right else BLOCK * per * (chips - 1) - ABOVE
        for piece in range(2):
            first_copy(to_right, piece).wait_recv()

            @pl.when(has_right if to_right else has_left)
            def _(piece=piece):
                first_copy(to_right, piece).start()

            start, count = first_rows(to_right, piece)
            blur_along(raw, start, count, start + HALO, 0)
            begin, height = fresh_rows(to_right, piece)

            def one_tile(tile, carry, begin=begin, height=height):
                target = fresh_ref.at[slot, core, tile]
                across(0, tile, region + begin + HALO - half, target, begin, height)
                return carry

            lax.fori_loop(0, tiles, one_tile, 0)
            fresh_copy(to_right, slot, piece).start()

    def fresh_wait(to_right, slot):
        for piece in range(2):
            fresh_copy(to_right, slot, piece).wait_recv()

    def together(count):
        return max(JOIN // count, 1) if trials % 4 == 0 else 1

    def stack(first, count, unroll):
        def one_trial(trial, carry):
            stack_rows(shifts_ref, blurred, done_ref, trial, first, count, 0, False, unroll)
            return carry

        lax.fori_loop(0, trials, one_trial, 0, unroll=together(count))

    closing = last_row(chips, per, jnp.logical_not(low))
    other = last_row(chips, per, low)

    def stack_part(first, count, unroll):
        def one_trial(trial, carry):
            stack_rows(shifts_ref, blurred, part_ref, trial, first, count, closing, True, unroll)
            return carry

        lax.fori_loop(0, trials, one_trial, 0, unroll=together(count))


    def own_block(block, carry):
        blur_block(block, False)
        return carry

    def own_blur(blur, carry):
        blur_across(blur, False)
        pair_copy(blur, False).start()
        return carry

    def own_wait(blur, carry):
        from_partner(blur, False)
        return carry

    lax.fori_loop(chip * per, chip * per + per, own_block, 0)
    lax.fori_loop(chip * per + 1, chip * per + per, own_blur, 0)
    lax.fori_loop(chip * per + 1, chip * per + per, own_wait, 0)
    stack(pl.multiple_of((chip * per + 2) * BLOCK - 8, 8), BLOCK * (per - 3), 2)

    def stream(side, index):
        distance = index // per
        j = index % per
        origin = jnp.where(side == 1, chip + 1 + distance, chip - 1 - distance)
        present = (index >= 0) & (origin >= 0) & (origin < chips)
        edge = jnp.where(side == 1, origin == chips - 1, origin == 0)
        upward = (side == 1) != edge
        block = origin * per + jnp.where(upward, j, per - 1 - j)
        last = edge & (j == per - 1)
        return present, edge, upward, j, block, last

    def blurs(side, index, act):
        present, edge, upward, j, block, last = stream(side, index)
        count = jnp.where(present & jnp.logical_not(edge & (j == 0)), 1 + last.astype(jnp.int32), 0)
        begin = jnp.where(upward, block, block + 1)
        turn = jnp.where(upward, 1, -1)

        def one(k, carry):
            act(begin + turn * k)
            return carry

        lax.fori_loop(0, count, one, 0)

    def arrive(index):
        for side in (1, 0):
            present, edge, _, j, block, _ = stream(side, index)
            late = edge & (j > 1)

            @pl.when(present & late)
            def _(side=side, block=block):
                line_copy(block, True, True).wait_recv()

            @pl.when(present & jnp.logical_not(late))
            def _(side=side, block=block):
                line_copy(block, True, False).wait_recv()

            @pl.when(present & (has_left if side else has_right))
            def _(side=side, block=block):
                send_block(block, side == 0)

            @pl.when(present & edge & (j == 1) & (has_next if side else has_prev))
            def _(side=side):
                halo_copy(side == 1).start()

    def blur_side(index):
        def one_side(side, carry):
            present, edge, _, j, block, _ = stream(side, index)
            late = edge & (j > 1)

            @pl.when(present)
            def _():
                blur_block(block, late)

            def spread(blur):
                blur_across(blur, late)
                to_partner(blur, late)

            blurs(side, index, spread)
            return carry

        lax.fori_loop(0, 2, one_side, 0)

    def stack_side(index):
        def one_side(side, carry):
            present, edge, upward, j, block, last = stream(side, index)
            late = edge & (j > 1)
            blurs(side, index, lambda blur: from_partner(blur, late))
            begin = pl.multiple_of(jnp.where(upward, block - 1, block + 2) * BLOCK - 8, 8)
            closes = (side == 1) == low

            @pl.when(present & jnp.logical_not(edge))
            def _():
                stack(begin, BLOCK, True)

            @pl.when(present & edge & closes & jnp.logical_not(last) & (j > 2))
            def _():
                stack_part(begin, BLOCK, True)

            @pl.when(present & closes & last)
            def _():
                stack_part(pl.multiple_of((block - 1) * BLOCK - 8, 8), JOIN, True)

            return carry

        lax.fori_loop(0, 2, one_side, 0)

    limit = steps - 2
    mirror = chips - 1 - chip
    top_step = jnp.minimum(jnp.maximum(per * (mirror - 1) + 4, per * (chip - 1) + 2), limit)
    bottom_step = jnp.minimum(jnp.maximum(per * (chip - 1) + 4, per * (mirror - 1) + 2), limit)

    others = jnp.where(low, chip, mirror)
    other_step = jnp.where(others > 0, per * others + 2, -2)

    def step(index, carry):
        @pl.when(index < steps)
        def _():
            arrive(index)
            blur_side(index)

        @pl.when(index == top_step)
        def _():
            @pl.when(has_prev)
            def _():
                halo_copy(True).wait_recv()
                blur_along(top, 0, HALO, 0, 0)
                blur_along(top, 0, HALO, 0, 1)

            @pl.when(jnp.logical_not(has_prev))
            def _():
                for m in range(frames):
                    for tile in range(tiles + 1):
                        along[m, tile, pl.ds(0, HALO)] = jnp.zeros((HALO, LANES), jnp.float32)

            blur_across(-1, False)
            blur_across(0, False)

            @pl.when(jnp.logical_not(has_prev))
            def _():
                for m in range(frames):
                    for tile in range(tiles + 1):
                        blurred[core * frames + m, tile, pl.ds(0, ABOVE)] = jnp.zeros(
                            (ABOVE, LANES), jnp.float32
                        )

            pair_copy(-1, False).start()
            pair_copy(0, False).start()

        @pl.when(index == bottom_step)
        def _():
            @pl.when(has_next)
            def _():
                halo_copy(False).wait_recv()
                blur_along(bottom, 0, HALO, rows + HALO, 0)
                blur_along(bottom, 0, HALO, rows + HALO, 1)

            @pl.when(jnp.logical_not(has_next))
            def _():
                for m in range(frames):
                    for tile in range(tiles + 1):
                        along[m, tile, pl.ds(rows + HALO, HALO)] = jnp.zeros(
                            (HALO, LANES), jnp.float32
                        )

            blur_across(blocks, False)
            blur_across(blocks + 1, False)

            @pl.when(jnp.logical_not(has_next))
            def _():
                for m in range(frames):
                    for tile in range(tiles + 1):
                        blurred[core * frames + m, tile, pl.ds(rows + ABOVE, ABOVE)] = jnp.zeros(
                            (ABOVE, LANES), jnp.float32
                        )

            pair_copy(blocks, False).start()
            pair_copy(blocks + 1, False).start()

        @pl.when(index == other_step)
        def _():
            @pl.when(low)
            def _():
                first_arrives(True, 1)

            @pl.when(jnp.logical_not(low))
            def _():
                first_arrives(False, 1)

        stack_side(index - 1)

        @pl.when(index - 1 == other_step)
        def _():
            @pl.when(low)
            def _():
                fresh_wait(True, 1)

            @pl.when(jnp.logical_not(low))
            def _():
                fresh_wait(False, 1)

            behind = jnp.where(low, 0, BLOCK)
            count = BLOCK * (per - 1)
            place = pl.ds(pl.multiple_of(other + behind + ABOVE, 8), count)
            for kind in range(2):
                for tile in range(tiles):
                    there = pl.ds(pl.multiple_of(behind, 8), count)
                    blurred[kind * frames, tile, place] = fresh_ref[1, kind, tile, there]
            stack(other, BLOCK * per, 4)

        @pl.when(index - 1 == top_step)
        def _():
            from_partner(-1, False)
            from_partner(0, False)
            stack(0, ABOVE, True)

        @pl.when(index - 1 == bottom_step)
        def _():
            from_partner(blocks, False)
            from_partner(blocks + 1, False)
            stack(rows - ABOVE, ABOVE, True)

        return carry

    lax.fori_loop(0, steps + 1, step, 0)

    def drain_sends():
        for sides in (1, 2):
            late = (per - 1) * sides
            whole = blurred.at[pl.ds(0, frames), :, pl.ds(0, (blocks + 3 - late) * BLOCK)]
            most = blurred.at[pl.ds(0, frames - 1), :, pl.ds(0, late * BLOCK)]

            @pl.when(has_left.astype(jnp.int32) + has_right.astype(jnp.int32) == sides)
            def _(whole=whole, most=most):
                pltpu.make_async_copy(whole, whole, pair_sends.at[0]).wait()
                pltpu.make_async_copy(most, most, pair_sends.at[1]).wait()

        trade_copy(psi_ref).wait_send()

        def drain(origin, carry):
            part = raw.at[:, pl.ds(pl.multiple_of(origin * (2 * share), 8), 2 * share)]

            @pl.when(has_right & (origin <= chip))
            def _():
                pltpu.make_async_copy(part, part, right_sem.at[origin]).wait()

            @pl.when(has_left & (origin >= chip))
            def _():
                pltpu.make_async_copy(part, part, left_sem.at[origin]).wait()

            return carry

        lax.fori_loop(0, chips, drain, 0)

        @pl.when((other_step > 0) & low)
        def _():
            for piece in range(2):
                fresh_copy(True, 1, piece).wait_send()

        @pl.when((other_step > 0) & jnp.logical_not(low))
        def _():
            for piece in range(2):
                fresh_copy(False, 1, piece).wait_send()

        @pl.when(has_next)
        def _():
            halo_copy(True).wait_send()

        @pl.when(has_prev)
        def _():
            halo_copy(False).wait_send()


    @pl.when(others == 0)
    def _():
        drain_sends()

    @pl.when(low)
    def _():
        first_arrives(False, 0)

    @pl.when(jnp.logical_not(low))
    def _():
        first_arrives(True, 0)

    @pl.when(others > 0)
    def _():
        drain_sends()

    for piece in range(2):

        @pl.when(low)
        def _(piece=piece):
            fresh_copy(False, 0, piece).wait()

        @pl.when(jnp.logical_not(low))
        def _(piece=piece):
            fresh_copy(True, 0, piece).wait()


def per_device(vels, skies, psi_maps, phi_maps, psf_taps, shifts):
    frames, share, width = psi_maps.shape
    maps = 2 * frames
    tiles = width // LANES
    rows = share * vels
    trials = shifts.shape[0]
    blocks = rows // BLOCK
    taps = psf_taps.shape[0]
    shifts = pltpu.with_memory_space_constraint(jnp.transpose(shifts, (1, 2, 0)), pltpu.HBM)
    psf_taps = pltpu.with_memory_space_constraint(psf_taps, pltpu.HBM)
    psi_maps = pltpu.with_memory_space_constraint(psi_maps, pltpu.HBM)
    phi_maps = pltpu.with_memory_space_constraint(phi_maps, pltpu.HBM)
    dma = pltpu.SemaphoreType.DMA
    part, fresh, done = pl.pallas_call(
        functools.partial(gather_kernel, vels, skies),
        out_shape=(
            jax.ShapeDtypeStruct((2, trials, 2 * share, width), jnp.float32),
            jax.ShapeDtypeStruct((2, 2, tiles, 2 * share, LANES), jnp.float32),
            jax.ShapeDtypeStruct((trials, rows, width), jnp.float32),
        ),
        in_specs=[
            pl.BlockSpec(memory_space=pl.ANY),
            pl.BlockSpec(memory_space=pl.ANY),
            pl.BlockSpec(memory_space=pl.ANY),
            pl.BlockSpec(memory_space=pl.ANY),
        ],
        out_specs=(pl.BlockSpec(memory_space=pltpu.VMEM),) * 3,
        scratch_shapes=[
            pltpu.SMEM((taps,), jnp.float32),
            pltpu.SMEM(shifts.shape, jnp.int32),
            pltpu.VMEM((maps, tiles + 1, rows + 2 * ABOVE, LANES), jnp.float32),
            pltpu.VMEM((frames, rows, width), jnp.float32),
            pltpu.VMEM((frames, tiles + 1, rows + 2 * HALO, LANES), jnp.float32),
            pltpu.VMEM((blocks + 3, frames, tiles + 1, BLOCK, LANES), jnp.float32),
            pltpu.VMEM((frames, HALO, width), jnp.float32),
            pltpu.VMEM((frames, HALO, width), jnp.float32),
            pltpu.VMEM((9 * LANES, LANES), jnp.bfloat16),
            pltpu.VMEM((6 * LANES, LANES), jnp.bfloat16),
            pltpu.VMEM((taps, 8, LANES), jnp.float32),
            pltpu.SemaphoreType.REGULAR((4,)),
            dma((2,)),
            dma,
            dma((2,)),
            dma((blocks,)),
            dma((vels // 2,)),
            dma((vels // 2,)),
            dma((2,)),
            dma((blocks + 3,)),
            dma((2,)),
            dma((2,)),
            dma((2, 2)),
            dma((2, 2)),
            dma((2, 2)),
        ],
        compiler_params=pltpu.CompilerParams(
            collective_id=0, has_side_effects=True, vmem_limit_bytes=36 * 2**20
        ),
        name="gather",
    )(psf_taps, shifts, psi_maps, phi_maps)
    return pl.pallas_call(
        functools.partial(finish_kernel, vels),
        out_shape=jax.ShapeDtypeStruct((trials, rows, width), jnp.float32),
        in_specs=[pl.BlockSpec(memory_space=pltpu.VMEM)] * 3,
        out_specs=pl.BlockSpec(memory_space=pl.ANY),
        scratch_shapes=[
            pltpu.VMEM((trials, 2 * share, width), jnp.float32),
            dma((3, trials)),
        ],
        compiler_params=pltpu.CompilerParams(vmem_limit_bytes=4 * 2**20),
        name="finish",
    )(part, fresh, done)


def solution(mesh):
    return jax.shard_map(
        functools.partial(per_device, mesh.shape["vel"], mesh.shape["sky"]),
        mesh=mesh,
        in_specs=(
            P(None, ("sky", "vel"), None),
            P(None, ("sky", "vel"), None),
            P(),
            P("vel", None, None),
        ),
        out_specs=P("vel", "sky", None),
        check_vma=False,
    )
```

```python
import functools
import jax
import jax.numpy as jnp
from jax import lax
from jax.experimental import pallas as pl
from jax.experimental.pallas import tpu as pltpu
from jax.sharding import PartitionSpec as P

SHIFT = 16
BLOCK = 16
HALO = 2 * BLOCK
ABOVE = BLOCK + 8
JOIN = 4 * BLOCK
LANES = 128
MESH = pl.DeviceIdType.MESH


def stack_rows(shifts_ref, maps_ref, out_ref, trial, first, count, skip, partial, unroll):
    frames = shifts_ref.shape[0]
    tiles = maps_ref.shape[1]
    lane = lax.broadcasted_iota(jnp.int32, (8, LANES), 1)
    down, turn, inside = [], [], []
    for frame in range(1, frames):
        offset = shifts_ref[frame, 1, trial] + SHIFT
        down.append(shifts_ref[frame, 0, trial] + ABOVE)
        turn.append(lax.rem(LANES - offset, LANES))
        inside.append(lane >= offset)

    def one_group(group, carry):
        base = first + group * 8

        def stacked(kind):
            total = [None] * (tiles - 1)
            if not partial:
                total = [
                    maps_ref[kind * frames, tile, pl.ds(pl.multiple_of(base + ABOVE, 8), 8)]
                    for tile in range(tiles - 1)
                ]
            for step in range(frames - 1):
                m = kind * frames + step + 1
                pieces = [maps_ref[m, tile, pl.ds(base + down[step], 8)] for tile in range(tiles)]
                for tile in range(tiles - 1):
                    joined = jnp.where(inside[step], pieces[tile], pieces[tile + 1])
                    moved = pltpu.roll(joined, turn[step], 1)
                    total[tile] = moved if total[tile] is None else total[tile] + moved
            return total

        psi = stacked(0)
        phi = stacked(1)
        rows = pl.ds(pl.multiple_of(base - skip, 8), 8)
        for tile in range(tiles - 1):
            columns = slice(tile * LANES, (tile + 1) * LANES)
            if partial:
                out_ref[0, trial, rows, columns] = psi[tile]
                out_ref[1, trial, rows, columns] = phi[tile]
            else:
                out_ref[trial, rows, columns] = psi[tile] * lax.rsqrt(phi[tile])
        return carry

    lax.fori_loop(0, count // 8, one_group, 0, unroll=unroll)


def last_row(chips, per, to_right):
    return pl.multiple_of(jnp.where(to_right, ABOVE, BLOCK * per * (chips - 1) - ABOVE), 8)


def blur_columns(values, band, lead):
    tiles = values.shape[1] // LANES
    coarse = values.astype(jnp.bfloat16)
    fine = (values - coarse.astype(jnp.float32)).astype(jnp.bfloat16)

    def windows(part):
        blank = jnp.zeros((part.shape[0], LANES), part.dtype)
        columns = [blank] + [part[:, t * LANES : (t + 1) * LANES] for t in range(tiles)] + [blank]
        wide = 3 - lead
        return jnp.concatenate(
            [jnp.concatenate(columns[t : t + wide], axis=1) for t in range(tiles + lead)], axis=0
        )

    high, rest = windows(coarse), windows(fine)
    return jnp.dot(
        jnp.concatenate([high, rest, high], axis=1), band, preferred_element_type=jnp.float32
    )


def finish_kernel(
    vels, part_ref, ends_ref, bands_ref, weights_ref, done_ref, out_ref, along, fresh, closing, sems
):
    trials, rows, width = done_ref.shape
    count = part_ref.shape[2]
    height = ends_ref.shape[1]
    taps = weights_ref.shape[1]
    tiles = width // LANES
    chips = vels // 2
    low = lax.axis_index("vel") // 2 < chips // 2
    first = last_row(chips, count // BLOCK, jnp.logical_not(low))
    small = ABOVE
    large = rows - count - small
    large_row = pl.multiple_of(jnp.where(low, 0, small + count), 8)
    small_row = pl.multiple_of(jnp.where(low, large + count, 0), 8)

    def large_copy(trial):
        part = pl.ds(large_row, large)
        return pltpu.make_async_copy(done_ref.at[trial, part], out_ref.at[trial, part], sems.at[0, trial])

    def small_copy(trial):
        part = pl.ds(small_row, small)
        return pltpu.make_async_copy(done_ref.at[trial, part], out_ref.at[trial, part], sems.at[1, trial])

    def closing_copy(trial):
        part = pl.ds(first, count)
        return pltpu.make_async_copy(closing.at[trial], out_ref.at[trial, part], sems.at[2, trial])

    def begin(trial, carry):
        large_copy(trial).start()
        small_copy(trial).start()
        return carry

    lax.fori_loop(0, trials, begin, 0)

    for kind in range(2):
        blurred = blur_columns(ends_ref[kind], bands_ref[kind], 0)
        for tile in range(tiles):
            along[kind, tile] = blurred[tile * height : (tile + 1) * height]
    start = jnp.where(low, 8, ABOVE) - taps // 2

    def across(index, carry):
        kind, tile = index // tiles, index % tiles
        for group in range(count // 8):
            base = start + 8 * group
            value = weights_ref[kind, 0] * along[kind, tile, pl.ds(base, 8)]
            for i in range(1, taps):
                value += weights_ref[kind, i] * along[kind, tile, pl.ds(base + i, 8)]
            fresh[kind, tile, 8 * group : 8 * group + 8] = value
        return carry

    lax.fori_loop(0, 2 * tiles, across, 0)

    def compute(trial, carry):
        for tile in range(tiles):
            columns = slice(tile * LANES, (tile + 1) * LANES)
            psi = part_ref[0, trial, :, columns] + fresh[0, tile]
            phi = part_ref[1, trial, :, columns] + fresh[1, tile]
            closing[trial, :, columns] = psi * lax.rsqrt(phi)
        closing_copy(trial).start()
        return carry

    lax.fori_loop(0, trials, compute, 0)

    def finish(trial, carry):
        large_copy(trial).wait()
        small_copy(trial).wait()
        closing_copy(trial).wait()
        return carry

    lax.fori_loop(0, trials, finish, 0)


def gather_kernel(
    vels, skies, taps_hbm, shifts_hbm, psi_ref, phi_ref,
    part_ref, ends_ref, bands_ref, weights_ref, done_ref,
    taps_ref, shifts_ref, blurred, raw, along, landing, top, bottom, band1, fresh,
    answers, small_sems, own_sem, trade_sems, recv_sem, right_sem, left_sem, pair_sends, pair_recv, top_sems, bottom_sems,
    first_sems, fresh_send, fresh_recv, ends_send, ends_recv,
):
    frames, share, width = psi_ref.shape
    trials = shifts_ref.shape[2]
    taps = taps_ref.shape[0]
    half = taps // 2
    chips = vels // 2
    tiles = width // LANES
    rows = vels * share
    blocks = rows // BLOCK
    per = blocks // chips
    steps = per * (chips - 1)
    sky = lax.axis_index("sky")
    vel = lax.axis_index("vel")
    chip = vel // 2
    core = vel % 2
    has_right = chip < chips - 1
    has_left = chip > 0
    has_next = sky < skies - 1
    has_prev = sky > 0
    low = chip < chips // 2
    partner = (sky, vel + 1 - 2 * core)

    taps_copy = pltpu.make_async_copy(taps_hbm, taps_ref, small_sems.at[0])
    shifts_copy = pltpu.make_async_copy(shifts_hbm, shifts_ref, small_sems.at[1])
    own_rows = pl.ds(pl.multiple_of(vel * share, 8), share)

    def own_copy(source):
        return pltpu.make_async_copy(source, raw.at[:, own_rows], own_sem)

    @pl.when(core == 0)
    def _():
        own_copy(psi_ref).start()

    @pl.when(core == 1)
    def _():
        own_copy(phi_ref).start()

    taps_copy.start()
    shifts_copy.start()
    left, right = (sky, vel - 2), (sky, vel + 2)
    before, after = (sky - 1, vel), (sky + 1, vel)
    skies_near = ((has_prev & (core == 1), before), (has_next & (core == 1), after))
    barrier = pltpu.get_barrier_semaphore()

    def greet(semaphore, device, present):
        @pl.when(present)
        def _():
            pl.semaphore_signal(semaphore, inc=1, device_id=device, device_id_type=MESH)

    greet(barrier, right, has_right)
    greet(barrier, partner, (core == 0) | (chip == 0))
    for present, device in skies_near:
        greet(barrier, device, present)
    callers = (has_left | (core == 0)).astype(jnp.int32) + core
    for present, device in skies_near:
        callers = callers + present.astype(jnp.int32)
    pl.semaphore_wait(barrier, callers)
    greet(answers.at[0], left, has_left)
    greet(answers.at[1], partner, core == 1)
    for present, device in skies_near:
        greet(answers.at[2], device, present)

    def trade_copy(source):
        return pltpu.make_async_remote_copy(
            src_ref=source,
            dst_ref=raw.at[:, own_rows],
            send_sem=trade_sems.at[0],
            recv_sem=trade_sems.at[1],
            device_id=partner,
            device_id_type=MESH,
        )

    def block_rows(block):
        return pl.ds(pl.multiple_of(block * BLOCK, 8), BLOCK)

    def line_copy(block, to_right, late, source=None):
        maps = pl.ds(1, frames - 1) if late else pl.ds(0, frames)
        place = raw.at[maps, block_rows(block)]
        return pltpu.make_async_remote_copy(
            src_ref=place if source is None else source[0].at[maps, block_rows(source[1])],
            dst_ref=place,
            send_sem=(right_sem if to_right else left_sem).at[block // per],
            recv_sem=recv_sem.at[block],
            device_id=(sky, vel + 2) if to_right else (sky, vel - 2),
            device_id_type=MESH,
        )

    def send_block(block, to_right, source=None):
        if to_right:
            late = (block < per) & (block > 1)
        else:
            late = (block >= blocks - per) & (block < blocks - 2)

        @pl.when(late)
        def _():
            line_copy(block, to_right, True, source).start()

        @pl.when(jnp.logical_not(late))
        def _():
            line_copy(block, to_right, False, source).start()

    most = BLOCK * (per - 3)
    rest = 3 * BLOCK

    def first_rows(to_right, piece):
        begin = HALO if to_right else BLOCK * per * (chips - 1)
        if piece == 0:
            return begin + (0 if to_right else BLOCK), most
        return begin + (most if to_right else 0), BLOCK

    def fresh_rows(to_right, piece):
        if piece == 0:
            return (0 if to_right else rest), most
        return (most if to_right else 0), rest

    def first_copy(to_right, piece):
        place = raw.at[0, pl.ds(*first_rows(to_right, piece))]
        return pltpu.make_async_remote_copy(
            src_ref=place,
            dst_ref=place,
            send_sem=right_sem.at[0] if to_right else left_sem.at[chips - 1],
            recv_sem=first_sems.at[1 if to_right else 0, piece],
            device_id=(sky, vel + 2) if to_right else (sky, vel - 2),
            device_id_type=MESH,
        )

    def fresh_copy(to_right, piece):
        place = fresh.at[core, :, pl.ds(*fresh_rows(to_right, piece))]
        return pltpu.make_async_remote_copy(
            src_ref=place,
            dst_ref=place,
            send_sem=fresh_send.at[piece],
            recv_sem=fresh_recv.at[piece],
            device_id=partner,
            device_id_type=MESH,
        )

    def halo_copy(to_next):
        source = raw.at[:, pl.ds(rows - HALO if to_next else 0, HALO)]
        sems = top_sems if to_next else bottom_sems
        return pltpu.make_async_remote_copy(
            src_ref=source,
            dst_ref=top if to_next else bottom,
            send_sem=sems.at[0],
            recv_sem=sems.at[1],
            device_id=(sky + 1, vel) if to_next else (sky - 1, vel),
            device_id_type=MESH,
        )

    def pair_copy(blur, late):
        skip = 1 if late else 0
        place = pl.ds(pl.multiple_of((blur + 1) * BLOCK, 8), BLOCK)
        return pltpu.make_async_remote_copy(
            src_ref=blurred.at[pl.ds(core * frames + skip, frames - skip), :, place],
            dst_ref=landing.at[blur + 1, pl.ds(skip, frames - skip)],
            send_sem=pair_sends.at[skip],
            recv_sem=pair_recv.at[blur + 1],
            device_id=partner,
            device_id_type=MESH,
        )

    def to_partner(blur, late):
        @pl.when(late)
        def _():
            pair_copy(blur, True).start()

        @pl.when(jnp.logical_not(late))
        def _():
            pair_copy(blur, False).start()

    def from_partner(blur, late):
        place = pl.ds(pl.multiple_of((blur + 1) * BLOCK, 8), BLOCK)

        @pl.when(late)
        def _():
            pair_copy(blur, True).wait_recv()

        @pl.when(jnp.logical_not(late))
        def _():
            pair_copy(blur, False).wait_recv()
            for tile in range(tiles):
                blurred[(1 - core) * frames, tile, place] = landing[blur + 1, 0, tile]

        for m in range(1, frames):
            for tile in range(tiles + 1):
                blurred[(1 - core) * frames + m, tile, place] = landing[blur + 1, m, tile]

    right_up = chip == 0
    left_up = chip < chips - 1

    def send_half(to_right, upward, part, source=None):
        def one(index, carry):
            place = jnp.where(upward, index, per // 2 - 1 - index)
            there = None if source is None else (source, place)
            send_block(chip * per + part * (per // 2) + place, to_right, there)
            return carry

        lax.fori_loop(0, per // 2, one, 0)

    def send_first(to_right, upward, ready):
        for kind, source in ((0, psi_ref), (1, phi_ref)):

            @pl.when(ready & (core == kind))
            def _(source=source):
                send_half(to_right, upward, core, source)

    right_ready = (chip > 0) | (core == 0)
    left_ready = (chip < chips - 1) | (core == 1)
    send_first(False, left_up, has_left & left_ready)

    @pl.when(core == 0)
    def _():
        pl.semaphore_wait(answers.at[1], 1)
        trade_copy(phi_ref).start()

    @pl.when(core == 1)
    def _():
        trade_copy(psi_ref).start()

    @pl.when(has_right)
    def _():
        pl.semaphore_wait(answers.at[0], 1)

    send_first(True, right_up, has_right & right_ready)
    own_copy(psi_ref).wait()
    taps_copy.wait()
    shifts_copy.wait()
    total = taps_ref[0]
    for i in range(1, taps):
        total = total + taps_ref[i]
    scale = 1.0 / jnp.full((8, LANES), total, jnp.float32)
    for i in range(taps):
        value = jnp.full((8, LANES), taps_ref[i], jnp.float32) * scale
        weights_ref[0, i] = value
        weights_ref[1, i] = value * value

    def build(band, kind, lead):
        depth = (3 - lead) * LANES
        place = lax.broadcasted_iota(jnp.int32, (depth, LANES), 0)
        place = place - lax.broadcasted_iota(jnp.int32, (depth, LANES), 1)
        spot = place - (LANES - SHIFT * lead - half)
        matrix = jnp.zeros((depth, LANES), jnp.float32)
        for i in range(taps):
            value = jnp.broadcast_to(weights_ref[kind, i][:1], (depth, LANES))
            matrix = jnp.where(spot == i, value, matrix)
        coarse = matrix.astype(jnp.bfloat16)
        band[:depth] = coarse
        band[depth : 2 * depth] = coarse
        band[2 * depth :] = (matrix - coarse.astype(jnp.float32)).astype(jnp.bfloat16)

    build(bands_ref.at[0], 0, 0)
    build(bands_ref.at[1], 1, 0)
    build(band1, core, 1)
    trade_copy(psi_ref).wait_recv()

    def send_rest(to_right, upward, present, ready):
        @pl.when(present)
        def _():
            send_half(to_right, upward, 1 - core)

        @pl.when(present & jnp.logical_not(ready))
        def _():
            send_half(to_right, upward, core)

    send_rest(False, left_up, has_left, left_ready)
    send_rest(True, right_up, has_right, right_ready)

    @pl.when(chip == chips - 1)
    def _():
        first_copy(False, 0).start()
        first_copy(False, 1).start()

    @pl.when(chip == 0)
    def _():
        first_copy(True, 0).start()
        first_copy(True, 1).start()

    @pl.when(core == 1)
    def _():
        pl.semaphore_wait(answers.at[2], has_prev.astype(jnp.int32) + has_next.astype(jnp.int32))
        pl.semaphore_signal(answers.at[3], inc=1, device_id=partner, device_id_type=MESH)

    @pl.when(core == 0)
    def _():
        pl.semaphore_wait(answers.at[3], 1)

    @pl.when(has_next & (chip == chips - 1))
    def _():
        halo_copy(True).start()

    @pl.when(has_prev & (chip == 0))
    def _():
        halo_copy(False).start()

    def blur_along(source, start, count, place, lead):
        if lead:
            values = source[1:frames, pl.ds(start, count)].reshape((frames - 1) * count, width)
            banded = blur_columns(values, band1[...], 1)
        else:
            values = source[0, pl.ds(start, count)]
            banded = blur_columns(values, bands_ref[core], 0)
        height = values.shape[0]
        for tile in range(tiles + lead):
            piece = banded[tile * height : (tile + 1) * height]
            if lead and tile in (0, tiles):
                lane = lax.broadcasted_iota(jnp.int32, (height, LANES), 1)
                piece = jnp.where(lane >= SHIFT if tile == 0 else lane < SHIFT, piece, 0.0)
            for m in range(height // count):
                along[lead + m, tile, pl.ds(place, count)] = piece[m * count : (m + 1) * count]

    def blur_block(block, late):
        start = pl.multiple_of(block * BLOCK, 8)
        place = pl.multiple_of(start + HALO, 8)
        blur_along(raw, start, BLOCK, place, 1)

        @pl.when(jnp.logical_not(late))
        def _():
            blur_along(raw, start, BLOCK, place, 0)

    def across(m, tile, start, target, place, count):
        factors = [weights_ref[core, i] for i in range(taps)]
        for group in range(count // 8):
            base = start + 8 * group
            value = factors[0] * along[m, tile, pl.ds(base, 8)]
            for i in range(1, taps):
                value += factors[i] * along[m, tile, pl.ds(base + i, 8)]
            target[pl.ds(pl.multiple_of(place + 8 * group, 8), 8)] = value

    def blur_across(blur, late):
        start = blur * BLOCK + HALO - 8 - half
        place = (blur + 1) * BLOCK

        def one_map(m, carry):
            for tile in range(tiles + 1):
                across(m, tile, start, blurred.at[core * frames + m, tile], place, BLOCK)
            return carry

        lax.fori_loop(jnp.asarray(late, jnp.int32), frames, one_map, 0)

    def first_arrives(to_right):
        region = ABOVE if to_right else BLOCK * per * (chips - 1) - ABOVE
        for piece in range(2):
            first_copy(to_right, piece).wait_recv()

            @pl.when(has_right if to_right else has_left)
            def _(piece=piece):
                first_copy(to_right, piece).start()

            start, count = first_rows(to_right, piece)
            blur_along(raw, start, count, start + HALO, 0)
            begin, height = fresh_rows(to_right, piece)

            def one_tile(tile, carry, begin=begin, height=height):
                target = fresh.at[core, tile]
                across(0, tile, region + begin + HALO - half, target, begin, height)
                return carry

            lax.fori_loop(0, tiles, one_tile, 0)
            fresh_copy(to_right, piece).start()

    def ends_rows(to_right, piece):
        origin = 0 if to_right else BLOCK * per * (chips - 1) - HALO
        if piece < 2:
            begin, count = first_rows(to_right, piece)
            return (begin, count), (begin - origin, count)
        begin = 0 if piece == 2 else BLOCK * per
        return (origin + begin, HALO), (begin, HALO)

    def ends_copy(to_right, piece):
        there, here = ends_rows(to_right, piece)
        return pltpu.make_async_remote_copy(
            src_ref=raw.at[0, pl.ds(*there)],
            dst_ref=ends_ref.at[core, pl.ds(*here)],
            send_sem=ends_send.at[piece],
            recv_sem=ends_recv.at[piece],
            device_id=partner,
            device_id_type=MESH,
        )

    def last_arrives(to_right):
        for piece in (2, 3, 0, 1):
            if piece < 2:
                first_copy(to_right, piece).wait_recv()

                @pl.when(has_right if to_right else has_left)
                def _(piece=piece):
                    first_copy(to_right, piece).start()

            ends_copy(to_right, piece).start()
            there, here = ends_rows(to_right, piece)
            ends_ref[core, pl.ds(*here)] = raw[0, pl.ds(*there)]

    def fresh_wait(to_right):
        for piece in range(2):
            fresh_copy(to_right, piece).wait_recv()

    def together(count):
        return max(JOIN // count, 1) if trials % 4 == 0 else 1

    def stack(first, count, unroll):
        def one_trial(trial, carry):
            stack_rows(shifts_ref, blurred, done_ref, trial, first, count, 0, False, unroll)
            return carry

        lax.fori_loop(0, trials, one_trial, 0, unroll=together(count))

    closing = last_row(chips, per, jnp.logical_not(low))
    other = last_row(chips, per, low)

    def stack_part(first, count, unroll):
        def one_trial(trial, carry):
            stack_rows(shifts_ref, blurred, part_ref, trial, first, count, closing, True, unroll)
            return carry

        lax.fori_loop(0, trials, one_trial, 0, unroll=together(count))


    def own_block(block, carry):
        blur_block(block, False)
        return carry

    def own_blur(blur, carry):
        blur_across(blur, False)
        pair_copy(blur, False).start()
        return carry

    def own_wait(blur, carry):
        from_partner(blur, False)
        return carry

    lax.fori_loop(chip * per, chip * per + per, own_block, 0)
    lax.fori_loop(chip * per + 1, chip * per + per, own_blur, 0)
    lax.fori_loop(chip * per + 1, chip * per + per, own_wait, 0)
    stack(pl.multiple_of((chip * per + 2) * BLOCK - 8, 8), BLOCK * (per - 3), 2)

    def stream(side, index):
        distance = index // per
        j = index % per
        origin = jnp.where(side == 1, chip + 1 + distance, chip - 1 - distance)
        present = (index >= 0) & (origin >= 0) & (origin < chips)
        edge = jnp.where(side == 1, origin == chips - 1, origin == 0)
        upward = (side == 1) != edge
        block = origin * per + jnp.where(upward, j, per - 1 - j)
        last = edge & (j == per - 1)
        return present, edge, upward, j, block, last

    def blurs(side, index, act):
        present, edge, upward, j, block, last = stream(side, index)
        count = jnp.where(present & jnp.logical_not(edge & (j == 0)), 1 + last.astype(jnp.int32), 0)
        begin = jnp.where(upward, block, block + 1)
        turn = jnp.where(upward, 1, -1)

        def one(k, carry):
            act(begin + turn * k)
            return carry

        lax.fori_loop(0, count, one, 0)

    def arrive(index):
        for side in (1, 0):
            present, edge, _, j, block, _ = stream(side, index)
            late = edge & (j > 1)

            @pl.when(present & late)
            def _(side=side, block=block):
                line_copy(block, True, True).wait_recv()

            @pl.when(present & jnp.logical_not(late))
            def _(side=side, block=block):
                line_copy(block, True, False).wait_recv()

            @pl.when(present & (has_left if side else has_right))
            def _(side=side, block=block):
                send_block(block, side == 0)

            @pl.when(present & edge & (j == 1) & (has_next if side else has_prev))
            def _(side=side):
                halo_copy(side == 1).start()

    def blur_side(index):
        def one_side(side, carry):
            present, edge, _, j, block, _ = stream(side, index)
            late = edge & (j > 1)

            @pl.when(present)
            def _():
                blur_block(block, late)

            def spread(blur):
                blur_across(blur, late)
                to_partner(blur, late)

            blurs(side, index, spread)
            return carry

        lax.fori_loop(0, 2, one_side, 0)

    def stack_side(index):
        def one_side(side, carry):
            present, edge, upward, j, block, last = stream(side, index)
            late = edge & (j > 1)
            blurs(side, index, lambda blur: from_partner(blur, late))
            begin = pl.multiple_of(jnp.where(upward, block - 1, block + 2) * BLOCK - 8, 8)
            closes = (side == 1) == low

            @pl.when(present & jnp.logical_not(edge))
            def _():
                stack(begin, BLOCK, True)

            @pl.when(present & edge & closes & jnp.logical_not(last) & (j > 2))
            def _():
                stack_part(begin, BLOCK, True)

            @pl.when(present & closes & last)
            def _():
                stack_part(pl.multiple_of((block - 1) * BLOCK - 8, 8), JOIN, True)

            return carry

        lax.fori_loop(0, 2, one_side, 0)

    limit = steps - 2
    mirror = chips - 1 - chip
    top_step = jnp.minimum(jnp.maximum(per * (mirror - 1) + 4, per * (chip - 1) + 2), limit)
    bottom_step = jnp.minimum(jnp.maximum(per * (chip - 1) + 4, per * (mirror - 1) + 2), limit)

    others = jnp.where(low, chip, mirror)
    other_step = jnp.where(others > 0, per * others + 2, -2)

    def step(index, carry):
        @pl.when(index < steps)
        def _():
            arrive(index)
            blur_side(index)

        @pl.when(index == top_step)
        def _():
            @pl.when(has_prev)
            def _():
                halo_copy(True).wait_recv()
                blur_along(top, 0, HALO, 0, 0)
                blur_along(top, 0, HALO, 0, 1)

            @pl.when(jnp.logical_not(has_prev))
            def _():
                for m in range(frames):
                    for tile in range(tiles + 1):
                        along[m, tile, pl.ds(0, HALO)] = jnp.zeros((HALO, LANES), jnp.float32)

            blur_across(-1, False)
            blur_across(0, False)

            @pl.when(jnp.logical_not(has_prev))
            def _():
                for m in range(frames):
                    for tile in range(tiles + 1):
                        blurred[core * frames + m, tile, pl.ds(0, ABOVE)] = jnp.zeros(
                            (ABOVE, LANES), jnp.float32
                        )

            pair_copy(-1, False).start()
            pair_copy(0, False).start()

        @pl.when(index == bottom_step)
        def _():
            @pl.when(has_next)
            def _():
                halo_copy(False).wait_recv()
                blur_along(bottom, 0, HALO, rows + HALO, 0)
                blur_along(bottom, 0, HALO, rows + HALO, 1)

            @pl.when(jnp.logical_not(has_next))
            def _():
                for m in range(frames):
                    for tile in range(tiles + 1):
                        along[m, tile, pl.ds(rows + HALO, HALO)] = jnp.zeros(
                            (HALO, LANES), jnp.float32
                        )

            blur_across(blocks, False)
            blur_across(blocks + 1, False)

            @pl.when(jnp.logical_not(has_next))
            def _():
                for m in range(frames):
                    for tile in range(tiles + 1):
                        blurred[core * frames + m, tile, pl.ds(rows + ABOVE, ABOVE)] = jnp.zeros(
                            (ABOVE, LANES), jnp.float32
                        )

            pair_copy(blocks, False).start()
            pair_copy(blocks + 1, False).start()

        @pl.when(index == other_step)
        def _():
            @pl.when(low)
            def _():
                first_arrives(True)

            @pl.when(jnp.logical_not(low))
            def _():
                first_arrives(False)

        stack_side(index - 1)

        @pl.when(index - 1 == other_step)
        def _():
            @pl.when(low)
            def _():
                fresh_wait(True)

            @pl.when(jnp.logical_not(low))
            def _():
                fresh_wait(False)

            behind = jnp.where(low, 0, BLOCK)
            count = BLOCK * (per - 1)
            place = pl.ds(pl.multiple_of(other + behind + ABOVE, 8), count)
            for kind in range(2):
                for tile in range(tiles):
                    there = pl.ds(pl.multiple_of(behind, 8), count)
                    blurred[kind * frames, tile, place] = fresh[kind, tile, there]
            stack(other, BLOCK * per, 4)

        @pl.when(index - 1 == top_step)
        def _():
            from_partner(-1, False)
            from_partner(0, False)
            stack(0, ABOVE, True)

        @pl.when(index - 1 == bottom_step)
        def _():
            from_partner(blocks, False)
            from_partner(blocks + 1, False)
            stack(rows - ABOVE, ABOVE, True)

        return carry

    lax.fori_loop(0, steps + 1, step, 0)

    def drain_sends():
        for sides in (1, 2):
            late = (per - 1) * sides
            whole = blurred.at[pl.ds(0, frames), :, pl.ds(0, (blocks + 3 - late) * BLOCK)]
            most = blurred.at[pl.ds(0, frames - 1), :, pl.ds(0, late * BLOCK)]

            @pl.when(has_left.astype(jnp.int32) + has_right.astype(jnp.int32) == sides)
            def _(whole=whole, most=most):
                pltpu.make_async_copy(whole, whole, pair_sends.at[0]).wait()
                pltpu.make_async_copy(most, most, pair_sends.at[1]).wait()

        trade_copy(psi_ref).wait_send()

        def drain(origin, carry):
            part = raw.at[:, pl.ds(pl.multiple_of(origin * (2 * share), 8), 2 * share)]

            @pl.when(has_right & (origin <= chip))
            def _():
                pltpu.make_async_copy(part, part, right_sem.at[origin]).wait()

            @pl.when(has_left & (origin >= chip))
            def _():
                pltpu.make_async_copy(part, part, left_sem.at[origin]).wait()

            return carry

        lax.fori_loop(0, chips, drain, 0)

        @pl.when((other_step > 0) & low)
        def _():
            for piece in range(2):
                fresh_copy(True, piece).wait_send()

        @pl.when((other_step > 0) & jnp.logical_not(low))
        def _():
            for piece in range(2):
                fresh_copy(False, piece).wait_send()

        @pl.when(has_next)
        def _():
            halo_copy(True).wait_send()

        @pl.when(has_prev)
        def _():
            halo_copy(False).wait_send()


    @pl.when(others == 0)
    def _():
        drain_sends()

    @pl.when(low)
    def _():
        last_arrives(False)

    @pl.when(jnp.logical_not(low))
    def _():
        last_arrives(True)

    @pl.when(others > 0)
    def _():
        drain_sends()

    for piece in range(4):
        ends_copy(False, piece).wait()


def per_device(vels, skies, psi_maps, phi_maps, psf_taps, shifts):
    frames, share, width = psi_maps.shape
    maps = 2 * frames
    tiles = width // LANES
    rows = share * vels
    trials = shifts.shape[0]
    blocks = rows // BLOCK
    taps = psf_taps.shape[0]
    shifts = pltpu.with_memory_space_constraint(jnp.transpose(shifts, (1, 2, 0)), pltpu.HBM)
    psf_taps = pltpu.with_memory_space_constraint(psf_taps, pltpu.HBM)
    psi_maps = pltpu.with_memory_space_constraint(psi_maps, pltpu.HBM)
    phi_maps = pltpu.with_memory_space_constraint(phi_maps, pltpu.HBM)
    dma = pltpu.SemaphoreType.DMA
    part, ends, bands, weights, done = pl.pallas_call(
        functools.partial(gather_kernel, vels, skies),
        out_shape=(
            jax.ShapeDtypeStruct((2, trials, 2 * share, width), jnp.float32),
            jax.ShapeDtypeStruct((2, 2 * share + HALO, width), jnp.float32),
            jax.ShapeDtypeStruct((2, 9 * LANES, LANES), jnp.bfloat16),
            jax.ShapeDtypeStruct((2, taps, 8, LANES), jnp.float32),
            jax.ShapeDtypeStruct((trials, rows, width), jnp.float32),
        ),
        in_specs=[
            pl.BlockSpec(memory_space=pl.ANY),
            pl.BlockSpec(memory_space=pl.ANY),
            pl.BlockSpec(memory_space=pl.ANY),
            pl.BlockSpec(memory_space=pl.ANY),
        ],
        out_specs=(pl.BlockSpec(memory_space=pltpu.VMEM),) * 5,
        scratch_shapes=[
            pltpu.SMEM((taps,), jnp.float32),
            pltpu.SMEM(shifts.shape, jnp.int32),
            pltpu.VMEM((maps, tiles + 1, rows + 2 * ABOVE, LANES), jnp.float32),
            pltpu.VMEM((frames, rows, width), jnp.float32),
            pltpu.VMEM((frames, tiles + 1, rows + 2 * HALO, LANES), jnp.float32),
            pltpu.VMEM((blocks + 3, frames, tiles + 1, BLOCK, LANES), jnp.float32),
            pltpu.VMEM((frames, HALO, width), jnp.float32),
            pltpu.VMEM((frames, HALO, width), jnp.float32),
            pltpu.VMEM((6 * LANES, LANES), jnp.bfloat16),
            pltpu.VMEM((2, tiles, 2 * share, LANES), jnp.float32),
            pltpu.SemaphoreType.REGULAR((4,)),
            dma((2,)),
            dma,
            dma((2,)),
            dma((blocks,)),
            dma((vels // 2,)),
            dma((vels // 2,)),
            dma((2,)),
            dma((blocks + 3,)),
            dma((2,)),
            dma((2,)),
            dma((2, 2)),
            dma((2,)),
            dma((2,)),
            dma((4,)),
            dma((4,)),
        ],
        compiler_params=pltpu.CompilerParams(
            collective_id=0, has_side_effects=True, vmem_limit_bytes=36 * 2**20
        ),
        name="gather",
    )(psf_taps, shifts, psi_maps, phi_maps)
    return pl.pallas_call(
        functools.partial(finish_kernel, vels),
        out_shape=jax.ShapeDtypeStruct((trials, rows, width), jnp.float32),
        in_specs=[pl.BlockSpec(memory_space=pltpu.VMEM)] * 5,
        out_specs=pl.BlockSpec(memory_space=pl.ANY),
        scratch_shapes=[
            pltpu.VMEM((2, tiles, 2 * share + HALO, LANES), jnp.float32),
            pltpu.VMEM((2, tiles, 2 * share, LANES), jnp.float32),
            pltpu.VMEM((trials, 2 * share, width), jnp.float32),
            dma((3, trials)),
        ],
        compiler_params=pltpu.CompilerParams(vmem_limit_bytes=12 * 2**20),
        name="finish",
    )(part, ends, bands, weights, done)


def solution(mesh):
    return jax.shard_map(
        functools.partial(per_device, mesh.shape["vel"], mesh.shape["sky"]),
        mesh=mesh,
        in_specs=(
            P(None, ("sky", "vel"), None),
            P(None, ("sky", "vel"), None),
            P(),
            P("vel", None, None),
        ),
        out_specs=P("vel", "sky", None),
        check_vma=False,
    )
```

```python
import functools
import jax
import jax.numpy as jnp
from jax import lax
from jax.experimental import pallas as pl
from jax.experimental.pallas import tpu as pltpu
from jax.sharding import PartitionSpec as P

SHIFT = 16
BLOCK = 16
HALO = 2 * BLOCK
ABOVE = BLOCK + 8
JOIN = 4 * BLOCK
LANES = 128
MESH = pl.DeviceIdType.MESH


def stack_rows(shifts_ref, maps_ref, out_ref, trial, first, count, skip, partial, unroll):
    frames = shifts_ref.shape[0]
    tiles = maps_ref.shape[1]
    lane = lax.broadcasted_iota(jnp.int32, (8, LANES), 1)
    down, turn, inside = [], [], []
    for frame in range(1, frames):
        offset = shifts_ref[frame, 1, trial] + SHIFT
        down.append(shifts_ref[frame, 0, trial] + ABOVE)
        turn.append(lax.rem(LANES - offset, LANES))
        inside.append(lane >= offset)

    def one_group(group, carry):
        base = first + group * 8

        def stacked(kind):
            total = [None] * (tiles - 1)
            if not partial:
                total = [
                    maps_ref[kind * frames, tile, pl.ds(pl.multiple_of(base + ABOVE, 8), 8)]
                    for tile in range(tiles - 1)
                ]
            for step in range(frames - 1):
                m = kind * frames + step + 1
                pieces = [maps_ref[m, tile, pl.ds(base + down[step], 8)] for tile in range(tiles)]
                for tile in range(tiles - 1):
                    joined = jnp.where(inside[step], pieces[tile], pieces[tile + 1])
                    moved = pltpu.roll(joined, turn[step], 1)
                    total[tile] = moved if total[tile] is None else total[tile] + moved
            return total

        psi = stacked(0)
        phi = stacked(1)
        rows = pl.ds(pl.multiple_of(base - skip, 8), 8)
        for tile in range(tiles - 1):
            columns = slice(tile * LANES, (tile + 1) * LANES)
            if partial:
                out_ref[0, trial, rows, columns] = psi[tile]
                out_ref[1, trial, rows, columns] = phi[tile]
            else:
                out_ref[trial, rows, columns] = psi[tile] * lax.rsqrt(phi[tile])
        return carry

    lax.fori_loop(0, count // 8, one_group, 0, unroll=unroll)


def last_row(chips, per, to_right):
    return pl.multiple_of(jnp.where(to_right, ABOVE, BLOCK * per * (chips - 1) - ABOVE), 8)


def blur_columns(values, band, lead):
    tiles = values.shape[1] // LANES
    coarse = values.astype(jnp.bfloat16)
    fine = (values - coarse.astype(jnp.float32)).astype(jnp.bfloat16)

    def windows(part):
        blank = jnp.zeros((part.shape[0], LANES), part.dtype)
        columns = [blank] + [part[:, t * LANES : (t + 1) * LANES] for t in range(tiles)] + [blank]
        wide = 3 - lead
        return jnp.concatenate(
            [jnp.concatenate(columns[t : t + wide], axis=1) for t in range(tiles + lead)], axis=0
        )

    high, rest = windows(coarse), windows(fine)
    return jnp.dot(
        jnp.concatenate([high, rest, high], axis=1), band, preferred_element_type=jnp.float32
    )


def finish_kernel(
    vels, part_ref, ends_ref, bands_ref, weights_ref, done_ref, out_ref, along, fresh, closing, sems
):
    trials, rows, width = done_ref.shape
    count = part_ref.shape[2]
    height = ends_ref.shape[1]
    taps = weights_ref.shape[1]
    tiles = width // LANES
    chips = vels // 2
    low = lax.axis_index("vel") // 2 < chips // 2
    first = last_row(chips, count // BLOCK, jnp.logical_not(low))
    small = ABOVE
    large = rows - count - small
    large_row = pl.multiple_of(jnp.where(low, 0, small + count), 8)
    small_row = pl.multiple_of(jnp.where(low, large + count, 0), 8)

    def large_copy(trial):
        part = pl.ds(large_row, large)
        return pltpu.make_async_copy(done_ref.at[trial, part], out_ref.at[trial, part], sems.at[0, trial])

    def small_copy(trial):
        part = pl.ds(small_row, small)
        return pltpu.make_async_copy(done_ref.at[trial, part], out_ref.at[trial, part], sems.at[1, trial])

    def closing_copy(trial):
        part = pl.ds(first, count)
        return pltpu.make_async_copy(closing.at[trial], out_ref.at[trial, part], sems.at[2, trial])

    def begin(trial, carry):
        large_copy(trial).start()
        small_copy(trial).start()
        return carry

    lax.fori_loop(0, trials, begin, 0)

    for kind in range(2):
        blurred = blur_columns(ends_ref[kind], bands_ref[kind], 0)
        for tile in range(tiles):
            along[kind, tile] = blurred[tile * height : (tile + 1) * height]
    start = jnp.where(low, 8, ABOVE) - taps // 2

    def across(index, carry):
        kind, tile = index // tiles, index % tiles
        for group in range(count // 8):
            base = start + 8 * group
            value = weights_ref[kind, 0] * along[kind, tile, pl.ds(base, 8)]
            for i in range(1, taps):
                value += weights_ref[kind, i] * along[kind, tile, pl.ds(base + i, 8)]
            fresh[kind, tile, 8 * group : 8 * group + 8] = value
        return carry

    lax.fori_loop(0, 2 * tiles, across, 0)

    def compute(trial, carry):
        for tile in range(tiles):
            columns = slice(tile * LANES, (tile + 1) * LANES)
            psi = part_ref[0, trial, :, columns] + fresh[0, tile]
            phi = part_ref[1, trial, :, columns] + fresh[1, tile]
            closing[trial, :, columns] = psi * lax.rsqrt(phi)
        closing_copy(trial).start()
        return carry

    lax.fori_loop(0, trials, compute, 0)

    def finish(trial, carry):
        large_copy(trial).wait()
        small_copy(trial).wait()
        closing_copy(trial).wait()
        return carry

    lax.fori_loop(0, trials, finish, 0)


def gather_kernel(
    vels, skies, taps_hbm, shifts_hbm, psi_ref, phi_ref,
    part_ref, ends_ref, bands_ref, weights_ref, done_ref,
    taps_ref, shifts_ref, blurred, raw, along, landing, top, bottom, band1, fresh,
    answers, small_sems, own_sem, trade_sems, recv_sem, right_sem, left_sem, pair_sends, pair_recv, top_sems, bottom_sems,
    first_sems, fresh_send, fresh_recv, ends_send, ends_recv,
):
    frames, share, width = psi_ref.shape
    trials = shifts_ref.shape[2]
    taps = taps_ref.shape[0]
    half = taps // 2
    chips = vels // 2
    tiles = width // LANES
    rows = vels * share
    blocks = rows // BLOCK
    per = blocks // chips
    steps = per * (chips - 1)
    sky = lax.axis_index("sky")
    vel = lax.axis_index("vel")
    chip = vel // 2
    core = vel % 2
    has_right = chip < chips - 1
    has_left = chip > 0
    has_next = sky < skies - 1
    has_prev = sky > 0
    low = chip < chips // 2
    partner = (sky, vel + 1 - 2 * core)

    taps_copy = pltpu.make_async_copy(taps_hbm, taps_ref, small_sems.at[0])
    shifts_copy = pltpu.make_async_copy(shifts_hbm, shifts_ref, small_sems.at[1])
    own_rows = pl.ds(pl.multiple_of(vel * share, 8), share)

    def own_copy(source):
        return pltpu.make_async_copy(source, raw.at[:, own_rows], own_sem)

    left, right = (sky, vel - 2), (sky, vel + 2)
    before, after = (sky - 1, vel), (sky + 1, vel)
    skies_near = ((has_prev & (core == 1), before), (has_next & (core == 1), after))
    barrier = pltpu.get_barrier_semaphore()

    def greet(semaphore, device, present):
        @pl.when(present)
        def _():
            pl.semaphore_signal(semaphore, inc=1, device_id=device, device_id_type=MESH)

    greet(barrier, right, has_right)
    greet(barrier, partner, (core == 0) | (chip == 0))
    for present, device in skies_near:
        greet(barrier, device, present)
    @pl.when(core == 0)
    def _():
        own_copy(psi_ref).start()

    @pl.when(core == 1)
    def _():
        own_copy(phi_ref).start()

    taps_copy.start()
    shifts_copy.start()
    callers = (has_left | (core == 0)).astype(jnp.int32) + core
    for present, device in skies_near:
        callers = callers + present.astype(jnp.int32)
    pl.semaphore_wait(barrier, callers)
    greet(answers.at[0], left, has_left)
    greet(answers.at[1], partner, core == 1)
    for present, device in skies_near:
        greet(answers.at[2], device, present)

    def trade_copy(source):
        return pltpu.make_async_remote_copy(
            src_ref=source,
            dst_ref=raw.at[:, own_rows],
            send_sem=trade_sems.at[0],
            recv_sem=trade_sems.at[1],
            device_id=partner,
            device_id_type=MESH,
        )

    def block_rows(block):
        return pl.ds(pl.multiple_of(block * BLOCK, 8), BLOCK)

    def line_copy(block, to_right, late, source=None):
        maps = pl.ds(1, frames - 1) if late else pl.ds(0, frames)
        place = raw.at[maps, block_rows(block)]
        return pltpu.make_async_remote_copy(
            src_ref=place if source is None else source[0].at[maps, block_rows(source[1])],
            dst_ref=place,
            send_sem=(right_sem if to_right else left_sem).at[block // per],
            recv_sem=recv_sem.at[block],
            device_id=(sky, vel + 2) if to_right else (sky, vel - 2),
            device_id_type=MESH,
        )

    def send_block(block, to_right, source=None):
        if to_right:
            late = (block < per) & (block > 1)
        else:
            late = (block >= blocks - per) & (block < blocks - 2)

        @pl.when(late)
        def _():
            line_copy(block, to_right, True, source).start()

        @pl.when(jnp.logical_not(late))
        def _():
            line_copy(block, to_right, False, source).start()

    most = BLOCK * (per - 3)
    rest = 3 * BLOCK

    def first_rows(to_right, piece):
        begin = HALO if to_right else BLOCK * per * (chips - 1)
        if piece == 0:
            return begin + (0 if to_right else BLOCK), most
        return begin + (most if to_right else 0), BLOCK

    def fresh_rows(to_right, piece):
        if piece == 0:
            return (0 if to_right else rest), most
        return (most if to_right else 0), rest

    def first_copy(to_right, piece):
        place = raw.at[0, pl.ds(*first_rows(to_right, piece))]
        return pltpu.make_async_remote_copy(
            src_ref=place,
            dst_ref=place,
            send_sem=right_sem.at[0] if to_right else left_sem.at[chips - 1],
            recv_sem=first_sems.at[1 if to_right else 0, piece],
            device_id=(sky, vel + 2) if to_right else (sky, vel - 2),
            device_id_type=MESH,
        )

    def fresh_copy(to_right, piece):
        place = fresh.at[core, :, pl.ds(*fresh_rows(to_right, piece))]
        return pltpu.make_async_remote_copy(
            src_ref=place,
            dst_ref=place,
            send_sem=fresh_send.at[piece],
            recv_sem=fresh_recv.at[piece],
            device_id=partner,
            device_id_type=MESH,
        )

    def halo_copy(to_next):
        source = raw.at[:, pl.ds(rows - HALO if to_next else 0, HALO)]
        sems = top_sems if to_next else bottom_sems
        return pltpu.make_async_remote_copy(
            src_ref=source,
            dst_ref=top if to_next else bottom,
            send_sem=sems.at[0],
            recv_sem=sems.at[1],
            device_id=(sky + 1, vel) if to_next else (sky - 1, vel),
            device_id_type=MESH,
        )

    def pair_copy(blur, late):
        skip = 1 if late else 0
        place = pl.ds(pl.multiple_of((blur + 1) * BLOCK, 8), BLOCK)
        return pltpu.make_async_remote_copy(
            src_ref=blurred.at[pl.ds(core * frames + skip, frames - skip), :, place],
            dst_ref=landing.at[blur + 1, pl.ds(skip, frames - skip)],
            send_sem=pair_sends.at[skip],
            recv_sem=pair_recv.at[blur + 1],
            device_id=partner,
            device_id_type=MESH,
        )

    def to_partner(blur, late):
        @pl.when(late)
        def _():
            pair_copy(blur, True).start()

        @pl.when(jnp.logical_not(late))
        def _():
            pair_copy(blur, False).start()

    def from_partner(blur, late):
        place = pl.ds(pl.multiple_of((blur + 1) * BLOCK, 8), BLOCK)

        @pl.when(late)
        def _():
            pair_copy(blur, True).wait_recv()

        @pl.when(jnp.logical_not(late))
        def _():
            pair_copy(blur, False).wait_recv()
            for tile in range(tiles):
                blurred[(1 - core) * frames, tile, place] = landing[blur + 1, 0, tile]

        for m in range(1, frames):
            for tile in range(tiles + 1):
                blurred[(1 - core) * frames + m, tile, place] = landing[blur + 1, m, tile]

    right_up = chip == 0
    left_up = chip < chips - 1

    def send_half(to_right, upward, part, source=None):
        def one(index, carry):
            place = jnp.where(upward, index, per // 2 - 1 - index)
            there = None if source is None else (source, place)
            send_block(chip * per + part * (per // 2) + place, to_right, there)
            return carry

        lax.fori_loop(0, per // 2, one, 0)

    def send_first(to_right, upward, ready):
        for kind, source in ((0, psi_ref), (1, phi_ref)):

            @pl.when(ready & (core == kind))
            def _(source=source):
                send_half(to_right, upward, core, source)

    right_ready = (chip > 0) | (core == 0)
    left_ready = (chip < chips - 1) | (core == 1)
    send_first(False, left_up, has_left & left_ready)

    @pl.when(core == 0)
    def _():
        pl.semaphore_wait(answers.at[1], 1)
        trade_copy(phi_ref).start()

    @pl.when(core == 1)
    def _():
        trade_copy(psi_ref).start()

    @pl.when(has_right)
    def _():
        pl.semaphore_wait(answers.at[0], 1)

    send_first(True, right_up, has_right & right_ready)
    own_copy(psi_ref).wait()
    taps_copy.wait()
    shifts_copy.wait()
    total = taps_ref[0]
    for i in range(1, taps):
        total = total + taps_ref[i]
    scale = 1.0 / jnp.full((8, LANES), total, jnp.float32)
    for i in range(taps):
        value = jnp.full((8, LANES), taps_ref[i], jnp.float32) * scale
        weights_ref[0, i] = value
        weights_ref[1, i] = value * value

    def build(band, kind, lead):
        depth = (3 - lead) * LANES
        place = lax.broadcasted_iota(jnp.int32, (depth, LANES), 0)
        place = place - lax.broadcasted_iota(jnp.int32, (depth, LANES), 1)
        spot = place - (LANES - SHIFT * lead - half)
        matrix = jnp.zeros((depth, LANES), jnp.float32)
        for i in range(taps):
            value = jnp.broadcast_to(weights_ref[kind, i][:1], (depth, LANES))
            matrix = jnp.where(spot == i, value, matrix)
        coarse = matrix.astype(jnp.bfloat16)
        band[:depth] = coarse
        band[depth : 2 * depth] = coarse
        band[2 * depth :] = (matrix - coarse.astype(jnp.float32)).astype(jnp.bfloat16)

    build(bands_ref.at[0], 0, 0)
    build(bands_ref.at[1], 1, 0)
    build(band1, core, 1)
    trade_copy(psi_ref).wait_recv()

    def send_rest(to_right, upward, present, ready):
        @pl.when(present)
        def _():
            send_half(to_right, upward, 1 - core)

        @pl.when(present & jnp.logical_not(ready))
        def _():
            send_half(to_right, upward, core)

    send_rest(False, left_up, has_left, left_ready)
    send_rest(True, right_up, has_right, right_ready)

    @pl.when(chip == chips - 1)
    def _():
        first_copy(False, 0).start()
        first_copy(False, 1).start()

    @pl.when(chip == 0)
    def _():
        first_copy(True, 0).start()
        first_copy(True, 1).start()

    @pl.when(core == 1)
    def _():
        pl.semaphore_wait(answers.at[2], has_prev.astype(jnp.int32) + has_next.astype(jnp.int32))
        pl.semaphore_signal(answers.at[3], inc=1, device_id=partner, device_id_type=MESH)

    @pl.when(core == 0)
    def _():
        pl.semaphore_wait(answers.at[3], 1)

    @pl.when(has_next & (chip == chips - 1))
    def _():
        halo_copy(True).start()

    @pl.when(has_prev & (chip == 0))
    def _():
        halo_copy(False).start()

    def blur_along(source, start, count, place, lead):
        if lead:
            values = source[1:frames, pl.ds(start, count)].reshape((frames - 1) * count, width)
            banded = blur_columns(values, band1[...], 1)
        else:
            values = source[0, pl.ds(start, count)]
            banded = blur_columns(values, bands_ref[core], 0)
        height = values.shape[0]
        for tile in range(tiles + lead):
            piece = banded[tile * height : (tile + 1) * height]
            if lead and tile in (0, tiles):
                lane = lax.broadcasted_iota(jnp.int32, (height, LANES), 1)
                piece = jnp.where(lane >= SHIFT if tile == 0 else lane < SHIFT, piece, 0.0)
            for m in range(height // count):
                along[lead + m, tile, pl.ds(place, count)] = piece[m * count : (m + 1) * count]

    def blur_block(block, late):
        start = pl.multiple_of(block * BLOCK, 8)
        place = pl.multiple_of(start + HALO, 8)
        blur_along(raw, start, BLOCK, place, 1)

        @pl.when(jnp.logical_not(late))
        def _():
            blur_along(raw, start, BLOCK, place, 0)

    def across(m, tile, start, target, place, count):
        factors = [weights_ref[core, i] for i in range(taps)]
        for group in range(count // 8):
            base = start + 8 * group
            value = factors[0] * along[m, tile, pl.ds(base, 8)]
            for i in range(1, taps):
                value += factors[i] * along[m, tile, pl.ds(base + i, 8)]
            target[pl.ds(pl.multiple_of(place + 8 * group, 8), 8)] = value

    def blur_across(blur, late):
        start = blur * BLOCK + HALO - 8 - half
        place = (blur + 1) * BLOCK

        def one_map(m, carry):
            for tile in range(tiles + 1):
                across(m, tile, start, blurred.at[core * frames + m, tile], place, BLOCK)
            return carry

        lax.fori_loop(jnp.asarray(late, jnp.int32), frames, one_map, 0)

    def first_arrives(to_right):
        region = ABOVE if to_right else BLOCK * per * (chips - 1) - ABOVE
        for piece in range(2):
            first_copy(to_right, piece).wait_recv()

            @pl.when(has_right if to_right else has_left)
            def _(piece=piece):
                first_copy(to_right, piece).start()

            start, count = first_rows(to_right, piece)
            blur_along(raw, start, count, start + HALO, 0)
            begin, height = fresh_rows(to_right, piece)

            def one_tile(tile, carry, begin=begin, height=height):
                target = fresh.at[core, tile]
                across(0, tile, region + begin + HALO - half, target, begin, height)
                return carry

            lax.fori_loop(0, tiles, one_tile, 0)
            fresh_copy(to_right, piece).start()

    def ends_rows(to_right, piece):
        origin = 0 if to_right else BLOCK * per * (chips - 1) - HALO
        if piece < 2:
            begin, count = first_rows(to_right, piece)
            return (begin, count), (begin - origin, count)
        begin = 0 if piece == 2 else BLOCK * per
        return (origin + begin, HALO), (begin, HALO)

    def ends_copy(to_right, piece):
        there, here = ends_rows(to_right, piece)
        return pltpu.make_async_remote_copy(
            src_ref=raw.at[0, pl.ds(*there)],
            dst_ref=ends_ref.at[core, pl.ds(*here)],
            send_sem=ends_send.at[piece],
            recv_sem=ends_recv.at[piece],
            device_id=partner,
            device_id_type=MESH,
        )

    def ends_begin(to_right, piece):
        ends_copy(to_right, piece).start()
        there, here = ends_rows(to_right, piece)
        ends_ref[core, pl.ds(*here)] = raw[0, pl.ds(*there)]

    def last_arrives(to_right):
        ends_copy(to_right, 2).wait()
        ends_copy(to_right, 3).wait()
        for piece in range(2):
            first_copy(to_right, piece).wait_recv()

            @pl.when(has_right if to_right else has_left)
            def _(piece=piece):
                first_copy(to_right, piece).start()

            ends_begin(to_right, piece)

    def fresh_wait(to_right):
        for piece in range(2):
            fresh_copy(to_right, piece).wait_recv()

    def together(count):
        if trials % 4:
            return 1
        return 2 if count == JOIN else max(JOIN // count, 1)

    def stack(first, count, unroll):
        def one_trial(trial, carry):
            stack_rows(shifts_ref, blurred, done_ref, trial, first, count, 0, False, unroll)
            return carry

        lax.fori_loop(0, trials, one_trial, 0, unroll=together(count))

    closing = last_row(chips, per, jnp.logical_not(low))
    other = last_row(chips, per, low)

    def stack_part(first, count, unroll):
        def one_trial(trial, carry):
            stack_rows(shifts_ref, blurred, part_ref, trial, first, count, closing, True, unroll)
            return carry

        lax.fori_loop(0, trials, one_trial, 0, unroll=together(count))


    def own_block(block, carry):
        blur_block(block, False)
        return carry

    def own_blur(blur, carry):
        blur_across(blur, False)
        pair_copy(blur, False).start()
        return carry

    def own_wait(blur, carry):
        from_partner(blur, False)
        return carry

    lax.fori_loop(chip * per, chip * per + per, own_block, 0)
    lax.fori_loop(chip * per + 1, chip * per + per, own_blur, 0)
    lax.fori_loop(chip * per + 1, chip * per + per, own_wait, 0)
    stack(pl.multiple_of((chip * per + 2) * BLOCK - 8, 8), BLOCK * (per - 3), 2)

    def stream(side, index):
        distance = index // per
        j = index % per
        origin = jnp.where(side == 1, chip + 1 + distance, chip - 1 - distance)
        present = (index >= 0) & (origin >= 0) & (origin < chips)
        edge = jnp.where(side == 1, origin == chips - 1, origin == 0)
        upward = (side == 1) != edge
        block = origin * per + jnp.where(upward, j, per - 1 - j)
        last = edge & (j == per - 1)
        return present, edge, upward, j, block, last

    def blurs(side, index, act):
        present, edge, upward, j, block, last = stream(side, index)
        count = jnp.where(present & jnp.logical_not(edge & (j == 0)), 1 + last.astype(jnp.int32), 0)
        begin = jnp.where(upward, block, block + 1)
        turn = jnp.where(upward, 1, -1)

        def one(k, carry):
            act(begin + turn * k)
            return carry

        lax.fori_loop(0, count, one, 0)

    def arrive(index):
        for side in (1, 0):
            present, edge, _, j, block, _ = stream(side, index)
            late = edge & (j > 1)

            @pl.when(present & late)
            def _(side=side, block=block):
                line_copy(block, True, True).wait_recv()

            @pl.when(present & jnp.logical_not(late))
            def _(side=side, block=block):
                line_copy(block, True, False).wait_recv()

            @pl.when(present & (has_left if side else has_right))
            def _(side=side, block=block):
                send_block(block, side == 0)

            @pl.when(present & edge & (j == 1) & (has_next if side else has_prev))
            def _(side=side):
                halo_copy(side == 1).start()

    def blur_side(index):
        def one_side(side, carry):
            present, edge, _, j, block, _ = stream(side, index)
            late = edge & (j > 1)

            @pl.when(present)
            def _():
                blur_block(block, late)

            def spread(blur):
                blur_across(blur, late)
                to_partner(blur, late)

            blurs(side, index, spread)
            return carry

        lax.fori_loop(0, 2, one_side, 0)

    def stack_side(index):
        def one_side(side, carry):
            present, edge, upward, j, block, last = stream(side, index)
            late = edge & (j > 1)
            blurs(side, index, lambda blur: from_partner(blur, late))
            begin = pl.multiple_of(jnp.where(upward, block - 1, block + 2) * BLOCK - 8, 8)
            closes = (side == 1) == low

            @pl.when(present & jnp.logical_not(edge))
            def _():
                stack(begin, BLOCK, True)

            @pl.when(present & edge & closes & jnp.logical_not(last) & (j > 2))
            def _():
                stack_part(begin, BLOCK, True)

            @pl.when(present & closes & last)
            def _():
                stack_part(pl.multiple_of((block - 1) * BLOCK - 8, 8), JOIN, True)

            return carry

        lax.fori_loop(0, 2, one_side, 0)

    limit = steps - 2
    mirror = chips - 1 - chip
    top_step = jnp.minimum(jnp.maximum(per * (mirror - 1) + 4, per * (chip - 1) + 2), limit)
    bottom_step = jnp.minimum(jnp.maximum(per * (chip - 1) + 4, per * (mirror - 1) + 2), limit)

    others = jnp.where(low, chip, mirror)
    other_step = jnp.where(others > 0, per * others + 2, -2)

    def step(index, carry):
        @pl.when(index < steps)
        def _():
            arrive(index)
            blur_side(index)

        @pl.when(index == top_step)
        def _():
            @pl.when(has_prev)
            def _():
                halo_copy(True).wait_recv()
                blur_along(top, 0, HALO, 0, 0)
                blur_along(top, 0, HALO, 0, 1)

            @pl.when(jnp.logical_not(has_prev))
            def _():
                for m in range(frames):
                    for tile in range(tiles + 1):
                        along[m, tile, pl.ds(0, HALO)] = jnp.zeros((HALO, LANES), jnp.float32)

            blur_across(-1, False)
            blur_across(0, False)

            @pl.when(jnp.logical_not(has_prev))
            def _():
                for m in range(frames):
                    for tile in range(tiles + 1):
                        blurred[core * frames + m, tile, pl.ds(0, ABOVE)] = jnp.zeros(
                            (ABOVE, LANES), jnp.float32
                        )

            pair_copy(-1, False).start()
            pair_copy(0, False).start()

        @pl.when(index == bottom_step)
        def _():
            @pl.when(has_next)
            def _():
                halo_copy(False).wait_recv()
                blur_along(bottom, 0, HALO, rows + HALO, 0)
                blur_along(bottom, 0, HALO, rows + HALO, 1)

            @pl.when(jnp.logical_not(has_next))
            def _():
                for m in range(frames):
                    for tile in range(tiles + 1):
                        along[m, tile, pl.ds(rows + HALO, HALO)] = jnp.zeros(
                            (HALO, LANES), jnp.float32
                        )

            blur_across(blocks, False)
            blur_across(blocks + 1, False)

            @pl.when(jnp.logical_not(has_next))
            def _():
                for m in range(frames):
                    for tile in range(tiles + 1):
                        blurred[core * frames + m, tile, pl.ds(rows + ABOVE, ABOVE)] = jnp.zeros(
                            (ABOVE, LANES), jnp.float32
                        )

            pair_copy(blocks, False).start()
            pair_copy(blocks + 1, False).start()

        @pl.when((index == steps - 1) & low)
        def _():
            ends_begin(False, 2)
            ends_begin(False, 3)

        @pl.when((index == steps - 1) & jnp.logical_not(low))
        def _():
            ends_begin(True, 2)
            ends_begin(True, 3)

        @pl.when(index == other_step)
        def _():
            @pl.when(low)
            def _():
                first_arrives(True)

            @pl.when(jnp.logical_not(low))
            def _():
                first_arrives(False)

        stack_side(index - 1)

        @pl.when(index - 1 == other_step)
        def _():
            @pl.when(low)
            def _():
                fresh_wait(True)

            @pl.when(jnp.logical_not(low))
            def _():
                fresh_wait(False)

            behind = jnp.where(low, 0, BLOCK)
            count = BLOCK * (per - 1)
            place = pl.ds(pl.multiple_of(other + behind + ABOVE, 8), count)
            for kind in range(2):
                for tile in range(tiles):
                    there = pl.ds(pl.multiple_of(behind, 8), count)
                    blurred[kind * frames, tile, place] = fresh[kind, tile, there]
            stack(other, BLOCK * per, 4)

        @pl.when(index - 1 == top_step)
        def _():
            from_partner(-1, False)
            from_partner(0, False)
            stack(0, ABOVE, True)

        @pl.when(index - 1 == bottom_step)
        def _():
            from_partner(blocks, False)
            from_partner(blocks + 1, False)
            stack(rows - ABOVE, ABOVE, True)

        return carry

    lax.fori_loop(0, steps + 1, step, 0)

    def drain_sends():
        for sides in (1, 2):
            late = (per - 1) * sides
            whole = blurred.at[pl.ds(0, frames), :, pl.ds(0, (blocks + 3 - late) * BLOCK)]
            most = blurred.at[pl.ds(0, frames - 1), :, pl.ds(0, late * BLOCK)]

            @pl.when(has_left.astype(jnp.int32) + has_right.astype(jnp.int32) == sides)
            def _(whole=whole, most=most):
                pltpu.make_async_copy(whole, whole, pair_sends.at[0]).wait()
                pltpu.make_async_copy(most, most, pair_sends.at[1]).wait()

        trade_copy(psi_ref).wait_send()

        def drain(origin, carry):
            part = raw.at[:, pl.ds(pl.multiple_of(origin * (2 * share), 8), 2 * share)]

            @pl.when(has_right & (origin <= chip))
            def _():
                pltpu.make_async_copy(part, part, right_sem.at[origin]).wait()

            @pl.when(has_left & (origin >= chip))
            def _():
                pltpu.make_async_copy(part, part, left_sem.at[origin]).wait()

            return carry

        lax.fori_loop(0, chips, drain, 0)

        @pl.when((other_step > 0) & low)
        def _():
            for piece in range(2):
                fresh_copy(True, piece).wait_send()

        @pl.when((other_step > 0) & jnp.logical_not(low))
        def _():
            for piece in range(2):
                fresh_copy(False, piece).wait_send()

        @pl.when(has_next)
        def _():
            halo_copy(True).wait_send()

        @pl.when(has_prev)
        def _():
            halo_copy(False).wait_send()


    @pl.when(others == 0)
    def _():
        drain_sends()

    @pl.when(low)
    def _():
        last_arrives(False)

    @pl.when(jnp.logical_not(low))
    def _():
        last_arrives(True)

    @pl.when(others > 0)
    def _():
        drain_sends()

    for piece in range(2):
        ends_copy(False, piece).wait()


def per_device(vels, skies, psi_maps, phi_maps, psf_taps, shifts):
    frames, share, width = psi_maps.shape
    maps = 2 * frames
    tiles = width // LANES
    rows = share * vels
    trials = shifts.shape[0]
    blocks = rows // BLOCK
    taps = psf_taps.shape[0]
    shifts = pltpu.with_memory_space_constraint(jnp.transpose(shifts, (1, 2, 0)), pltpu.HBM)
    psf_taps = pltpu.with_memory_space_constraint(psf_taps, pltpu.HBM)
    psi_maps = pltpu.with_memory_space_constraint(psi_maps, pltpu.HBM)
    phi_maps = pltpu.with_memory_space_constraint(phi_maps, pltpu.HBM)
    dma = pltpu.SemaphoreType.DMA
    part, ends, bands, weights, done = pl.pallas_call(
        functools.partial(gather_kernel, vels, skies),
        out_shape=(
            jax.ShapeDtypeStruct((2, trials, 2 * share, width), jnp.float32),
            jax.ShapeDtypeStruct((2, 2 * share + HALO, width), jnp.float32),
            jax.ShapeDtypeStruct((2, 9 * LANES, LANES), jnp.bfloat16),
            jax.ShapeDtypeStruct((2, taps, 8, LANES), jnp.float32),
            jax.ShapeDtypeStruct((trials, rows, width), jnp.float32),
        ),
        in_specs=[
            pl.BlockSpec(memory_space=pl.ANY),
            pl.BlockSpec(memory_space=pl.ANY),
            pl.BlockSpec(memory_space=pl.ANY),
            pl.BlockSpec(memory_space=pl.ANY),
        ],
        out_specs=(pl.BlockSpec(memory_space=pltpu.VMEM),) * 5,
        scratch_shapes=[
            pltpu.SMEM((taps,), jnp.float32),
            pltpu.SMEM(shifts.shape, jnp.int32),
            pltpu.VMEM((maps, tiles + 1, rows + 2 * ABOVE, LANES), jnp.float32),
            pltpu.VMEM((frames, rows, width), jnp.float32),
            pltpu.VMEM((frames, tiles + 1, rows + 2 * HALO, LANES), jnp.float32),
            pltpu.VMEM((blocks + 3, frames, tiles + 1, BLOCK, LANES), jnp.float32),
            pltpu.VMEM((frames, HALO, width), jnp.float32),
            pltpu.VMEM((frames, HALO, width), jnp.float32),
            pltpu.VMEM((6 * LANES, LANES), jnp.bfloat16),
            pltpu.VMEM((2, tiles, 2 * share, LANES), jnp.float32),
            pltpu.SemaphoreType.REGULAR((4,)),
            dma((2,)),
            dma,
            dma((2,)),
            dma((blocks,)),
            dma((vels // 2,)),
            dma((vels // 2,)),
            dma((2,)),
            dma((blocks + 3,)),
            dma((2,)),
            dma((2,)),
            dma((2, 2)),
            dma((2,)),
            dma((2,)),
            dma((4,)),
            dma((4,)),
        ],
        compiler_params=pltpu.CompilerParams(
            collective_id=0, has_side_effects=True, vmem_limit_bytes=36 * 2**20
        ),
        name="gather",
    )(psf_taps, shifts, psi_maps, phi_maps)
    return pl.pallas_call(
        functools.partial(finish_kernel, vels),
        out_shape=jax.ShapeDtypeStruct((trials, rows, width), jnp.float32),
        in_specs=[pl.BlockSpec(memory_space=pltpu.VMEM)] * 5,
        out_specs=pl.BlockSpec(memory_space=pl.ANY),
        scratch_shapes=[
            pltpu.VMEM((2, tiles, 2 * share + HALO, LANES), jnp.float32),
            pltpu.VMEM((2, tiles, 2 * share, LANES), jnp.float32),
            pltpu.VMEM((trials, 2 * share, width), jnp.float32),
            dma((3, trials)),
        ],
        compiler_params=pltpu.CompilerParams(vmem_limit_bytes=12 * 2**20),
        name="finish",
    )(part, ends, bands, weights, done)


def solution(mesh):
    return jax.shard_map(
        functools.partial(per_device, mesh.shape["vel"], mesh.shape["sky"]),
        mesh=mesh,
        in_specs=(
            P(None, ("sky", "vel"), None),
            P(None, ("sky", "vel"), None),
            P(),
            P("vel", None, None),
        ),
        out_specs=P("vel", "sky", None),
        check_vma=False,
    )
```

```python
import functools
import jax
import jax.numpy as jnp
from jax import lax
from jax.experimental import pallas as pl
from jax.experimental.pallas import tpu as pltpu
from jax.sharding import PartitionSpec as P

SHIFT = 16
BLOCK = 16
HALO = 2 * BLOCK
ABOVE = BLOCK + 8
JOIN = 4 * BLOCK
LANES = 128
MESH = pl.DeviceIdType.MESH


def stack_rows(shifts_ref, maps_ref, out_ref, trial, first, count, skip, partial, unroll):
    frames = shifts_ref.shape[0]
    tiles = maps_ref.shape[1]
    lane = lax.broadcasted_iota(jnp.int32, (8, LANES), 1)
    down, turn, inside = [], [], []
    for frame in range(1, frames):
        offset = shifts_ref[frame, 1, trial] + SHIFT
        down.append(shifts_ref[frame, 0, trial] + ABOVE)
        turn.append(lax.rem(LANES - offset, LANES))
        inside.append(lane >= offset)

    def one_group(group, carry):
        base = first + group * 8

        def stacked(kind):
            total = [None] * (tiles - 1)
            if not partial:
                total = [
                    maps_ref[kind * frames, tile, pl.ds(pl.multiple_of(base + ABOVE, 8), 8)]
                    for tile in range(tiles - 1)
                ]
            for step in range(frames - 1):
                m = kind * frames + step + 1
                pieces = [maps_ref[m, tile, pl.ds(base + down[step], 8)] for tile in range(tiles)]
                for tile in range(tiles - 1):
                    joined = jnp.where(inside[step], pieces[tile], pieces[tile + 1])
                    moved = pltpu.roll(joined, turn[step], 1)
                    total[tile] = moved if total[tile] is None else total[tile] + moved
            return total

        psi = stacked(0)
        phi = stacked(1)
        rows = pl.ds(pl.multiple_of(base - skip, 8), 8)
        for tile in range(tiles - 1):
            columns = slice(tile * LANES, (tile + 1) * LANES)
            if partial:
                out_ref[0, trial, rows, columns] = psi[tile]
                out_ref[1, trial, rows, columns] = phi[tile]
            else:
                out_ref[trial, rows, columns] = psi[tile] * lax.rsqrt(phi[tile])
        return carry

    lax.fori_loop(0, count // 8, one_group, 0, unroll=unroll)


def last_row(chips, per, to_right):
    return pl.multiple_of(jnp.where(to_right, ABOVE, BLOCK * per * (chips - 1) - ABOVE), 8)


def blur_columns(values, band, lead):
    tiles = values.shape[1] // LANES
    coarse = values.astype(jnp.bfloat16)
    fine = (values - coarse.astype(jnp.float32)).astype(jnp.bfloat16)

    def windows(part):
        blank = jnp.zeros((part.shape[0], LANES), part.dtype)
        columns = [blank] + [part[:, t * LANES : (t + 1) * LANES] for t in range(tiles)] + [blank]
        wide = 3 - lead
        return jnp.concatenate(
            [jnp.concatenate(columns[t : t + wide], axis=1) for t in range(tiles + lead)], axis=0
        )

    high, rest = windows(coarse), windows(fine)
    return jnp.dot(
        jnp.concatenate([high, rest, high], axis=1), band, preferred_element_type=jnp.float32
    )


def finish_kernel(
    vels, part_ref, ends_ref, bands_ref, weights_ref, done_ref, out_ref, along, fresh, closing, sems
):
    trials, rows, width = done_ref.shape
    count = part_ref.shape[2]
    height = ends_ref.shape[1]
    taps = weights_ref.shape[1]
    tiles = width // LANES
    chips = vels // 2
    low = lax.axis_index("vel") // 2 < chips // 2
    first = last_row(chips, count // BLOCK, jnp.logical_not(low))
    small = ABOVE
    large = rows - count - small
    large_row = pl.multiple_of(jnp.where(low, 0, small + count), 8)
    small_row = pl.multiple_of(jnp.where(low, large + count, 0), 8)

    def large_copy(trial):
        part = pl.ds(large_row, large)
        return pltpu.make_async_copy(done_ref.at[trial, part], out_ref.at[trial, part], sems.at[0, trial])

    def small_copy(trial):
        part = pl.ds(small_row, small)
        return pltpu.make_async_copy(done_ref.at[trial, part], out_ref.at[trial, part], sems.at[1, trial])

    def closing_copy(trial):
        part = pl.ds(first, count)
        return pltpu.make_async_copy(closing.at[trial], out_ref.at[trial, part], sems.at[2, trial])

    def begin(trial, carry):
        large_copy(trial).start()
        small_copy(trial).start()
        return carry

    lax.fori_loop(0, trials, begin, 0)

    for kind in range(2):
        blurred = blur_columns(ends_ref[kind], bands_ref[kind], 0)
        for tile in range(tiles):
            along[kind, tile] = blurred[tile * height : (tile + 1) * height]
    start = jnp.where(low, 8, ABOVE) - taps // 2

    def across(index, carry):
        kind, tile = index // tiles, index % tiles
        for group in range(count // 8):
            base = start + 8 * group
            value = weights_ref[kind, 0] * along[kind, tile, pl.ds(base, 8)]
            for i in range(1, taps):
                value += weights_ref[kind, i] * along[kind, tile, pl.ds(base + i, 8)]
            fresh[kind, tile, 8 * group : 8 * group + 8] = value
        return carry

    lax.fori_loop(0, 2 * tiles, across, 0)

    def compute(trial, carry):
        for tile in range(tiles):
            columns = slice(tile * LANES, (tile + 1) * LANES)
            psi = part_ref[0, trial, :, columns] + fresh[0, tile]
            phi = part_ref[1, trial, :, columns] + fresh[1, tile]
            closing[trial, :, columns] = psi * lax.rsqrt(phi)
        closing_copy(trial).start()
        return carry

    lax.fori_loop(0, trials, compute, 0)

    def finish(trial, carry):
        large_copy(trial).wait()
        small_copy(trial).wait()
        closing_copy(trial).wait()
        return carry

    lax.fori_loop(0, trials, finish, 0)


def gather_kernel(
    vels, skies, taps_hbm, shifts_hbm, psi_ref, phi_ref,
    part_ref, ends_ref, bands_ref, weights_ref, done_ref,
    taps_ref, shifts_ref, blurred, raw, along, landing, top, bottom, band1, fresh,
    answers, small_sems, own_sem, trade_sems, recv_sem, right_sem, left_sem, pair_sends, pair_recv, top_sems, bottom_sems,
    first_sems, fresh_send, fresh_recv, ends_send, ends_recv,
):
    frames, share, width = psi_ref.shape
    trials = shifts_ref.shape[2]
    taps = taps_ref.shape[0]
    half = taps // 2
    chips = vels // 2
    tiles = width // LANES
    rows = vels * share
    blocks = rows // BLOCK
    per = blocks // chips
    steps = per * (chips - 1)
    sky = lax.axis_index("sky")
    vel = lax.axis_index("vel")
    chip = vel // 2
    core = vel % 2
    has_right = chip < chips - 1
    has_left = chip > 0
    has_next = sky < skies - 1
    has_prev = sky > 0
    low = chip < chips // 2
    partner = (sky, vel + 1 - 2 * core)

    taps_copy = pltpu.make_async_copy(taps_hbm, taps_ref, small_sems.at[0])
    shifts_copy = pltpu.make_async_copy(shifts_hbm, shifts_ref, small_sems.at[1])
    own_rows = pl.ds(pl.multiple_of(vel * share, 8), share)

    def own_copy(source):
        return pltpu.make_async_copy(source, raw.at[:, own_rows], own_sem)

    left, right = (sky, vel - 2), (sky, vel + 2)
    before, after = (sky - 1, vel), (sky + 1, vel)
    skies_near = ((has_prev & (core == 1), before), (has_next & (core == 1), after))
    barrier = pltpu.get_barrier_semaphore()

    def greet(semaphore, device, present):
        @pl.when(present)
        def _():
            pl.semaphore_signal(semaphore, inc=1, device_id=device, device_id_type=MESH)

    greet(barrier, right, has_right)
    greet(barrier, partner, (core == 0) | (chip == 0))
    for present, device in skies_near:
        greet(barrier, device, present)
    @pl.when(core == 0)
    def _():
        own_copy(psi_ref).start()

    @pl.when(core == 1)
    def _():
        own_copy(phi_ref).start()

    taps_copy.start()
    shifts_copy.start()
    callers = (has_left | (core == 0)).astype(jnp.int32) + core
    for present, device in skies_near:
        callers = callers + present.astype(jnp.int32)
    pl.semaphore_wait(barrier, callers)
    greet(answers.at[0], left, has_left)
    greet(answers.at[1], partner, core == 1)
    for present, device in skies_near:
        greet(answers.at[2], device, present)

    def trade_copy(source):
        return pltpu.make_async_remote_copy(
            src_ref=source,
            dst_ref=raw.at[:, own_rows],
            send_sem=trade_sems.at[0],
            recv_sem=trade_sems.at[1],
            device_id=partner,
            device_id_type=MESH,
        )

    def block_rows(block):
        return pl.ds(pl.multiple_of(block * BLOCK, 8), BLOCK)

    def line_copy(block, to_right, late, source=None):
        maps = pl.ds(1, frames - 1) if late else pl.ds(0, frames)
        place = raw.at[maps, block_rows(block)]
        return pltpu.make_async_remote_copy(
            src_ref=place if source is None else source[0].at[maps, block_rows(source[1])],
            dst_ref=place,
            send_sem=(right_sem if to_right else left_sem).at[block // per],
            recv_sem=recv_sem.at[block],
            device_id=(sky, vel + 2) if to_right else (sky, vel - 2),
            device_id_type=MESH,
        )

    def send_block(block, to_right, source=None):
        if to_right:
            late = (block < per) & (block > 1)
        else:
            late = (block >= blocks - per) & (block < blocks - 2)

        @pl.when(late)
        def _():
            line_copy(block, to_right, True, source).start()

        @pl.when(jnp.logical_not(late))
        def _():
            line_copy(block, to_right, False, source).start()

    most = BLOCK * (per - 3)
    rest = 3 * BLOCK

    def first_rows(to_right, piece):
        begin = HALO if to_right else BLOCK * per * (chips - 1)
        if piece == 0:
            return begin + (0 if to_right else BLOCK), most
        return begin + (most if to_right else 0), BLOCK

    def fresh_rows(to_right, piece):
        if piece == 0:
            return (0 if to_right else rest), most
        return (most if to_right else 0), rest

    def first_copy(to_right, piece):
        place = raw.at[0, pl.ds(*first_rows(to_right, piece))]
        return pltpu.make_async_remote_copy(
            src_ref=place,
            dst_ref=place,
            send_sem=right_sem.at[0] if to_right else left_sem.at[chips - 1],
            recv_sem=first_sems.at[1 if to_right else 0, piece],
            device_id=(sky, vel + 2) if to_right else (sky, vel - 2),
            device_id_type=MESH,
        )

    def fresh_copy(to_right, piece):
        place = fresh.at[core, :, pl.ds(*fresh_rows(to_right, piece))]
        return pltpu.make_async_remote_copy(
            src_ref=place,
            dst_ref=place,
            send_sem=fresh_send.at[piece],
            recv_sem=fresh_recv.at[piece],
            device_id=partner,
            device_id_type=MESH,
        )

    def halo_copy(to_next):
        source = raw.at[:, pl.ds(rows - HALO if to_next else 0, HALO)]
        sems = top_sems if to_next else bottom_sems
        return pltpu.make_async_remote_copy(
            src_ref=source,
            dst_ref=top if to_next else bottom,
            send_sem=sems.at[0],
            recv_sem=sems.at[1],
            device_id=(sky + 1, vel) if to_next else (sky - 1, vel),
            device_id_type=MESH,
        )

    def pair_copy(blur, late):
        skip = 1 if late else 0
        place = pl.ds(pl.multiple_of((blur + 1) * BLOCK, 8), BLOCK)
        return pltpu.make_async_remote_copy(
            src_ref=blurred.at[pl.ds(core * frames + skip, frames - skip), :, place],
            dst_ref=landing.at[blur + 1, pl.ds(skip, frames - skip)],
            send_sem=pair_sends.at[skip],
            recv_sem=pair_recv.at[blur + 1],
            device_id=partner,
            device_id_type=MESH,
        )

    def to_partner(blur, late):
        @pl.when(late)
        def _():
            pair_copy(blur, True).start()

        @pl.when(jnp.logical_not(late))
        def _():
            pair_copy(blur, False).start()

    def from_partner(blur, late):
        place = pl.ds(pl.multiple_of((blur + 1) * BLOCK, 8), BLOCK)

        @pl.when(late)
        def _():
            pair_copy(blur, True).wait_recv()

        @pl.when(jnp.logical_not(late))
        def _():
            pair_copy(blur, False).wait_recv()
            for tile in range(tiles):
                blurred[(1 - core) * frames, tile, place] = landing[blur + 1, 0, tile]

        for m in range(1, frames):
            for tile in range(tiles + 1):
                blurred[(1 - core) * frames + m, tile, place] = landing[blur + 1, m, tile]

    right_up = chip == 0
    left_up = chip < chips - 1

    def send_half(to_right, upward, part, source=None):
        def one(index, carry):
            place = jnp.where(upward, index, per // 2 - 1 - index)
            there = None if source is None else (source, place)
            send_block(chip * per + part * (per // 2) + place, to_right, there)
            return carry

        lax.fori_loop(0, per // 2, one, 0)

    def send_first(to_right, upward, ready):
        for kind, source in ((0, psi_ref), (1, phi_ref)):

            @pl.when(ready & (core == kind))
            def _(source=source):
                send_half(to_right, upward, core, source)

    right_ready = (chip > 0) | (core == 0)
    left_ready = (chip < chips - 1) | (core == 1)
    send_first(False, left_up, has_left & left_ready)

    @pl.when(core == 0)
    def _():
        pl.semaphore_wait(answers.at[1], 1)
        trade_copy(phi_ref).start()

    @pl.when(core == 1)
    def _():
        trade_copy(psi_ref).start()

    @pl.when(has_right)
    def _():
        pl.semaphore_wait(answers.at[0], 1)

    send_first(True, right_up, has_right & right_ready)
    own_copy(psi_ref).wait()
    taps_copy.wait()
    shifts_copy.wait()
    total = taps_ref[0]
    for i in range(1, taps):
        total = total + taps_ref[i]
    scale = 1.0 / jnp.full((8, LANES), total, jnp.float32)
    for i in range(taps):
        value = jnp.full((8, LANES), taps_ref[i], jnp.float32) * scale
        weights_ref[0, i] = value
        weights_ref[1, i] = value * value

    def build(band, kind, lead):
        depth = (3 - lead) * LANES
        place = lax.broadcasted_iota(jnp.int32, (depth, LANES), 0)
        place = place - lax.broadcasted_iota(jnp.int32, (depth, LANES), 1)
        spot = place - (LANES - SHIFT * lead - half)
        matrix = jnp.zeros((depth, LANES), jnp.float32)
        for i in range(taps):
            value = jnp.broadcast_to(weights_ref[kind, i][:1], (depth, LANES))
            matrix = jnp.where(spot == i, value, matrix)
        coarse = matrix.astype(jnp.bfloat16)
        band[:depth] = coarse
        band[depth : 2 * depth] = coarse
        band[2 * depth :] = (matrix - coarse.astype(jnp.float32)).astype(jnp.bfloat16)

    build(bands_ref.at[0], 0, 0)
    build(bands_ref.at[1], 1, 0)
    build(band1, core, 1)
    trade_copy(psi_ref).wait_recv()

    def send_rest(to_right, upward, present, ready):
        @pl.when(present)
        def _():
            send_half(to_right, upward, 1 - core)

        @pl.when(present & jnp.logical_not(ready))
        def _():
            send_half(to_right, upward, core)

    send_rest(False, left_up, has_left, left_ready)
    send_rest(True, right_up, has_right, right_ready)

    @pl.when(chip == chips - 1)
    def _():
        first_copy(False, 0).start()
        first_copy(False, 1).start()

    @pl.when(chip == 0)
    def _():
        first_copy(True, 0).start()
        first_copy(True, 1).start()

    @pl.when(core == 1)
    def _():
        pl.semaphore_wait(answers.at[2], has_prev.astype(jnp.int32) + has_next.astype(jnp.int32))
        pl.semaphore_signal(answers.at[3], inc=1, device_id=partner, device_id_type=MESH)

    @pl.when(core == 0)
    def _():
        pl.semaphore_wait(answers.at[3], 1)

    @pl.when(has_next & (chip == chips - 1))
    def _():
        halo_copy(True).start()

    @pl.when(has_prev & (chip == 0))
    def _():
        halo_copy(False).start()

    def blur_along(source, start, count, place, lead):
        if lead:
            values = source[1:frames, pl.ds(start, count)].reshape((frames - 1) * count, width)
            banded = blur_columns(values, band1[...], 1)
        else:
            values = source[0, pl.ds(start, count)]
            banded = blur_columns(values, bands_ref[core], 0)
        height = values.shape[0]
        for tile in range(tiles + lead):
            piece = banded[tile * height : (tile + 1) * height]
            if lead and tile in (0, tiles):
                lane = lax.broadcasted_iota(jnp.int32, (height, LANES), 1)
                piece = jnp.where(lane >= SHIFT if tile == 0 else lane < SHIFT, piece, 0.0)
            for m in range(height // count):
                along[lead + m, tile, pl.ds(place, count)] = piece[m * count : (m + 1) * count]

    def blur_block(block, late):
        start = pl.multiple_of(block * BLOCK, 8)
        place = pl.multiple_of(start + HALO, 8)
        blur_along(raw, start, BLOCK, place, 1)

        @pl.when(jnp.logical_not(late))
        def _():
            blur_along(raw, start, BLOCK, place, 0)

    def across(m, tile, start, target, place, count):
        factors = [weights_ref[core, i] for i in range(taps)]
        for group in range(count // 8):
            base = start + 8 * group
            value = factors[0] * along[m, tile, pl.ds(base, 8)]
            for i in range(1, taps):
                value += factors[i] * along[m, tile, pl.ds(base + i, 8)]
            target[pl.ds(pl.multiple_of(place + 8 * group, 8), 8)] = value

    def blur_across(blur, late):
        start = blur * BLOCK + HALO - 8 - half
        place = (blur + 1) * BLOCK

        def one_map(m, carry):
            for tile in range(tiles + 1):
                across(m, tile, start, blurred.at[core * frames + m, tile], place, BLOCK)
            return carry

        lax.fori_loop(jnp.asarray(late, jnp.int32), frames, one_map, 0)

    def first_arrives(to_right):
        region = ABOVE if to_right else BLOCK * per * (chips - 1) - ABOVE
        for piece in range(2):
            first_copy(to_right, piece).wait_recv()

            @pl.when(has_right if to_right else has_left)
            def _(piece=piece):
                first_copy(to_right, piece).start()

            start, count = first_rows(to_right, piece)
            blur_along(raw, start, count, start + HALO, 0)
            begin, height = fresh_rows(to_right, piece)

            def one_tile(tile, carry, begin=begin, height=height):
                target = fresh.at[core, tile]
                across(0, tile, region + begin + HALO - half, target, begin, height)
                return carry

            lax.fori_loop(0, tiles, one_tile, 0)
            fresh_copy(to_right, piece).start()

    def ends_rows(to_right, piece):
        origin = 0 if to_right else BLOCK * per * (chips - 1) - HALO
        if piece < 2:
            begin, count = first_rows(to_right, piece)
            return (begin, count), (begin - origin, count)
        begin = 0 if piece == 2 else BLOCK * per
        return (origin + begin, HALO), (begin, HALO)

    def ends_copy(to_right, piece):
        there, here = ends_rows(to_right, piece)
        return pltpu.make_async_remote_copy(
            src_ref=raw.at[0, pl.ds(*there)],
            dst_ref=ends_ref.at[core, pl.ds(*here)],
            send_sem=ends_send.at[piece],
            recv_sem=ends_recv.at[piece],
            device_id=partner,
            device_id_type=MESH,
        )

    def ends_begin(to_right, piece):
        ends_copy(to_right, piece).start()
        there, here = ends_rows(to_right, piece)
        ends_ref[core, pl.ds(*here)] = raw[0, pl.ds(*there)]

    def last_arrives(to_right):
        ends_copy(to_right, 2).wait()
        ends_copy(to_right, 3).wait()
        for piece in range(2):
            first_copy(to_right, piece).wait_recv()

            @pl.when(has_right if to_right else has_left)
            def _(piece=piece):
                first_copy(to_right, piece).start()

            ends_begin(to_right, piece)

    def fresh_wait(to_right):
        for piece in range(2):
            fresh_copy(to_right, piece).wait_recv()

    def together(count):
        if trials % 4:
            return 1
        return 2 if count == JOIN else max(JOIN // count, 1)

    def stack(first, count, unroll):
        def one_trial(trial, carry):
            stack_rows(shifts_ref, blurred, done_ref, trial, first, count, 0, False, unroll)
            return carry

        lax.fori_loop(0, trials, one_trial, 0, unroll=together(count))

    closing = last_row(chips, per, jnp.logical_not(low))
    other = last_row(chips, per, low)

    def stack_part(first, count, unroll):
        def one_trial(trial, carry):
            stack_rows(shifts_ref, blurred, part_ref, trial, first, count, closing, True, unroll)
            return carry

        lax.fori_loop(0, trials, one_trial, 0, unroll=together(count))


    def own_block(block, carry):
        blur_block(block, False)
        return carry

    def own_blur(blur, carry):
        blur_across(blur, False)
        pair_copy(blur, False).start()
        return carry

    def own_wait(blur, carry):
        from_partner(blur, False)
        return carry

    lax.fori_loop(chip * per, chip * per + per, own_block, 0)
    lax.fori_loop(chip * per + 1, chip * per + per, own_blur, 0)
    lax.fori_loop(chip * per + 1, chip * per + per, own_wait, 0)
    stack(pl.multiple_of((chip * per + 2) * BLOCK - 8, 8), BLOCK * (per - 3), 2)

    def stream(side, index):
        distance = index // per
        j = index % per
        origin = jnp.where(side == 1, chip + 1 + distance, chip - 1 - distance)
        present = (index >= 0) & (origin >= 0) & (origin < chips)
        edge = jnp.where(side == 1, origin == chips - 1, origin == 0)
        upward = (side == 1) != edge
        block = origin * per + jnp.where(upward, j, per - 1 - j)
        last = edge & (j == per - 1)
        return present, edge, upward, j, block, last

    def blurs(side, index, act):
        present, edge, upward, j, block, last = stream(side, index)
        count = jnp.where(present & jnp.logical_not(edge & (j == 0)), 1 + last.astype(jnp.int32), 0)
        begin = jnp.where(upward, block, block + 1)
        turn = jnp.where(upward, 1, -1)

        def one(k, carry):
            act(begin + turn * k)
            return carry

        lax.fori_loop(0, count, one, 0)

    def arrive(index):
        for side in (1, 0):
            present, edge, _, j, block, _ = stream(side, index)
            late = edge & (j > 1)

            @pl.when(present & late)
            def _(side=side, block=block):
                line_copy(block, True, True).wait_recv()

            @pl.when(present & jnp.logical_not(late))
            def _(side=side, block=block):
                line_copy(block, True, False).wait_recv()

            @pl.when(present & (has_left if side else has_right))
            def _(side=side, block=block):
                send_block(block, side == 0)

            @pl.when(present & edge & (j == 1) & (has_next if side else has_prev))
            def _(side=side):
                halo_copy(side == 1).start()

    def blur_side(index):
        def one_side(side, carry):
            present, edge, _, j, block, _ = stream(side, index)
            late = edge & (j > 1)

            @pl.when(present)
            def _():
                blur_block(block, late)

            def spread(blur):
                blur_across(blur, late)
                to_partner(blur, late)

            blurs(side, index, spread)
            return carry

        lax.fori_loop(0, 2, one_side, 0)

    def stack_side(index):
        def one_side(side, carry):
            present, edge, upward, j, block, last = stream(side, index)
            late = edge & (j > 1)
            blurs(side, index, lambda blur: from_partner(blur, late))
            begin = pl.multiple_of(jnp.where(upward, block - 1, block + 2) * BLOCK - 8, 8)
            closes = (side == 1) == low

            @pl.when(present & jnp.logical_not(edge))
            def _():
                stack(begin, BLOCK, True)

            @pl.when(present & edge & closes & jnp.logical_not(last) & (j > 2))
            def _():
                stack_part(begin, BLOCK, True)

            @pl.when(present & closes & last)
            def _():
                stack_part(pl.multiple_of((block - 1) * BLOCK - 8, 8), JOIN, True)

            return carry

        lax.fori_loop(0, 2, one_side, 0)

    limit = steps - 2
    mirror = chips - 1 - chip
    top_step = jnp.minimum(jnp.maximum(per * (mirror - 1) + 4, per * (chip - 1) + 2), limit)
    bottom_step = jnp.minimum(jnp.maximum(per * (chip - 1) + 4, per * (mirror - 1) + 2), limit)

    others = jnp.where(low, chip, mirror)
    other_step = jnp.where(others > 0, per * others + 2, -2)

    def step(index, carry):
        @pl.when(index < steps)
        def _():
            arrive(index)
            blur_side(index)

        @pl.when(index == top_step)
        def _():
            @pl.when(has_prev)
            def _():
                halo_copy(True).wait_recv()
                blur_along(top, 0, HALO, 0, 0)
                blur_along(top, 0, HALO, 0, 1)

            @pl.when(jnp.logical_not(has_prev))
            def _():
                for m in range(frames):
                    for tile in range(tiles + 1):
                        along[m, tile, pl.ds(0, HALO)] = jnp.zeros((HALO, LANES), jnp.float32)

            blur_across(-1, False)
            blur_across(0, False)

            @pl.when(jnp.logical_not(has_prev))
            def _():
                for m in range(frames):
                    for tile in range(tiles + 1):
                        blurred[core * frames + m, tile, pl.ds(0, ABOVE)] = jnp.zeros(
                            (ABOVE, LANES), jnp.float32
                        )

            pair_copy(-1, False).start()
            pair_copy(0, False).start()

        @pl.when(index == bottom_step)
        def _():
            @pl.when(has_next)
            def _():
                halo_copy(False).wait_recv()
                blur_along(bottom, 0, HALO, rows + HALO, 0)
                blur_along(bottom, 0, HALO, rows + HALO, 1)

            @pl.when(jnp.logical_not(has_next))
            def _():
                for m in range(frames):
                    for tile in range(tiles + 1):
                        along[m, tile, pl.ds(rows + HALO, HALO)] = jnp.zeros(
                            (HALO, LANES), jnp.float32
                        )

            blur_across(blocks, False)
            blur_across(blocks + 1, False)

            @pl.when(jnp.logical_not(has_next))
            def _():
                for m in range(frames):
                    for tile in range(tiles + 1):
                        blurred[core * frames + m, tile, pl.ds(rows + ABOVE, ABOVE)] = jnp.zeros(
                            (ABOVE, LANES), jnp.float32
                        )

            pair_copy(blocks, False).start()
            pair_copy(blocks + 1, False).start()

        @pl.when((index == steps - 3) & low)
        def _():
            ends_begin(False, 2)
            ends_begin(False, 3)

        @pl.when((index == steps - 3) & jnp.logical_not(low))
        def _():
            ends_begin(True, 2)
            ends_begin(True, 3)

        @pl.when(index == other_step)
        def _():
            @pl.when(low)
            def _():
                first_arrives(True)

            @pl.when(jnp.logical_not(low))
            def _():
                first_arrives(False)

        stack_side(index - 1)

        @pl.when(index - 1 == other_step)
        def _():
            @pl.when(low)
            def _():
                fresh_wait(True)

            @pl.when(jnp.logical_not(low))
            def _():
                fresh_wait(False)

            behind = jnp.where(low, 0, BLOCK)
            count = BLOCK * (per - 1)
            place = pl.ds(pl.multiple_of(other + behind + ABOVE, 8), count)
            for kind in range(2):
                for tile in range(tiles):
                    there = pl.ds(pl.multiple_of(behind, 8), count)
                    blurred[kind * frames, tile, place] = fresh[kind, tile, there]
            stack(other, BLOCK * per, 4)

        @pl.when(index - 1 == top_step)
        def _():
            from_partner(-1, False)
            from_partner(0, False)
            stack(0, ABOVE, True)

        @pl.when(index - 1 == bottom_step)
        def _():
            from_partner(blocks, False)
            from_partner(blocks + 1, False)
            stack(rows - ABOVE, ABOVE, True)

        return carry

    lax.fori_loop(0, steps + 1, step, 0)

    def drain_sends():
        for sides in (1, 2):
            late = (per - 1) * sides
            whole = blurred.at[pl.ds(0, frames), :, pl.ds(0, (blocks + 3 - late) * BLOCK)]
            most = blurred.at[pl.ds(0, frames - 1), :, pl.ds(0, late * BLOCK)]

            @pl.when(has_left.astype(jnp.int32) + has_right.astype(jnp.int32) == sides)
            def _(whole=whole, most=most):
                pltpu.make_async_copy(whole, whole, pair_sends.at[0]).wait()
                pltpu.make_async_copy(most, most, pair_sends.at[1]).wait()

        trade_copy(psi_ref).wait_send()

        def drain(origin, carry):
            part = raw.at[:, pl.ds(pl.multiple_of(origin * (2 * share), 8), 2 * share)]

            @pl.when(has_right & (origin <= chip))
            def _():
                pltpu.make_async_copy(part, part, right_sem.at[origin]).wait()

            @pl.when(has_left & (origin >= chip))
            def _():
                pltpu.make_async_copy(part, part, left_sem.at[origin]).wait()

            return carry

        lax.fori_loop(0, chips, drain, 0)

        @pl.when((other_step > 0) & low)
        def _():
            for piece in range(2):
                fresh_copy(True, piece).wait_send()

        @pl.when((other_step > 0) & jnp.logical_not(low))
        def _():
            for piece in range(2):
                fresh_copy(False, piece).wait_send()

        @pl.when(has_next)
        def _():
            halo_copy(True).wait_send()

        @pl.when(has_prev)
        def _():
            halo_copy(False).wait_send()


    @pl.when(others == 0)
    def _():
        drain_sends()

    @pl.when(low)
    def _():
        last_arrives(False)

    @pl.when(jnp.logical_not(low))
    def _():
        last_arrives(True)

    @pl.when(others > 0)
    def _():
        drain_sends()

    for piece in range(2):
        ends_copy(False, piece).wait()


def per_device(vels, skies, psi_maps, phi_maps, psf_taps, shifts):
    frames, share, width = psi_maps.shape
    maps = 2 * frames
    tiles = width // LANES
    rows = share * vels
    trials = shifts.shape[0]
    blocks = rows // BLOCK
    taps = psf_taps.shape[0]
    shifts = pltpu.with_memory_space_constraint(jnp.transpose(shifts, (1, 2, 0)), pltpu.HBM)
    psf_taps = pltpu.with_memory_space_constraint(psf_taps, pltpu.HBM)
    psi_maps = pltpu.with_memory_space_constraint(psi_maps, pltpu.HBM)
    phi_maps = pltpu.with_memory_space_constraint(phi_maps, pltpu.HBM)
    dma = pltpu.SemaphoreType.DMA
    part, ends, bands, weights, done = pl.pallas_call(
        functools.partial(gather_kernel, vels, skies),
        out_shape=(
            jax.ShapeDtypeStruct((2, trials, 2 * share, width), jnp.float32),
            jax.ShapeDtypeStruct((2, 2 * share + HALO, width), jnp.float32),
            jax.ShapeDtypeStruct((2, 9 * LANES, LANES), jnp.bfloat16),
            jax.ShapeDtypeStruct((2, taps, 8, LANES), jnp.float32),
            jax.ShapeDtypeStruct((trials, rows, width), jnp.float32),
        ),
        in_specs=[
            pl.BlockSpec(memory_space=pl.ANY),
            pl.BlockSpec(memory_space=pl.ANY),
            pl.BlockSpec(memory_space=pl.ANY),
            pl.BlockSpec(memory_space=pl.ANY),
        ],
        out_specs=(pl.BlockSpec(memory_space=pltpu.VMEM),) * 5,
        scratch_shapes=[
            pltpu.SMEM((taps,), jnp.float32),
            pltpu.SMEM(shifts.shape, jnp.int32),
            pltpu.VMEM((maps, tiles + 1, rows + 2 * ABOVE, LANES), jnp.float32),
            pltpu.VMEM((frames, rows, width), jnp.float32),
            pltpu.VMEM((frames, tiles + 1, rows + 2 * HALO, LANES), jnp.float32),
            pltpu.VMEM((blocks + 3, frames, tiles + 1, BLOCK, LANES), jnp.float32),
            pltpu.VMEM((frames, HALO, width), jnp.float32),
            pltpu.VMEM((frames, HALO, width), jnp.float32),
            pltpu.VMEM((6 * LANES, LANES), jnp.bfloat16),
            pltpu.VMEM((2, tiles, 2 * share, LANES), jnp.float32),
            pltpu.SemaphoreType.REGULAR((4,)),
            dma((2,)),
            dma,
            dma((2,)),
            dma((blocks,)),
            dma((vels // 2,)),
            dma((vels // 2,)),
            dma((2,)),
            dma((blocks + 3,)),
            dma((2,)),
            dma((2,)),
            dma((2, 2)),
            dma((2,)),
            dma((2,)),
            dma((4,)),
            dma((4,)),
        ],
        compiler_params=pltpu.CompilerParams(
            collective_id=0, has_side_effects=True, vmem_limit_bytes=36 * 2**20
        ),
        name="gather",
    )(psf_taps, shifts, psi_maps, phi_maps)
    return pl.pallas_call(
        functools.partial(finish_kernel, vels),
        out_shape=jax.ShapeDtypeStruct((trials, rows, width), jnp.float32),
        in_specs=[pl.BlockSpec(memory_space=pltpu.VMEM)] * 5,
        out_specs=pl.BlockSpec(memory_space=pl.ANY),
        scratch_shapes=[
            pltpu.VMEM((2, tiles, 2 * share + HALO, LANES), jnp.float32),
            pltpu.VMEM((2, tiles, 2 * share, LANES), jnp.float32),
            pltpu.VMEM((trials, 2 * share, width), jnp.float32),
            dma((3, trials)),
        ],
        compiler_params=pltpu.CompilerParams(vmem_limit_bytes=12 * 2**20),
        name="finish",
    )(part, ends, bands, weights, done)


def solution(mesh):
    return jax.shard_map(
        functools.partial(per_device, mesh.shape["vel"], mesh.shape["sky"]),
        mesh=mesh,
        in_specs=(
            P(None, ("sky", "vel"), None),
            P(None, ("sky", "vel"), None),
            P(),
            P("vel", None, None),
        ),
        out_specs=P("vel", "sky", None),
        check_vma=False,
    )
```

```python
import functools
import jax
import jax.numpy as jnp
from jax import lax
from jax.experimental import pallas as pl
from jax.experimental.pallas import tpu as pltpu
from jax.sharding import PartitionSpec as P

SHIFT = 16
BLOCK = 16
HALO = 2 * BLOCK
ABOVE = BLOCK + 8
JOIN = 4 * BLOCK
LANES = 128
MESH = pl.DeviceIdType.MESH


def stack_rows(
    shifts_ref, maps_ref, out_ref, trial, first, count, skip, partial, unroll, kinds=(0, 1)
):
    frames = shifts_ref.shape[0]
    tiles = maps_ref.shape[1]
    lane = lax.broadcasted_iota(jnp.int32, (8, LANES), 1)
    down, turn, inside = [], [], []
    for frame in range(1, frames):
        offset = shifts_ref[frame, 1, trial] + SHIFT
        down.append(shifts_ref[frame, 0, trial] + ABOVE)
        turn.append(lax.rem(LANES - offset, LANES))
        inside.append(lane >= offset)

    def one_group(group, carry):
        base = first + group * 8

        def stacked(kind):
            total = [None] * (tiles - 1)
            if not partial:
                total = [
                    maps_ref[kind * frames, tile, pl.ds(pl.multiple_of(base + ABOVE, 8), 8)]
                    for tile in range(tiles - 1)
                ]
            for step in range(frames - 1):
                m = kind * frames + step + 1
                pieces = [maps_ref[m, tile, pl.ds(base + down[step], 8)] for tile in range(tiles)]
                for tile in range(tiles - 1):
                    joined = jnp.where(inside[step], pieces[tile], pieces[tile + 1])
                    moved = pltpu.roll(joined, turn[step], 1)
                    total[tile] = moved if total[tile] is None else total[tile] + moved
            return total

        sums = [stacked(kind) for kind in kinds]
        rows = pl.ds(pl.multiple_of(base - skip, 8), 8)
        for tile in range(tiles - 1):
            columns = slice(tile * LANES, (tile + 1) * LANES)
            if partial:
                for kind, total in zip(kinds, sums):
                    out_ref[kind, trial, rows, columns] = total[tile]
            else:
                out_ref[trial, rows, columns] = sums[0][tile] * lax.rsqrt(sums[1][tile])
        return carry

    lax.fori_loop(0, count // 8, one_group, 0, unroll=unroll)


def last_row(chips, per, to_right):
    return pl.multiple_of(jnp.where(to_right, ABOVE, BLOCK * per * (chips - 1) - ABOVE), 8)


def blur_columns(values, band, lead):
    tiles = values.shape[1] // LANES
    coarse = values.astype(jnp.bfloat16)
    fine = (values - coarse.astype(jnp.float32)).astype(jnp.bfloat16)

    def windows(part):
        blank = jnp.zeros((part.shape[0], LANES), part.dtype)
        columns = [blank] + [part[:, t * LANES : (t + 1) * LANES] for t in range(tiles)] + [blank]
        wide = 3 - lead
        return jnp.concatenate(
            [jnp.concatenate(columns[t : t + wide], axis=1) for t in range(tiles + lead)], axis=0
        )

    high, rest = windows(coarse), windows(fine)
    return jnp.dot(
        jnp.concatenate([high, rest, high], axis=1), band, preferred_element_type=jnp.float32
    )


def finish_kernel(
    vels, part_ref, ends_ref, bands_ref, weights_ref, done_ref, out_ref, along, fresh, closing, sems
):
    trials, rows, width = done_ref.shape
    count = part_ref.shape[2]
    height = ends_ref.shape[1]
    taps = weights_ref.shape[1]
    tiles = width // LANES
    chips = vels // 2
    low = lax.axis_index("vel") // 2 < chips // 2
    first = last_row(chips, count // BLOCK, jnp.logical_not(low))
    small = ABOVE
    large = rows - count - small
    large_row = pl.multiple_of(jnp.where(low, 0, small + count), 8)
    small_row = pl.multiple_of(jnp.where(low, large + count, 0), 8)

    def large_copy(trial):
        part = pl.ds(large_row, large)
        return pltpu.make_async_copy(done_ref.at[trial, part], out_ref.at[trial, part], sems.at[0, trial])

    def small_copy(trial):
        part = pl.ds(small_row, small)
        return pltpu.make_async_copy(done_ref.at[trial, part], out_ref.at[trial, part], sems.at[1, trial])

    def closing_copy(trial):
        part = pl.ds(first, count)
        return pltpu.make_async_copy(closing.at[trial], out_ref.at[trial, part], sems.at[2, trial])

    def begin(trial, carry):
        large_copy(trial).start()
        small_copy(trial).start()
        return carry

    lax.fori_loop(0, trials, begin, 0)

    for kind in range(2):
        blurred = blur_columns(ends_ref[kind], bands_ref[kind], 0)
        for tile in range(tiles):
            along[kind, tile] = blurred[tile * height : (tile + 1) * height]
    start = jnp.where(low, 8, ABOVE) - taps // 2

    def across(index, carry):
        kind, tile = index // tiles, index % tiles
        for group in range(count // 8):
            base = start + 8 * group
            value = weights_ref[kind, 0] * along[kind, tile, pl.ds(base, 8)]
            for i in range(1, taps):
                value += weights_ref[kind, i] * along[kind, tile, pl.ds(base + i, 8)]
            fresh[kind, tile, 8 * group : 8 * group + 8] = value
        return carry

    lax.fori_loop(0, 2 * tiles, across, 0)

    def compute(trial, carry):
        for tile in range(tiles):
            columns = slice(tile * LANES, (tile + 1) * LANES)
            psi = part_ref[0, trial, :, columns] + fresh[0, tile]
            phi = part_ref[1, trial, :, columns] + fresh[1, tile]
            closing[trial, :, columns] = psi * lax.rsqrt(phi)
        closing_copy(trial).start()
        return carry

    lax.fori_loop(0, trials, compute, 0)

    def finish(trial, carry):
        large_copy(trial).wait()
        small_copy(trial).wait()
        closing_copy(trial).wait()
        return carry

    lax.fori_loop(0, trials, finish, 0)


def gather_kernel(
    vels, skies, taps_hbm, shifts_hbm, psi_ref, phi_ref,
    part_ref, ends_ref, bands_ref, weights_ref, done_ref,
    taps_ref, shifts_ref, blurred, raw, along, landing, top, bottom, band1, fresh,
    answers, small_sems, own_sem, trade_sems, recv_sem, right_sem, left_sem, pair_sends, pair_recv, top_sems, bottom_sems,
    first_sems, fresh_send, fresh_recv, ends_send, ends_recv,
):
    frames, share, width = psi_ref.shape
    trials = shifts_ref.shape[2]
    taps = taps_ref.shape[0]
    half = taps // 2
    chips = vels // 2
    tiles = width // LANES
    rows = vels * share
    blocks = rows // BLOCK
    per = blocks // chips
    steps = per * (chips - 1)
    sky = lax.axis_index("sky")
    vel = lax.axis_index("vel")
    chip = vel // 2
    core = vel % 2
    has_right = chip < chips - 1
    has_left = chip > 0
    has_next = sky < skies - 1
    has_prev = sky > 0
    low = chip < chips // 2
    partner = (sky, vel + 1 - 2 * core)

    taps_copy = pltpu.make_async_copy(taps_hbm, taps_ref, small_sems.at[0])
    shifts_copy = pltpu.make_async_copy(shifts_hbm, shifts_ref, small_sems.at[1])
    own_rows = pl.ds(pl.multiple_of(vel * share, 8), share)

    def own_copy(source):
        return pltpu.make_async_copy(source, raw.at[:, own_rows], own_sem)

    left, right = (sky, vel - 2), (sky, vel + 2)
    before, after = (sky - 1, vel), (sky + 1, vel)
    skies_near = ((has_prev & (core == 1), before), (has_next & (core == 1), after))
    barrier = pltpu.get_barrier_semaphore()

    def greet(semaphore, device, present):
        @pl.when(present)
        def _():
            pl.semaphore_signal(semaphore, inc=1, device_id=device, device_id_type=MESH)

    greet(barrier, right, has_right)
    greet(barrier, partner, (core == 0) | (chip == 0))
    for present, device in skies_near:
        greet(barrier, device, present)
    @pl.when(core == 0)
    def _():
        own_copy(psi_ref).start()

    @pl.when(core == 1)
    def _():
        own_copy(phi_ref).start()

    taps_copy.start()
    shifts_copy.start()
    callers = (has_left | (core == 0)).astype(jnp.int32) + core
    for present, device in skies_near:
        callers = callers + present.astype(jnp.int32)
    pl.semaphore_wait(barrier, callers)
    greet(answers.at[0], left, has_left)
    greet(answers.at[1], partner, core == 1)
    for present, device in skies_near:
        greet(answers.at[2], device, present)

    def trade_copy(source):
        return pltpu.make_async_remote_copy(
            src_ref=source,
            dst_ref=raw.at[:, own_rows],
            send_sem=trade_sems.at[0],
            recv_sem=trade_sems.at[1],
            device_id=partner,
            device_id_type=MESH,
        )

    def block_rows(block):
        return pl.ds(pl.multiple_of(block * BLOCK, 8), BLOCK)

    def line_copy(block, to_right, late, source=None):
        maps = pl.ds(1, frames - 1) if late else pl.ds(0, frames)
        place = raw.at[maps, block_rows(block)]
        return pltpu.make_async_remote_copy(
            src_ref=place if source is None else source[0].at[maps, block_rows(source[1])],
            dst_ref=place,
            send_sem=(right_sem if to_right else left_sem).at[block // per],
            recv_sem=recv_sem.at[block],
            device_id=(sky, vel + 2) if to_right else (sky, vel - 2),
            device_id_type=MESH,
        )

    def send_block(block, to_right, source=None):
        if to_right:
            late = (block < per) & (block > 1)
        else:
            late = (block >= blocks - per) & (block < blocks - 2)

        @pl.when(late)
        def _():
            line_copy(block, to_right, True, source).start()

        @pl.when(jnp.logical_not(late))
        def _():
            line_copy(block, to_right, False, source).start()

    most = BLOCK * (per - 3)
    rest = 3 * BLOCK

    def first_rows(to_right, piece):
        begin = HALO if to_right else BLOCK * per * (chips - 1)
        if piece == 0:
            return begin + (0 if to_right else BLOCK), most
        return begin + (most if to_right else 0), BLOCK

    def fresh_rows(to_right, piece):
        if piece == 0:
            return (0 if to_right else rest), most
        return (most if to_right else 0), rest

    def first_copy(to_right, piece):
        place = raw.at[0, pl.ds(*first_rows(to_right, piece))]
        return pltpu.make_async_remote_copy(
            src_ref=place,
            dst_ref=place,
            send_sem=right_sem.at[0] if to_right else left_sem.at[chips - 1],
            recv_sem=first_sems.at[1 if to_right else 0, piece],
            device_id=(sky, vel + 2) if to_right else (sky, vel - 2),
            device_id_type=MESH,
        )

    def fresh_copy(to_right, piece):
        place = fresh.at[core, :, pl.ds(*fresh_rows(to_right, piece))]
        return pltpu.make_async_remote_copy(
            src_ref=place,
            dst_ref=place,
            send_sem=fresh_send.at[piece],
            recv_sem=fresh_recv.at[piece],
            device_id=partner,
            device_id_type=MESH,
        )

    def halo_copy(to_next):
        source = raw.at[:, pl.ds(rows - HALO if to_next else 0, HALO)]
        sems = top_sems if to_next else bottom_sems
        return pltpu.make_async_remote_copy(
            src_ref=source,
            dst_ref=top if to_next else bottom,
            send_sem=sems.at[0],
            recv_sem=sems.at[1],
            device_id=(sky + 1, vel) if to_next else (sky - 1, vel),
            device_id_type=MESH,
        )

    def pair_copy(blur, late):
        skip = 1 if late else 0
        place = pl.ds(pl.multiple_of((blur + 1) * BLOCK, 8), BLOCK)
        return pltpu.make_async_remote_copy(
            src_ref=blurred.at[pl.ds(core * frames + skip, frames - skip), :, place],
            dst_ref=landing.at[blur + 1, pl.ds(skip, frames - skip)],
            send_sem=pair_sends.at[skip],
            recv_sem=pair_recv.at[blur + 1],
            device_id=partner,
            device_id_type=MESH,
        )

    def to_partner(blur, late):
        @pl.when(late)
        def _():
            pair_copy(blur, True).start()

        @pl.when(jnp.logical_not(late))
        def _():
            pair_copy(blur, False).start()

    def from_partner(blur, late):
        place = pl.ds(pl.multiple_of((blur + 1) * BLOCK, 8), BLOCK)

        @pl.when(late)
        def _():
            pair_copy(blur, True).wait_recv()

        @pl.when(jnp.logical_not(late))
        def _():
            pair_copy(blur, False).wait_recv()
            for tile in range(tiles):
                blurred[(1 - core) * frames, tile, place] = landing[blur + 1, 0, tile]

        for m in range(1, frames):
            for tile in range(tiles + 1):
                blurred[(1 - core) * frames + m, tile, place] = landing[blur + 1, m, tile]

    right_up = chip == 0
    left_up = chip < chips - 1

    def send_half(to_right, upward, part, source=None):
        def one(index, carry):
            place = jnp.where(upward, index, per // 2 - 1 - index)
            there = None if source is None else (source, place)
            send_block(chip * per + part * (per // 2) + place, to_right, there)
            return carry

        lax.fori_loop(0, per // 2, one, 0)

    def send_first(to_right, upward, ready):
        for kind, source in ((0, psi_ref), (1, phi_ref)):

            @pl.when(ready & (core == kind))
            def _(source=source):
                send_half(to_right, upward, core, source)

    right_ready = (chip > 0) | (core == 0)
    left_ready = (chip < chips - 1) | (core == 1)
    send_first(False, left_up, has_left & left_ready)

    @pl.when(core == 0)
    def _():
        pl.semaphore_wait(answers.at[1], 1)
        trade_copy(phi_ref).start()

    @pl.when(core == 1)
    def _():
        trade_copy(psi_ref).start()

    @pl.when(has_right)
    def _():
        pl.semaphore_wait(answers.at[0], 1)

    send_first(True, right_up, has_right & right_ready)
    own_copy(psi_ref).wait()
    taps_copy.wait()
    shifts_copy.wait()
    total = taps_ref[0]
    for i in range(1, taps):
        total = total + taps_ref[i]
    scale = 1.0 / jnp.full((8, LANES), total, jnp.float32)
    for i in range(taps):
        value = jnp.full((8, LANES), taps_ref[i], jnp.float32) * scale
        weights_ref[0, i] = value
        weights_ref[1, i] = value * value

    def build(band, kind, lead):
        depth = (3 - lead) * LANES
        place = lax.broadcasted_iota(jnp.int32, (depth, LANES), 0)
        place = place - lax.broadcasted_iota(jnp.int32, (depth, LANES), 1)
        spot = place - (LANES - SHIFT * lead - half)
        matrix = jnp.zeros((depth, LANES), jnp.float32)
        for i in range(taps):
            value = jnp.broadcast_to(weights_ref[kind, i][:1], (depth, LANES))
            matrix = jnp.where(spot == i, value, matrix)
        coarse = matrix.astype(jnp.bfloat16)
        band[:depth] = coarse
        band[depth : 2 * depth] = coarse
        band[2 * depth :] = (matrix - coarse.astype(jnp.float32)).astype(jnp.bfloat16)

    build(bands_ref.at[0], 0, 0)
    build(bands_ref.at[1], 1, 0)
    build(band1, core, 1)
    trade_copy(psi_ref).wait_recv()

    def send_rest(to_right, upward, present, ready):
        @pl.when(present)
        def _():
            send_half(to_right, upward, 1 - core)

        @pl.when(present & jnp.logical_not(ready))
        def _():
            send_half(to_right, upward, core)

    send_rest(False, left_up, has_left, left_ready)
    send_rest(True, right_up, has_right, right_ready)

    @pl.when(chip == chips - 1)
    def _():
        first_copy(False, 0).start()
        first_copy(False, 1).start()

    @pl.when(chip == 0)
    def _():
        first_copy(True, 0).start()
        first_copy(True, 1).start()

    @pl.when(core == 1)
    def _():
        pl.semaphore_wait(answers.at[2], has_prev.astype(jnp.int32) + has_next.astype(jnp.int32))
        pl.semaphore_signal(answers.at[3], inc=1, device_id=partner, device_id_type=MESH)

    @pl.when(core == 0)
    def _():
        pl.semaphore_wait(answers.at[3], 1)

    @pl.when(has_next & (chip == chips - 1))
    def _():
        halo_copy(True).start()

    @pl.when(has_prev & (chip == 0))
    def _():
        halo_copy(False).start()

    def blur_along(source, start, count, place, lead):
        if lead:
            values = source[1:frames, pl.ds(start, count)].reshape((frames - 1) * count, width)
            banded = blur_columns(values, band1[...], 1)
        else:
            values = source[0, pl.ds(start, count)]
            banded = blur_columns(values, bands_ref[core], 0)
        height = values.shape[0]
        for tile in range(tiles + lead):
            piece = banded[tile * height : (tile + 1) * height]
            if lead and tile in (0, tiles):
                lane = lax.broadcasted_iota(jnp.int32, (height, LANES), 1)
                piece = jnp.where(lane >= SHIFT if tile == 0 else lane < SHIFT, piece, 0.0)
            for m in range(height // count):
                along[lead + m, tile, pl.ds(place, count)] = piece[m * count : (m + 1) * count]

    def blur_block(block, late):
        start = pl.multiple_of(block * BLOCK, 8)
        place = pl.multiple_of(start + HALO, 8)
        blur_along(raw, start, BLOCK, place, 1)

        @pl.when(jnp.logical_not(late))
        def _():
            blur_along(raw, start, BLOCK, place, 0)

    def across(m, tile, start, target, place, count):
        factors = [weights_ref[core, i] for i in range(taps)]
        for group in range(count // 8):
            base = start + 8 * group
            value = factors[0] * along[m, tile, pl.ds(base, 8)]
            for i in range(1, taps):
                value += factors[i] * along[m, tile, pl.ds(base + i, 8)]
            target[pl.ds(pl.multiple_of(place + 8 * group, 8), 8)] = value

    def blur_across(blur, late):
        start = blur * BLOCK + HALO - 8 - half
        place = (blur + 1) * BLOCK

        def one_map(m, carry):
            for tile in range(tiles + 1):
                across(m, tile, start, blurred.at[core * frames + m, tile], place, BLOCK)
            return carry

        lax.fori_loop(jnp.asarray(late, jnp.int32), frames, one_map, 0)

    def first_arrives(to_right):
        region = ABOVE if to_right else BLOCK * per * (chips - 1) - ABOVE
        for piece in range(2):
            first_copy(to_right, piece).wait_recv()

            @pl.when(has_right if to_right else has_left)
            def _(piece=piece):
                first_copy(to_right, piece).start()

            start, count = first_rows(to_right, piece)
            blur_along(raw, start, count, start + HALO, 0)
            begin, height = fresh_rows(to_right, piece)

            def one_tile(tile, carry, begin=begin, height=height):
                target = fresh.at[core, tile]
                across(0, tile, region + begin + HALO - half, target, begin, height)
                return carry

            lax.fori_loop(0, tiles, one_tile, 0)
            fresh_copy(to_right, piece).start()

    def ends_rows(to_right, piece):
        origin = 0 if to_right else BLOCK * per * (chips - 1) - HALO
        if piece < 2:
            begin, count = first_rows(to_right, piece)
            return (begin, count), (begin - origin, count)
        begin = 0 if piece == 2 else BLOCK * per
        return (origin + begin, HALO), (begin, HALO)

    def ends_copy(to_right, piece):
        there, here = ends_rows(to_right, piece)
        return pltpu.make_async_remote_copy(
            src_ref=raw.at[0, pl.ds(*there)],
            dst_ref=ends_ref.at[core, pl.ds(*here)],
            send_sem=ends_send.at[piece],
            recv_sem=ends_recv.at[piece],
            device_id=partner,
            device_id_type=MESH,
        )

    def ends_begin(to_right, piece):
        ends_copy(to_right, piece).start()
        there, here = ends_rows(to_right, piece)
        ends_ref[core, pl.ds(*here)] = raw[0, pl.ds(*there)]

    def last_arrives(to_right):
        ends_copy(to_right, 2).wait()
        ends_copy(to_right, 3).wait()
        for piece in range(2):
            first_copy(to_right, piece).wait_recv()

            @pl.when(has_right if to_right else has_left)
            def _(piece=piece):
                first_copy(to_right, piece).start()

            ends_begin(to_right, piece)

    def fresh_wait(to_right):
        for piece in range(2):
            fresh_copy(to_right, piece).wait_recv()

    def together(count):
        if trials % 4:
            return 1
        return 2 if count == JOIN else max(JOIN // count, 1)

    def stack(first, count, unroll):
        def one_trial(trial, carry):
            stack_rows(shifts_ref, blurred, done_ref, trial, first, count, 0, False, unroll)
            return carry

        lax.fori_loop(0, trials, one_trial, 0, unroll=together(count))

    closing = last_row(chips, per, jnp.logical_not(low))
    other = last_row(chips, per, low)

    def stack_part(first, count, unroll, kinds=(0, 1)):
        def one_trial(trial, carry):
            stack_rows(
                shifts_ref, blurred, part_ref, trial, first, count, closing, True, unroll, kinds
            )
            return carry

        several = together(count) * (2 if len(kinds) == 1 else 1)
        lax.fori_loop(0, trials, one_trial, 0, unroll=several)


    def own_block(block, carry):
        blur_block(block, False)
        return carry

    def own_blur(blur, carry):
        blur_across(blur, False)
        pair_copy(blur, False).start()
        return carry

    def own_wait(blur, carry):
        from_partner(blur, False)
        return carry

    lax.fori_loop(chip * per, chip * per + per, own_block, 0)
    lax.fori_loop(chip * per + 1, chip * per + per, own_blur, 0)
    lax.fori_loop(chip * per + 1, chip * per + per, own_wait, 0)
    stack(pl.multiple_of((chip * per + 2) * BLOCK - 8, 8), BLOCK * (per - 3), 2)

    def stream(side, index):
        distance = index // per
        j = index % per
        origin = jnp.where(side == 1, chip + 1 + distance, chip - 1 - distance)
        present = (index >= 0) & (origin >= 0) & (origin < chips)
        edge = jnp.where(side == 1, origin == chips - 1, origin == 0)
        upward = (side == 1) != edge
        block = origin * per + jnp.where(upward, j, per - 1 - j)
        last = edge & (j == per - 1)
        return present, edge, upward, j, block, last

    def blurs(side, index, act):
        present, edge, upward, j, block, last = stream(side, index)
        count = jnp.where(present & jnp.logical_not(edge & (j == 0)), 1 + last.astype(jnp.int32), 0)
        begin = jnp.where(upward, block, block + 1)
        turn = jnp.where(upward, 1, -1)

        def one(k, carry):
            act(begin + turn * k)
            return carry

        lax.fori_loop(0, count, one, 0)

    def arrive(index):
        for side in (1, 0):
            present, edge, _, j, block, _ = stream(side, index)
            late = edge & (j > 1)

            @pl.when(present & late)
            def _(side=side, block=block):
                line_copy(block, True, True).wait_recv()

            @pl.when(present & jnp.logical_not(late))
            def _(side=side, block=block):
                line_copy(block, True, False).wait_recv()

            @pl.when(present & (has_left if side else has_right))
            def _(side=side, block=block):
                send_block(block, side == 0)

            @pl.when(present & edge & (j == 1) & (has_next if side else has_prev))
            def _(side=side):
                halo_copy(side == 1).start()

    def blur_side(index):
        def one_side(side, carry):
            present, edge, _, j, block, last = stream(side, index)
            late = edge & (j > 1)

            @pl.when(present)
            def _():
                blur_block(block, late)

            def spread(blur):
                blur_across(blur, late)
                to_partner(blur, late)

            blurs(side, index, spread)

            @pl.when(present & last & ((side == 1) == low))
            def _():
                stack_part(pl.multiple_of((block - 1) * BLOCK - 8, 8), JOIN, True, (core,))

            return carry

        lax.fori_loop(0, 2, one_side, 0)

    def stack_side(index):
        def one_side(side, carry):
            present, edge, upward, j, block, last = stream(side, index)
            late = edge & (j > 1)
            blurs(side, index, lambda blur: from_partner(blur, late))
            begin = pl.multiple_of(jnp.where(upward, block - 1, block + 2) * BLOCK - 8, 8)
            closes = (side == 1) == low

            @pl.when(present & jnp.logical_not(edge))
            def _():
                stack(begin, BLOCK, True)

            @pl.when(present & edge & closes & jnp.logical_not(last) & (j > 2))
            def _():
                stack_part(begin, BLOCK, True)

            @pl.when(present & closes & last)
            def _():
                stack_part(pl.multiple_of((block - 1) * BLOCK - 8, 8), JOIN, True, (1 - core,))

            return carry

        lax.fori_loop(0, 2, one_side, 0)

    limit = steps - 2
    mirror = chips - 1 - chip
    top_step = jnp.minimum(jnp.maximum(per * (mirror - 1) + 4, per * (chip - 1) + 2), limit)
    bottom_step = jnp.minimum(jnp.maximum(per * (chip - 1) + 4, per * (mirror - 1) + 2), limit)

    others = jnp.where(low, chip, mirror)
    other_step = jnp.where(others > 0, per * others + 2, -2)

    def step(index, carry):
        @pl.when(index < steps)
        def _():
            arrive(index)
            blur_side(index)

        @pl.when(index == top_step)
        def _():
            @pl.when(has_prev)
            def _():
                halo_copy(True).wait_recv()
                blur_along(top, 0, HALO, 0, 0)
                blur_along(top, 0, HALO, 0, 1)

            @pl.when(jnp.logical_not(has_prev))
            def _():
                for m in range(frames):
                    for tile in range(tiles + 1):
                        along[m, tile, pl.ds(0, HALO)] = jnp.zeros((HALO, LANES), jnp.float32)

            blur_across(-1, False)
            blur_across(0, False)

            @pl.when(jnp.logical_not(has_prev))
            def _():
                for m in range(frames):
                    for tile in range(tiles + 1):
                        blurred[core * frames + m, tile, pl.ds(0, ABOVE)] = jnp.zeros(
                            (ABOVE, LANES), jnp.float32
                        )

            pair_copy(-1, False).start()
            pair_copy(0, False).start()

        @pl.when(index == bottom_step)
        def _():
            @pl.when(has_next)
            def _():
                halo_copy(False).wait_recv()
                blur_along(bottom, 0, HALO, rows + HALO, 0)
                blur_along(bottom, 0, HALO, rows + HALO, 1)

            @pl.when(jnp.logical_not(has_next))
            def _():
                for m in range(frames):
                    for tile in range(tiles + 1):
                        along[m, tile, pl.ds(rows + HALO, HALO)] = jnp.zeros(
                            (HALO, LANES), jnp.float32
                        )

            blur_across(blocks, False)
            blur_across(blocks + 1, False)

            @pl.when(jnp.logical_not(has_next))
            def _():
                for m in range(frames):
                    for tile in range(tiles + 1):
                        blurred[core * frames + m, tile, pl.ds(rows + ABOVE, ABOVE)] = jnp.zeros(
                            (ABOVE, LANES), jnp.float32
                        )

            pair_copy(blocks, False).start()
            pair_copy(blocks + 1, False).start()

        @pl.when((index == steps - 3) & low)
        def _():
            ends_begin(False, 2)
            ends_begin(False, 3)

        @pl.when((index == steps - 3) & jnp.logical_not(low))
        def _():
            ends_begin(True, 2)
            ends_begin(True, 3)

        @pl.when(index == other_step)
        def _():
            @pl.when(low)
            def _():
                first_arrives(True)

            @pl.when(jnp.logical_not(low))
            def _():
                first_arrives(False)

        stack_side(index - 1)

        @pl.when(index - 1 == other_step)
        def _():
            @pl.when(low)
            def _():
                fresh_wait(True)

            @pl.when(jnp.logical_not(low))
            def _():
                fresh_wait(False)

            behind = jnp.where(low, 0, BLOCK)
            count = BLOCK * (per - 1)
            place = pl.ds(pl.multiple_of(other + behind + ABOVE, 8), count)
            for kind in range(2):
                for tile in range(tiles):
                    there = pl.ds(pl.multiple_of(behind, 8), count)
                    blurred[kind * frames, tile, place] = fresh[kind, tile, there]
            stack(other, BLOCK * per, 4)

        @pl.when(index - 1 == top_step)
        def _():
            from_partner(-1, False)
            from_partner(0, False)
            stack(0, ABOVE, True)

        @pl.when(index - 1 == bottom_step)
        def _():
            from_partner(blocks, False)
            from_partner(blocks + 1, False)
            stack(rows - ABOVE, ABOVE, True)

        return carry

    lax.fori_loop(0, steps + 1, step, 0)

    def drain_sends():
        for sides in (1, 2):
            late = (per - 1) * sides
            whole = blurred.at[pl.ds(0, frames), :, pl.ds(0, (blocks + 3 - late) * BLOCK)]
            most = blurred.at[pl.ds(0, frames - 1), :, pl.ds(0, late * BLOCK)]

            @pl.when(has_left.astype(jnp.int32) + has_right.astype(jnp.int32) == sides)
            def _(whole=whole, most=most):
                pltpu.make_async_copy(whole, whole, pair_sends.at[0]).wait()
                pltpu.make_async_copy(most, most, pair_sends.at[1]).wait()

        trade_copy(psi_ref).wait_send()

        def drain(origin, carry):
            part = raw.at[:, pl.ds(pl.multiple_of(origin * (2 * share), 8), 2 * share)]

            @pl.when(has_right & (origin <= chip))
            def _():
                pltpu.make_async_copy(part, part, right_sem.at[origin]).wait()

            @pl.when(has_left & (origin >= chip))
            def _():
                pltpu.make_async_copy(part, part, left_sem.at[origin]).wait()

            return carry

        lax.fori_loop(0, chips, drain, 0)

        @pl.when((other_step > 0) & low)
        def _():
            for piece in range(2):
                fresh_copy(True, piece).wait_send()

        @pl.when((other_step > 0) & jnp.logical_not(low))
        def _():
            for piece in range(2):
                fresh_copy(False, piece).wait_send()

        @pl.when(has_next)
        def _():
            halo_copy(True).wait_send()

        @pl.when(has_prev)
        def _():
            halo_copy(False).wait_send()


    @pl.when(others == 0)
    def _():
        drain_sends()

    @pl.when(low)
    def _():
        last_arrives(False)

    @pl.when(jnp.logical_not(low))
    def _():
        last_arrives(True)

    @pl.when(others > 0)
    def _():
        drain_sends()

    for piece in range(2):
        ends_copy(False, piece).wait()


def per_device(vels, skies, psi_maps, phi_maps, psf_taps, shifts):
    frames, share, width = psi_maps.shape
    maps = 2 * frames
    tiles = width // LANES
    rows = share * vels
    trials = shifts.shape[0]
    blocks = rows // BLOCK
    taps = psf_taps.shape[0]
    shifts = pltpu.with_memory_space_constraint(jnp.transpose(shifts, (1, 2, 0)), pltpu.HBM)
    psf_taps = pltpu.with_memory_space_constraint(psf_taps, pltpu.HBM)
    psi_maps = pltpu.with_memory_space_constraint(psi_maps, pltpu.HBM)
    phi_maps = pltpu.with_memory_space_constraint(phi_maps, pltpu.HBM)
    dma = pltpu.SemaphoreType.DMA
    part, ends, bands, weights, done = pl.pallas_call(
        functools.partial(gather_kernel, vels, skies),
        out_shape=(
            jax.ShapeDtypeStruct((2, trials, 2 * share, width), jnp.float32),
            jax.ShapeDtypeStruct((2, 2 * share + HALO, width), jnp.float32),
            jax.ShapeDtypeStruct((2, 9 * LANES, LANES), jnp.bfloat16),
            jax.ShapeDtypeStruct((2, taps, 8, LANES), jnp.float32),
            jax.ShapeDtypeStruct((trials, rows, width), jnp.float32),
        ),
        in_specs=[
            pl.BlockSpec(memory_space=pl.ANY),
            pl.BlockSpec(memory_space=pl.ANY),
            pl.BlockSpec(memory_space=pl.ANY),
            pl.BlockSpec(memory_space=pl.ANY),
        ],
        out_specs=(pl.BlockSpec(memory_space=pltpu.VMEM),) * 5,
        scratch_shapes=[
            pltpu.SMEM((taps,), jnp.float32),
            pltpu.SMEM(shifts.shape, jnp.int32),
            pltpu.VMEM((maps, tiles + 1, rows + 2 * ABOVE, LANES), jnp.float32),
            pltpu.VMEM((frames, rows, width), jnp.float32),
            pltpu.VMEM((frames, tiles + 1, rows + 2 * HALO, LANES), jnp.float32),
            pltpu.VMEM((blocks + 3, frames, tiles + 1, BLOCK, LANES), jnp.float32),
            pltpu.VMEM((frames, HALO, width), jnp.float32),
            pltpu.VMEM((frames, HALO, width), jnp.float32),
            pltpu.VMEM((6 * LANES, LANES), jnp.bfloat16),
            pltpu.VMEM((2, tiles, 2 * share, LANES), jnp.float32),
            pltpu.SemaphoreType.REGULAR((4,)),
            dma((2,)),
            dma,
            dma((2,)),
            dma((blocks,)),
            dma((vels // 2,)),
            dma((vels // 2,)),
            dma((2,)),
            dma((blocks + 3,)),
            dma((2,)),
            dma((2,)),
            dma((2, 2)),
            dma((2,)),
            dma((2,)),
            dma((4,)),
            dma((4,)),
        ],
        compiler_params=pltpu.CompilerParams(
            collective_id=0, has_side_effects=True, vmem_limit_bytes=36 * 2**20
        ),
        name="gather",
    )(psf_taps, shifts, psi_maps, phi_maps)
    return pl.pallas_call(
        functools.partial(finish_kernel, vels),
        out_shape=jax.ShapeDtypeStruct((trials, rows, width), jnp.float32),
        in_specs=[pl.BlockSpec(memory_space=pltpu.VMEM)] * 5,
        out_specs=pl.BlockSpec(memory_space=pl.ANY),
        scratch_shapes=[
            pltpu.VMEM((2, tiles, 2 * share + HALO, LANES), jnp.float32),
            pltpu.VMEM((2, tiles, 2 * share, LANES), jnp.float32),
            pltpu.VMEM((trials, 2 * share, width), jnp.float32),
            dma((3, trials)),
        ],
        compiler_params=pltpu.CompilerParams(vmem_limit_bytes=12 * 2**20),
        name="finish",
    )(part, ends, bands, weights, done)


def solution(mesh):
    return jax.shard_map(
        functools.partial(per_device, mesh.shape["vel"], mesh.shape["sky"]),
        mesh=mesh,
        in_specs=(
            P(None, ("sky", "vel"), None),
            P(None, ("sky", "vel"), None),
            P(),
            P("vel", None, None),
        ),
        out_specs=P("vel", "sky", None),
        check_vma=False,
    )
```
